128 devices in a mesh: group: 16 (over y, z), fold: 8 (over x, core).
Axes of the slice: x: 4, y: 4, z: 4, core: 2. Of those that a mesh axis runs over, the one named last changes fastest.
Arguments:
- right_side: float32 [16, 262144], P(None, ('group', 'fold')), may hold values from -6 to 6
- initial: float32 [16, 262144], P(None, ('group', 'fold')), may hold values from -6 to 6
- counts: int32 [16, 8], P('group'), may hold values from 1 to 2048, 8192 in all within a row
- columns: int32 [1024, 5], P('group'), may hold values from 0 to 69, as said below
- blocks: float32 [1024, 5, 128, 128], P('group')
Outputs:
- smoothed: float32 [16, 262144], P(None, ('group', 'fold'))
The draws below stay inside these ranges and needn't reach their ends.
Inputs may be any that keep to these rules, and one draw needn't show every extreme that they name: Every row of counts sums to 8192, and its largest entry is 2048. `columns`: index j of row block g * 64 + i names block g * 64 + j - 3; the 5 indices of a row block are distinct and lie within 3 of i + 3.
All inputs are finite; a program needn't handle non-finite values.
Results may differ from the reference program's by a relative error of at most 0.0001.
Values sent between devices are 32-bit elements; how exact they have to be, the bound alone decides.
A program may use at most 192 MiB of HBM per device.

```python
import math
import jax
import jax.numpy as jnp
import numpy as np
from jax import lax

NV = 16
BLOCK = 128
KB = 5
HB = 3
SWEEPS = 3
DEGREE = 4
OB = 64
OWN = 8192
NB = 1024
ROWS = 131072
CAP = 2048
SLOTS = 262144
N_GROUP = 16
N_FOLD = 8


def draw_columns(key, part):
    local_ids = jnp.arange(NB, dtype=jnp.int32) % OB
    nearby = 2 * (HB - 1)
    candidates = jnp.concatenate([jnp.arange(-(HB - 1), 0, dtype=jnp.int32), jnp.arange(1, HB, dtype=jnp.int32)])
    scores = jax.random.randint(key, (NB, nearby), 0, 1 << 20, dtype=jnp.int32) * nearby + jnp.arange(nearby, dtype=jnp.int32)[None, :]
    ordering = jnp.argsort(scores, axis=1, stable=True)
    chosen = candidates[ordering[:, :KB - 3]]
    fixed_part = jnp.stack([jnp.zeros((NB,), jnp.int32), jnp.full((NB,), -HB, jnp.int32), jnp.full((NB,), HB, jnp.int32)], axis=1)
    offsets = jnp.concatenate([fixed_part, chosen.astype(jnp.int32)], axis=1)
    return (local_ids[:, None] + HB + offsets).astype(jnp.int32)


def draw_blocks(key, part):
    noise_key, diag_key = jax.random.split(key)
    shape = (NB, KB, BLOCK, BLOCK)
    scale = 0.45 / (KB * BLOCK) ** 0.5
    noise = jax.random.normal(noise_key, shape, jnp.float32) * scale
    diag_values = jnp.exp(jax.random.uniform(diag_key, (NB, BLOCK), jnp.float32, jnp.log(0.5), jnp.log(4.0)))
    slot_zero = (jnp.arange(KB) == 0)[None, :, None, None]
    on_diagonal = (jnp.arange(BLOCK)[:, None] == jnp.arange(BLOCK)[None, :])[None, None, :, :]
    identity = jnp.logical_and(slot_zero, on_diagonal).astype(jnp.float32)
    return (noise * (1.0 - identity) + identity * diag_values[:, None, :, None]).astype(jnp.float32)


def level_of(own_key, dims, cuts, smallest, largest):
    gain = 1.0
    for position, blocks in cuts:
        heights = jax.random.uniform(jax.random.fold_in(jax.random.fold_in(own_key, 6), position), (blocks,), jnp.float32, smallest / len(cuts), largest / len(cuts))
        gain = gain * jnp.repeat(jnp.exp(heights), dims[position] // blocks).reshape((-1,) + (1,) * (len(dims) - 1 - position))
    return gain


def split_up(count, total, most, slope):
    weights = [(1 << 20) // math.isqrt(rank ** slope) + 1 for rank in range(2, count + 1)]
    surplus, holding = total - most - (count - 1), [1] * (count - 1)
    while surplus > 0:
        movable = [i for i in range(count - 1) if holding[i] < most]
        pool, budget = sum([weights[i] for i in movable]), surplus
        for i in movable:
            extra = min(most - holding[i], max(1, budget * weights[i] // pool), surplus)
            holding[i] = holding[i] + extra
            surplus = surplus - extra
    return np.array([most] + holding)


def ragged_sizes(stream_key, number_of, total, bound, lean):
    if number_of == 2:
        one = jax.random.randint(stream_key, (), max(1, total - bound), min(bound, total - 1) + 1)
        return jnp.stack([one, total - one])
    lengths = jnp.asarray(split_up(number_of, total, bound, lean), jnp.int32)
    twos = (number_of - 1) // 2
    source_of, sink = lengths[1:1 + 2 * twos:2], lengths[2:2 + 2 * twos:2]
    room = jnp.minimum(source_of - 1, bound - sink)
    shifted = jax.random.randint(jax.random.fold_in(stream_key, 1), (twos,), 0, 1 << 20) % (room + 1)
    lengths = lengths.at[1:1 + 2 * twos:2].set(source_of - shifted).at[2:2 + 2 * twos:2].set(sink + shifted)
    return lengths[jax.random.permutation(jax.random.fold_in(stream_key, 2), number_of)]


def scatter_about(key, extent, deviation, most, pieces=(), held_as=jnp.bfloat16):
    values = deviation * jax.random.normal(key, extent, jnp.float32)
    if pieces:
        values = values * level_of(key, extent, pieces, -0.22, 0.18)
    return jnp.clip(values, -most, most).astype(held_as)


def setup_inputs(seed: int = 0) -> dict:
    keys = jax.random.split(jax.random.key(seed), 6)
    right_side = scatter_about(keys[0], (NV, SLOTS), 1.0, 6.0, ((1, 128),), jnp.float32)
    initial = scatter_about(keys[1], (NV, SLOTS), 1.0, 6.0, ((1, 128),), jnp.float32)
    counts = jax.vmap(lambda own: ragged_sizes(own, N_FOLD, OWN, CAP, 2))(jax.random.split(keys[2], N_GROUP)).reshape((N_GROUP, N_FOLD)).astype(jnp.int32)
    columns = draw_columns(jax.random.fold_in(keys[5], 71), 0)
    blocks = draw_blocks(jax.random.fold_in(keys[5], 71), 0)
    return {"right_side": right_side, "initial": initial, "counts": counts, "columns": columns, "blocks": blocks}


upper_bound = 4.5
lower_bound = 1.35


def slot_sources(counts):
    starts = jnp.cumsum(counts, axis=1) - counts
    row_ids = jnp.arange(OWN, dtype=jnp.int32)
    owner_slot = jnp.sum((starts[:, None, :] <= row_ids[None, :, None]).astype(jnp.int32), axis=2) - 1
    row_start = jnp.take_along_axis(starts, owner_slot, axis=1)
    group_ids = jnp.arange(N_GROUP, dtype=jnp.int32)[:, None]
    source = (group_ids * N_FOLD + owner_slot) * CAP + row_ids[None, :] - row_start
    return source.reshape(-1).astype(jnp.int32), starts


def operate(vector, columns, blocks):
    padding = jnp.zeros((NV, HB * BLOCK), jnp.float32)
    extended = jnp.concatenate([padding, vector, padding], axis=1).reshape(NV, NB + 2 * HB, BLOCK)
    base = (jnp.arange(NB, dtype=jnp.int32) // OB * OB).astype(jnp.int32)
    global_ids = (base[:, None] + columns).astype(jnp.int32)
    picked = extended[:, global_ids, :]
    result = jnp.einsum("nikc,ikrc->nir", picked, blocks, precision=lax.Precision.HIGHEST)
    return result.reshape(NV, ROWS)


def reference(right_side, initial, counts, columns, blocks):
    source, starts = slot_sources(counts)
    target = right_side[:, source]
    iterate = initial[:, source]
    theta = (upper_bound + lower_bound) / 2.0
    delta = (upper_bound - lower_bound) / 2.0
    for sweep in range(SWEEPS):
        resid = target - operate(iterate, columns, blocks)
        update = resid / theta
        ratio_now = delta / theta
        for step in range(DEGREE):
            iterate = iterate + update
            if step + 1 < DEGREE:
                resid = resid - operate(update, columns, blocks)
                ratio_next = 1.0 / (2.0 * theta / delta - ratio_now)
                update = ratio_next * ratio_now * update + (2.0 * ratio_next / delta) * resid
                ratio_now = ratio_next
    slot_ids = jnp.arange(SLOTS, dtype=jnp.int32)
    device_ids = slot_ids // CAP
    within = slot_ids % CAP
    group_ids = device_ids // N_FOLD
    fold_ids = device_ids % N_FOLD
    live_counts = counts[group_ids, fold_ids]
    row_start = starts[group_ids, fold_ids]
    clipped = jnp.minimum(within, live_counts - 1)
    target_rows = (group_ids * OWN + row_start + clipped).astype(jnp.int32)
    values = iterate[:, target_rows]
    return jnp.where((within < live_counts)[None, :], values, jnp.float32(0.0))
```

```python
import functools

import jax
import jax.numpy as jnp
import numpy as np
from jax import lax
from jax.experimental import pallas as pl
from jax.experimental.pallas import tpu as pltpu
from jax.sharding import PartitionSpec as P

MESH = pl.DeviceIdType.MESH
HB = 3
SWEEPS = 3
DEGREE = 4
KB = 5
NV = 16
LANES = 128
FOLDS = 8
CHIPS = 4

upper_bound = 4.5
lower_bound = 1.35


def step_factors():
    theta = (upper_bound + lower_bound) / 2.0
    delta = (upper_bound - lower_bound) / 2.0
    keep, gain = [0.0], [1.0 / theta]
    for sweep in range(SWEEPS):
        ratio = delta / theta
        for step in range(DEGREE - 1):
            ratio_next = 1.0 / (2.0 * theta / delta - ratio)
            keep.append(ratio_next * ratio)
            gain.append(2.0 * ratio_next / delta)
            ratio = ratio_next
        if sweep + 1 < SWEEPS:
            keep.append(0.0)
            gain.append(1.0 / theta)
    return np.array([keep, gain], np.float32)


def split(value):
    high = value.astype(jnp.bfloat16)
    low = (value - high.astype(jnp.float32)).astype(jnp.bfloat16)
    return high, low


def position_of(fold):
    chip, core = fold // 2, fold % 2
    return chip + core * (7 - 2 * chip)


def fold_of(position):
    core = position // 4
    chip = position + core * (7 - 2 * position)
    return 2 * chip + core


def kernel(
    steps, rows, groups,
    factors, counts, columns, right_side, initial, blocks, out,
    raw, aligned, sent, parts, raw_blocks, weights, order, vector, update, resid, iterate, partial, halo, gathered,
    block_sem, a_send, a_recv, b_send, b_recv, h_send, h_recv, c_send, c_recv,
):
    group, fold = lax.axis_index("group"), lax.axis_index("fold")
    chip, core = fold // 2, fold % 2
    place = position_of(fold)
    partner = chip * 2 + (1 - core)
    slots = right_side.shape[1] // LANES
    total_rows = rows * FOLDS

    own_blocks = pltpu.make_async_copy(blocks.at[pl.ds(place * rows, rows)], raw_blocks, block_sem)
    own_blocks.start()

    rank = group * FOLDS + place
    has_left, has_right = rank > 0, rank < groups * FOLDS - 1
    at_left, at_right = place == 0, place == FOLDS - 1
    left = {"group": group - (7 - place) // 7, "fold": fold_of((place + 7) % 8)}
    right = {"group": group + place // 7, "fold": fold_of((place + 1) % 8)}

    barrier = pltpu.get_barrier_semaphore()
    for other in range(1, FOLDS):
        pl.semaphore_signal(barrier, inc=1, device_id={"group": group, "fold": (fold + other) % FOLDS}, device_id_type=MESH)

    @pl.when(jnp.logical_and(at_left, has_left))
    def _():
        pl.semaphore_signal(barrier, inc=1, device_id=left, device_id_type=MESH)

    @pl.when(jnp.logical_and(at_right, has_right))
    def _():
        pl.semaphore_signal(barrier, inc=1, device_id=right, device_id_type=MESH)

    last = groups * FOLDS - 1
    outside = (7 - place) // 7 * ((rank + last) // (last + 1)) + place // 7 * (1 - (rank + 1) // (last + 1))
    pl.semaphore_wait(barrier, FOLDS - 1 + outside)

    def swap(source):
        return pltpu.make_async_remote_copy(
            src_ref=source, dst_ref=raw, send_sem=a_send, recv_sem=a_recv,
            device_id={"group": group, "fold": partner}, device_id_type=MESH,
        )

    @pl.when(core == 0)
    def _():
        swap(initial).start()

    @pl.when(core == 1)
    def _():
        swap(right_side).start()

    lane = lax.broadcasted_iota(jnp.int32, (NV, LANES), 1)

    def start_of(which):
        total = jnp.int32(0)
        for i in range(FOLDS):
            total = total + jnp.where(i < which, counts[0, i], 0)
        return total

    def count_of(which):
        total = jnp.int32(0)
        for i in range(FOLDS):
            total = total + jnp.where(i == which, counts[0, i], 0)
        return total

    def align(source, which):
        start, count = start_of(chip * 2 + which), count_of(chip * 2 + which)
        shift = start & (LANES - 1)
        aligned[which, 0] = jnp.zeros((NV, LANES), jnp.float32)
        aligned[which, slots + 2] = jnp.zeros((NV, LANES), jnp.float32)
        before = jnp.zeros((NV, LANES), jnp.float32)
        for m in range(slots + 1):
            if m < slots:
                now = pltpu.roll(source[:, m * LANES:(m + 1) * LANES], shift, 1)
            else:
                now = jnp.zeros((NV, LANES), jnp.float32)
            slot = lane + (m * LANES - shift)
            value = jnp.where(lane < shift, before, now)
            live = jnp.logical_and(slot >= 0, slot < count)
            aligned[which, m + 1] = jnp.where(live, value, 0.0)
            before = now

    @pl.when(core == 0)
    def _():
        align(right_side, 0)

    @pl.when(core == 1)
    def _():
        align(initial, 1)

    swap(initial).wait()

    @pl.when(core == 0)
    def _():
        align(raw, 1)

    @pl.when(core == 1)
    def _():
        align(raw, 0)

    first = [start_of(chip * 2) // LANES, start_of(chip * 2 + 1) // LANES]

    def row_block(index):
        at = [jnp.clip(index - first[i], -1, slots + 1) + 1 for i in range(2)]
        return aligned[0, at[0]] + aligned[1, at[1]]

    def message(other):
        dest = (fold + other) % FOLDS
        where = position_of(dest) * rows
        return where, pltpu.make_async_remote_copy(
            src_ref=sent.at[pl.ds(where, rows)], dst_ref=parts.at[fold],
            send_sem=b_send.at[other], recv_sem=b_recv.at[fold],
            device_id={"group": group, "fold": dest}, device_id_type=MESH,
        )

    def arrival(source):
        return pltpu.make_async_remote_copy(
            src_ref=sent.at[pl.ds(0, rows)], dst_ref=parts.at[source],
            send_sem=b_send.at[0], recv_sem=b_recv.at[source],
            device_id={"group": group, "fold": fold}, device_id_type=MESH,
        )

    for other in (4, 3, 5, 2, 6, 1, 7):
        where, copy = message(other)
        for b in range(rows):
            sent[where + b] = row_block(where + b)
        copy.start()
    for b in range(rows):
        parts[fold, b] = row_block(place * rows + b)

    own_blocks.wait()
    zero = jnp.zeros((NV, LANES), jnp.float32)

    @pl.loop(0, rows)
    def _(j):
        column = [columns[place * rows + j, k] for k in range(KB)]
        ranks = []
        for k in range(KB):
            r = jnp.int32(0)
            for other in range(KB):
                if other != k:
                    ahead = column[other] <= column[k] if other < k else column[other] < column[k]
                    r = r + ahead.astype(jnp.int32)
            ranks.append(r)
        for s in range(KB):
            from_slot, at = jnp.int32(0), jnp.int32(0)
            for k in range(KB):
                from_slot = from_slot + jnp.where(ranks[k] == s, k, 0)
                at = at + jnp.where(ranks[k] == s, column[k], 0)
            order[j, s] = jnp.clip(at - place * rows, 0, rows + 2 * HB - 1)
            high, low = split(raw_blocks[j, from_slot].T)
            weights[j, s * LANES:(s + 1) * LANES, 0:LANES] = high
            weights[j, s * LANES:(s + 1) * LANES, LANES:2 * LANES] = low
        iterate[j] = zero

    @pl.when(jnp.logical_not(has_left))
    def _():
        for parity in range(2):
            for b in range(HB):
                halo[parity, 0, b] = zero

    @pl.when(jnp.logical_not(has_right))
    def _():
        for parity in range(2):
            for b in range(HB):
                halo[parity, 1, b] = zero

    for other in range(1, FOLDS):
        arrival((fold + other) % FOLDS).wait_recv()
    for b in range(rows):
        resid[b] = (parts[0, b] + parts[2, b]) + (parts[4, b] + parts[6, b])
        update[0, b] = (parts[1, b] + parts[3, b]) + (parts[5, b] + parts[7, b])
    for other in range(1, FOLDS):
        message(other)[1].wait_send()

    def to_left(parity):
        return pltpu.make_async_remote_copy(
            src_ref=update.at[parity, pl.ds(0, HB)], dst_ref=halo.at[parity, 1],
            send_sem=h_send.at[parity, 0], recv_sem=h_recv.at[parity, 1],
            device_id=left, device_id_type=MESH,
        )

    def to_right(parity):
        return pltpu.make_async_remote_copy(
            src_ref=update.at[parity, pl.ds(rows - HB, HB)], dst_ref=halo.at[parity, 0],
            send_sem=h_send.at[parity, 1], recv_sem=h_recv.at[parity, 0],
            device_id=right, device_id_type=MESH,
        )

    def store_vector(index, value):
        high, low = split(value)
        vector[index, 0:NV] = high
        vector[index, NV:2 * NV] = low

    def product(j, low, high):
        lhs = jnp.concatenate([vector[order[j, s]] for s in range(low, high)], axis=1)
        full = jnp.dot(lhs, weights[j, low * LANES:high * LANES, :], preferred_element_type=jnp.float32)
        return (full[:NV, :LANES] + full[:NV, LANES:]) + (full[NV:, :LANES] + full[NV:, LANES:])

    def own_slots(j):
        return max(0, HB - j), KB - max(0, HB - (rows - 1 - j))

    @pl.loop(0, steps)
    def _(k):
        parity = k % 2
        keep, gain = factors[0, k], factors[1, k]

        @pl.when(has_left)
        def _():
            to_left(parity).start()

        @pl.when(has_right)
        def _():
            to_right(parity).start()

        for b in range(rows):
            now = update[parity, b]
            iterate[b] = iterate[b] + now
            store_vector(HB + b, now)

        def finish(j, applied):
            left_over = resid[j] - applied
            resid[j] = left_over
            update[1 - parity, j] = keep * update[parity, j] + gain * left_over

        for j in range(rows):
            low, high = own_slots(j)
            applied = product(j, low, high)
            if high - low == KB:
                finish(j, applied)
            else:
                partial[j] = applied

        @pl.when(has_left)
        def _():
            to_right(parity).wait_recv()

        @pl.when(has_right)
        def _():
            to_left(parity).wait_recv()

        for b in range(HB):
            store_vector(b, halo[parity, 0, b])
            store_vector(HB + rows + b, halo[parity, 1, b])
        for j in range(rows):
            low, high = own_slots(j)
            if low > 0:
                finish(j, partial[j] + product(j, 0, low))
            elif high < KB:
                finish(j, partial[j] + product(j, high, KB))

        @pl.when(has_left)
        def _():
            to_left(parity).wait_send()

        @pl.when(has_right)
        def _():
            to_right(parity).wait_send()

    for b in range(rows):
        gathered[place * rows + b] = iterate[b] + update[steps % 2, b]

    def piece(where, dest, which):
        return pltpu.make_async_remote_copy(
            src_ref=gathered.at[pl.ds(where * rows, rows)], dst_ref=gathered.at[pl.ds(where * rows, rows)],
            send_sem=c_send.at[which], recv_sem=c_recv.at[where],
            device_id={"group": group, "fold": dest}, device_id_type=MESH,
        )

    for other in (2, 1, 3):
        piece(place, (fold + 2 * other) % FOLDS, other).start()
    piece(place, partner, 0).start()
    for other in (1, 3, 2):
        where = position_of((fold + 2 * other) % FOLDS)
        piece(where, partner, 0).wait_recv()
        piece(where, partner, 3 + other).start()
    for other in range(CHIPS):
        where = position_of((partner + 2 * other) % FOLDS)
        piece(where, partner, 0).wait_recv()

    begin, live = start_of(fold), count_of(fold)
    shift = begin & (LANES - 1)
    base = begin // LANES
    back = (LANES - shift) & (LANES - 1)

    def shifted(m):
        return pltpu.roll(gathered[jnp.minimum(base + m, total_rows - 1)], back, 1)

    here = shifted(0)
    for m in range(slots):
        after = shifted(m + 1)
        value = jnp.where(lane < LANES - shift, here, after)
        out[:, m * LANES:(m + 1) * LANES] = jnp.where(lane + m * LANES < live, value, 0.0)
        here = after

    for which in range(7):
        piece(place, partner, which).wait_send()


def on_device(right_side, initial, counts, columns, blocks):
    folds, groups = lax.axis_size("fold"), lax.axis_size("group")
    slots = right_side.shape[1] // LANES
    owned = blocks.shape[0]
    rows = owned // folds
    factors = step_factors()
    steps = factors.shape[1]
    smem = pl.BlockSpec(memory_space=pltpu.SMEM)
    vmem = pl.BlockSpec(memory_space=pltpu.VMEM)
    f32 = jnp.float32
    dma = pltpu.SemaphoreType.DMA
    return pl.pallas_call(
        functools.partial(kernel, steps, rows, groups),
        out_shape=jax.ShapeDtypeStruct(right_side.shape, f32),
        in_specs=[smem, smem, smem, vmem, vmem, pl.BlockSpec(memory_space=pl.ANY)],
        out_specs=vmem,
        scratch_shapes=[
            pltpu.VMEM(right_side.shape, f32),
            pltpu.VMEM((2, slots + 3, NV, LANES), f32),
            pltpu.VMEM((owned, NV, LANES), f32),
            pltpu.VMEM((folds, rows, NV, LANES), f32),
            pltpu.VMEM((rows, KB, LANES, LANES), f32),
            pltpu.VMEM((rows, KB * LANES, 2 * LANES), jnp.bfloat16),
            pltpu.SMEM((rows, KB), jnp.int32),
            pltpu.VMEM((rows + 2 * HB, 2 * NV, LANES), jnp.bfloat16),
            pltpu.VMEM((2, rows, NV, LANES), f32),
            pltpu.VMEM((rows, NV, LANES), f32),
            pltpu.VMEM((rows, NV, LANES), f32),
            pltpu.VMEM((rows, NV, LANES), f32),
            pltpu.VMEM((2, 2, HB, NV, LANES), f32),
            pltpu.VMEM((owned, NV, LANES), f32),
            dma, dma, dma, dma((8,)), dma((8,)), dma((2, 2)), dma((2, 2)), dma((7,)), dma((8,)),
        ],
        compiler_params=pltpu.CompilerParams(collective_id=0, has_side_effects=True),
    )(jnp.asarray(factors), counts, columns, right_side, initial, blocks)


def solution(mesh):
    placed = (
        P(None, ("group", "fold")),
        P(None, ("group", "fold")),
        P("group", None),
        P("group", None),
        P("group", None, None, None),
    )
    return jax.shard_map(
        on_device, mesh=mesh, in_specs=placed, out_specs=P(None, ("group", "fold")), check_vma=False
    )
```

```python
import functools

import jax
import jax.numpy as jnp
import numpy as np
from jax import lax
from jax.experimental import pallas as pl
from jax.experimental.pallas import tpu as pltpu
from jax.sharding import PartitionSpec as P

MESH = pl.DeviceIdType.MESH
HB = 3
SWEEPS = 3
DEGREE = 4
KB = 5
NV = 16
LANES = 128
FOLDS = 8
CHIPS = 4
DEPTH = 2

upper_bound = 4.5
lower_bound = 1.35


def step_factors():
    theta = (upper_bound + lower_bound) / 2.0
    delta = (upper_bound - lower_bound) / 2.0
    keep, gain = [0.0], [1.0 / theta]
    for sweep in range(SWEEPS):
        ratio = delta / theta
        for step in range(DEGREE - 1):
            ratio_next = 1.0 / (2.0 * theta / delta - ratio)
            keep.append(ratio_next * ratio)
            gain.append(2.0 * ratio_next / delta)
            ratio = ratio_next
        if sweep + 1 < SWEEPS:
            keep.append(0.0)
            gain.append(1.0 / theta)
    return np.array([keep, gain], np.float32)


def split(value):
    high = value.astype(jnp.bfloat16)
    low = (value - high.astype(jnp.float32)).astype(jnp.bfloat16)
    return high, low


def position_of(fold):
    chip, core = fold // 2, fold % 2
    return chip + core * (7 - 2 * chip)


def fold_of(position):
    core = position // 4
    chip = position + core * (7 - 2 * position)
    return 2 * chip + core


def kernel(
    steps, rows, groups, depth,
    factors, counts, columns, right_side, initial, blocks, out,
    raw, aligned, sent, parts, raw_own, raw_left, raw_right, weights, order, all_columns, edge_columns,
    vector, update, resid, mid_update, mid_resid, iterate, partial, halo_update, halo_resid, gathered,
    block_sem, column_sem, edge_send, edge_recv, a_send, a_recv, b_send, b_recv, h_send, h_recv, c_send, c_recv,
):
    group, fold = lax.axis_index("group"), lax.axis_index("fold")
    chip, core = fold // 2, fold % 2
    place = position_of(fold)
    partner = chip * 2 + (1 - core)
    slots = right_side.shape[1] // LANES
    owned = rows * FOLDS
    reach = HB * depth
    outer = HB * (depth - 1)
    wide = rows + 2 * outer
    zero = jnp.zeros((NV, LANES), jnp.float32)

    rank = group * FOLDS + place
    last = groups * FOLDS - 1
    has_left, has_right = rank > 0, rank < last
    left_edge, right_edge = jnp.logical_and(place == 0, has_left), jnp.logical_and(place == FOLDS - 1, has_right)
    left = {"group": group - (7 - place) // 7, "fold": fold_of((place + 7) % 8)}
    right = {"group": group + place // 7, "fold": fold_of((place + 1) % 8)}

    own_blocks = pltpu.make_async_copy(
        blocks.at[pl.ds(place * rows, rows)], raw_own, block_sem.at[0]
    )
    left_blocks = pltpu.make_async_copy(
        blocks.at[pl.ds(jnp.maximum(place * rows - outer, 0), outer)], raw_left, block_sem.at[1]
    )
    right_blocks = pltpu.make_async_copy(
        blocks.at[pl.ds(jnp.minimum(place * rows + rows, owned - outer), outer)],
        raw_right, block_sem.at[2]
    )
    own_columns = pltpu.make_async_copy(columns, all_columns.at[pl.ds(8, owned)], column_sem.at[0])
    own_columns.start()
    own_blocks.start()

    @pl.when(place > 0)
    def _():
        left_blocks.start()

    @pl.when(place < FOLDS - 1)
    def _():
        right_blocks.start()

    barrier = pltpu.get_barrier_semaphore()
    for other in range(1, FOLDS):
        pl.semaphore_signal(barrier, inc=1, device_id={"group": group, "fold": (fold + other) % FOLDS}, device_id_type=MESH)

    @pl.when(left_edge)
    def _():
        pl.semaphore_signal(barrier, inc=1, device_id=left, device_id_type=MESH)

    @pl.when(right_edge)
    def _():
        pl.semaphore_signal(barrier, inc=1, device_id=right, device_id_type=MESH)

    outside = (7 - place) // 7 * ((rank + last) // (last + 1)) + place // 7 * (1 - (rank + 1) // (last + 1))
    pl.semaphore_wait(barrier, FOLDS - 1 + outside)

    def swap(source):
        return pltpu.make_async_remote_copy(
            src_ref=source, dst_ref=raw, send_sem=a_send, recv_sem=a_recv,
            device_id={"group": group, "fold": partner}, device_id_type=MESH,
        )

    @pl.when(core == 0)
    def _():
        swap(initial).start()

    @pl.when(core == 1)
    def _():
        swap(right_side).start()

    def edge_left():
        return [
            pltpu.make_async_remote_copy(
                src_ref=columns.at[pl.ds(0, 8)], dst_ref=edge_columns.at[1],
                send_sem=edge_send.at[0, 0], recv_sem=edge_recv.at[0, 1], device_id=left, device_id_type=MESH,
            ),
            pltpu.make_async_remote_copy(
                src_ref=blocks.at[pl.ds(0, outer)], dst_ref=raw_right,
                send_sem=edge_send.at[1, 0], recv_sem=edge_recv.at[1, 1], device_id=left, device_id_type=MESH,
            ),
        ]

    def edge_right():
        return [
            pltpu.make_async_remote_copy(
                src_ref=columns.at[pl.ds(owned - 8, 8)], dst_ref=edge_columns.at[0],
                send_sem=edge_send.at[0, 1], recv_sem=edge_recv.at[0, 0], device_id=right, device_id_type=MESH,
            ),
            pltpu.make_async_remote_copy(
                src_ref=blocks.at[pl.ds(owned - outer, outer)], dst_ref=raw_left,
                send_sem=edge_send.at[1, 1], recv_sem=edge_recv.at[1, 0], device_id=right, device_id_type=MESH,
            ),
        ]

    @pl.when(left_edge)
    def _():
        for copy in edge_left():
            copy.start()

    @pl.when(right_edge)
    def _():
        for copy in edge_right():
            copy.start()

    lane = lax.broadcasted_iota(jnp.int32, (NV, LANES), 1)

    def start_of(which):
        total = jnp.int32(0)
        for i in range(FOLDS):
            total = total + jnp.where(i < which, counts[0, i], 0)
        return total

    def count_of(which):
        total = jnp.int32(0)
        for i in range(FOLDS):
            total = total + jnp.where(i == which, counts[0, i], 0)
        return total

    def align(source, which):
        start, count = start_of(chip * 2 + which), count_of(chip * 2 + which)
        shift = start & (LANES - 1)
        aligned[which, 0] = zero
        aligned[which, slots + 2] = zero
        before = zero
        for m in range(slots + 1):
            if m < slots:
                now = pltpu.roll(source[:, m * LANES:(m + 1) * LANES], shift, 1)
            else:
                now = zero
            slot = lane + (m * LANES - shift)
            value = jnp.where(lane < shift, before, now)
            live = jnp.logical_and(slot >= 0, slot < count)
            aligned[which, m + 1] = jnp.where(live, value, 0.0)
            before = now

    @pl.when(core == 0)
    def _():
        align(right_side, 0)

    @pl.when(core == 1)
    def _():
        align(initial, 1)

    swap(initial).wait()

    @pl.when(core == 0)
    def _():
        align(raw, 1)

    @pl.when(core == 1)
    def _():
        align(raw, 0)

    first = [start_of(chip * 2) // LANES, start_of(chip * 2 + 1) // LANES]

    def row_block(index):
        at = [jnp.clip(index - first[i], -1, slots + 1) + 1 for i in range(2)]
        return aligned[0, at[0]] + aligned[1, at[1]]

    def message(other):
        dest = (fold + other) % FOLDS
        where = position_of(dest) * rows
        return where, pltpu.make_async_remote_copy(
            src_ref=sent.at[pl.ds(where, rows)], dst_ref=parts.at[fold],
            send_sem=b_send.at[other], recv_sem=b_recv.at[fold],
            device_id={"group": group, "fold": dest}, device_id_type=MESH,
        )

    def arrival(source):
        return pltpu.make_async_remote_copy(
            src_ref=sent.at[pl.ds(0, rows)], dst_ref=parts.at[source],
            send_sem=b_send.at[0], recv_sem=b_recv.at[source],
            device_id={"group": group, "fold": fold}, device_id_type=MESH,
        )

    for other in (4, 3, 5, 2, 6, 1, 7):
        where, copy = message(other)
        for b in range(rows):
            sent[where + b] = row_block(where + b)
        copy.start()
    for b in range(rows):
        parts[fold, b] = row_block(place * rows + b)

    def prepare(source, low, high):
        @pl.loop(low, high)
        def _(e):
            at_row = place * rows + e - outer + 8
            move = jnp.where(at_row < 8, -owned, jnp.where(at_row >= owned + 8, owned, 0)) - place * rows + outer
            column = [all_columns[at_row, k] for k in range(KB)]
            ranks = []
            for k in range(KB):
                r = jnp.int32(0)
                for other in range(KB):
                    if other != k:
                        ahead = column[other] <= column[k] if other < k else column[other] < column[k]
                        r = r + ahead.astype(jnp.int32)
                ranks.append(r)
            for s in range(KB):
                from_slot, at = jnp.int32(0), jnp.int32(0)
                for k in range(KB):
                    from_slot = from_slot + jnp.where(ranks[k] == s, k, 0)
                    at = at + jnp.where(ranks[k] == s, column[k], 0)
                order[e, s] = jnp.clip(at + move, 0, rows + 2 * reach - 1)
                high_part, low_part = split(source[e - low, from_slot].T)
                weights[e, s * LANES:(s + 1) * LANES, 0:LANES] = high_part
                weights[e, s * LANES:(s + 1) * LANES, LANES:2 * LANES] = low_part

    def absent(low, side):
        for e in range(low, low + outer):
            for s in range(KB):
                order[e, s] = 0
            weights[e] = jnp.zeros((KB * LANES, 2 * LANES), jnp.bfloat16)
        for parity in range(2):
            for b in range(reach):
                halo_update[parity, side, b] = zero
            for b in range(outer):
                halo_resid[parity, side, b] = zero

    own_columns.wait()
    own_blocks.wait()
    prepare(raw_own, outer, outer + rows)

    @pl.when(place > 0)
    def _():
        left_blocks.wait()
        prepare(raw_left, 0, outer)

    @pl.when(place < FOLDS - 1)
    def _():
        right_blocks.wait()
        prepare(raw_right, outer + rows, wide)

    @pl.when(jnp.logical_not(has_left))
    def _():
        absent(0, 0)

    @pl.when(jnp.logical_not(has_right))
    def _():
        absent(outer + rows, 1)

    def store_vector(which, index, value):
        high, low = split(value)
        vector[which, index, 0:NV] = high
        vector[which, index, NV:2 * NV] = low

    for other in range(1, FOLDS):
        arrival((fold + other) % FOLDS).wait_recv()
    for b in range(rows):
        resid[0, b] = (parts[0, b] + parts[2, b]) + (parts[4, b] + parts[6, b])
        begun = (parts[1, b] + parts[3, b]) + (parts[5, b] + parts[7, b])
        update[0, b] = begun
        iterate[b] = zero
        store_vector(0, reach + b, begun)

    def exchange(parity):
        def copy(source, target, side, which):
            return pltpu.make_async_remote_copy(
                src_ref=source, dst_ref=target,
                send_sem=h_send.at[parity, side, which], recv_sem=h_recv.at[parity, 1 - side, which],
                device_id=right if side else left, device_id_type=MESH,
            )

        return [
            [
                copy(update.at[parity, pl.ds(0, reach)], halo_update.at[parity, 1], 0, 0),
                copy(resid.at[parity, pl.ds(0, outer)], halo_resid.at[parity, 1], 0, 1),
            ],
            [
                copy(update.at[parity, pl.ds(rows - reach, reach)], halo_update.at[parity, 0], 1, 0),
                copy(resid.at[parity, pl.ds(rows - outer, outer)], halo_resid.at[parity, 0], 1, 1),
            ],
        ]

    def send(parity):
        copies = exchange(parity)
        for which in range(2):
            @pl.when(has_left)
            def _():
                copies[0][which].start()

            @pl.when(has_right)
            def _():
                copies[1][which].start()

    def receive(parity, which):
        copies = exchange(parity)

        @pl.when(has_left)
        def _():
            copies[1][which].wait_recv()

        @pl.when(has_right)
        def _():
            copies[0][which].wait_recv()

    send(0)

    for other in range(1, FOLDS):
        message(other)[1].wait_send()

    def edge_done(side):
        arrived = (edge_left if side else edge_right)()
        arrived[0].wait_recv()
        into = pltpu.make_async_copy(
            edge_columns.at[side], all_columns.at[pl.ds(side * (owned + 8), 8)], column_sem.at[1 + side]
        )
        into.start()
        into.wait()
        arrived[1].wait_recv()
        prepare(raw_right if side else raw_left, side * (outer + rows), side * (outer + rows) + outer)

    @pl.when(left_edge)
    def _():
        edge_done(0)
        for copy in edge_left():
            copy.wait_send()

    @pl.when(right_edge)
    def _():
        edge_done(1)
        for copy in edge_right():
            copy.wait_send()

    def product(which, e, low, high):
        lhs = jnp.concatenate([vector[which, order[e, s]] for s in range(low, high)], axis=1)
        full = jnp.dot(lhs, weights[e, low * LANES:high * LANES, :], preferred_element_type=jnp.float32)
        return (full[:NV, :LANES] + full[:NV, LANES:]) + (full[NV:, :LANES] + full[NV:, LANES:])

    def own_slots(j):
        return max(0, HB - j), KB - max(0, HB - (rows - 1 - j))

    rounds = steps // depth

    @pl.loop(0, rounds)
    def _(turn):
        parity = turn % 2

        for level in range(depth):
            now, later = level % 2, (level + 1) % 2
            k = turn * depth + level
            keep, gain = factors[0, k], factors[1, k]

            def finish(e, applied):
                own = e - outer
                inside = 0 <= own < rows
                if level > 0:
                    old, left_over = mid_update[e], mid_resid[e]
                elif inside:
                    old, left_over = update[parity, own], resid[parity, own]
                elif own < 0:
                    old, left_over = halo_update[parity, 0, e + HB], halo_resid[parity, 0, e]
                else:
                    old, left_over = halo_update[parity, 1, own - rows], halo_resid[parity, 1, own - rows]
                left_over = left_over - applied
                fresh = keep * old + gain * left_over
                if inside:
                    iterate[own] = iterate[own] + old
                if level == depth - 1:
                    update[1 - parity, own] = fresh
                    resid[1 - parity, own] = left_over
                else:
                    mid_update[e] = fresh
                    mid_resid[e] = left_over
                store_vector(later, e + HB, fresh)

            margin = HB * (depth - 1 - level)
            if level > 0:
                for e in range(outer - margin, outer + rows + margin):
                    finish(e, product(now, e, 0, KB))
                continue

            for j in range(rows):
                low, high = own_slots(j)
                applied = product(now, j + outer, low, high)
                if high - low == KB:
                    finish(j + outer, applied)
                else:
                    partial[j] = applied
            receive(parity, 0)
            for b in range(reach):
                store_vector(now, b, halo_update[parity, 0, b])
                store_vector(now, reach + rows + b, halo_update[parity, 1, b])
            for j in range(rows):
                low, high = own_slots(j)
                if low > 0:
                    finish(j + outer, partial[j] + product(now, j + outer, 0, low))
                elif high < KB:
                    finish(j + outer, partial[j] + product(now, j + outer, high, KB))
            receive(parity, 1)
            for e in list(range(outer)) + list(range(outer + rows, wide)):
                finish(e, product(now, e, 0, KB))

        copies = exchange(parity)
        for which in range(2):
            @pl.when(has_left)
            def _():
                copies[0][which].wait_send()

            @pl.when(has_right)
            def _():
                copies[1][which].wait_send()

        @pl.when(turn + 1 < rounds)
        def _():
            send(1 - parity)

    for b in range(rows):
        gathered[place * rows + b] = iterate[b] + update[rounds % 2, b]

    def piece(where, dest, which):
        return pltpu.make_async_remote_copy(
            src_ref=gathered.at[pl.ds(where * rows, rows)], dst_ref=gathered.at[pl.ds(where * rows, rows)],
            send_sem=c_send.at[which], recv_sem=c_recv.at[where],
            device_id={"group": group, "fold": dest}, device_id_type=MESH,
        )

    for other in (2, 1, 3):
        piece(place, (fold + 2 * other) % FOLDS, other).start()
    piece(place, partner, 0).start()
    for other in (1, 3, 2):
        where = position_of((fold + 2 * other) % FOLDS)
        piece(where, partner, 0).wait_recv()
        piece(where, partner, 3 + other).start()
    for other in range(CHIPS):
        where = position_of((partner + 2 * other) % FOLDS)
        piece(where, partner, 0).wait_recv()

    begin, live = start_of(fold), count_of(fold)
    shift = begin & (LANES - 1)
    base = begin // LANES
    back = (LANES - shift) & (LANES - 1)

    def shifted(m):
        return pltpu.roll(gathered[jnp.minimum(base + m, owned - 1)], back, 1)

    here = shifted(0)
    for m in range(slots):
        after = shifted(m + 1)
        value = jnp.where(lane < LANES - shift, here, after)
        out[:, m * LANES:(m + 1) * LANES] = jnp.where(lane + m * LANES < live, value, 0.0)
        here = after

    for which in range(7):
        piece(place, partner, which).wait_send()


def on_device(right_side, initial, counts, columns, blocks):
    folds, groups = lax.axis_size("fold"), lax.axis_size("group")
    slots = right_side.shape[1] // LANES
    owned = blocks.shape[0]
    rows = owned // folds
    factors = step_factors()
    steps, depth = factors.shape[1], DEPTH
    reach, outer = HB * depth, HB * (depth - 1)
    smem = pl.BlockSpec(memory_space=pltpu.SMEM)
    vmem = pl.BlockSpec(memory_space=pltpu.VMEM)
    anywhere = pl.BlockSpec(memory_space=pl.ANY)
    f32, i32 = jnp.float32, jnp.int32
    dma = pltpu.SemaphoreType.DMA

    def vectors(*shape):
        return pltpu.VMEM(shape + (NV, LANES), f32)

    return pl.pallas_call(
        functools.partial(kernel, steps, rows, groups, depth),
        out_shape=jax.ShapeDtypeStruct(right_side.shape, f32),
        in_specs=[smem, smem, anywhere, vmem, vmem, anywhere],
        out_specs=vmem,
        scratch_shapes=[
            pltpu.VMEM(right_side.shape, f32),
            vectors(2, slots + 3),
            vectors(owned),
            vectors(folds, rows),
            pltpu.VMEM((rows, KB, LANES, LANES), f32),
            pltpu.VMEM((outer, KB, LANES, LANES), f32),
            pltpu.VMEM((outer, KB, LANES, LANES), f32),
            pltpu.VMEM((rows + 2 * outer, KB * LANES, 2 * LANES), jnp.bfloat16),
            pltpu.SMEM((rows + 2 * outer, KB), i32),
            pltpu.SMEM((owned + 16, KB), i32),
            pltpu.VMEM((2, 8, KB), i32),
            pltpu.VMEM((2, rows + 2 * reach, 2 * NV, LANES), jnp.bfloat16),
            vectors(2, rows),
            vectors(2, rows),
            vectors(rows + 2 * outer),
            vectors(rows + 2 * outer),
            vectors(rows),
            vectors(rows),
            vectors(2, 2, reach),
            vectors(2, 2, outer),
            vectors(owned),
            dma((3,)), dma((3,)), dma((2, 2)), dma((2, 2)), dma, dma, dma((8,)), dma((8,)),
            dma((2, 2, 2)), dma((2, 2, 2)), dma((7,)), dma((8,)),
        ],
        compiler_params=pltpu.CompilerParams(collective_id=0, has_side_effects=True),
    )(jnp.asarray(factors), counts, columns, right_side, initial, blocks)


def solution(mesh):
    placed = (
        P(None, ("group", "fold")),
        P(None, ("group", "fold")),
        P("group", None),
        P("group", None),
        P("group", None, None, None),
    )
    return jax.shard_map(
        on_device, mesh=mesh, in_specs=placed, out_specs=P(None, ("group", "fold")), check_vma=False
    )
```

```python
import functools

import jax
import jax.numpy as jnp
from jax import lax
from jax.experimental import pallas as pl
from jax.experimental.pallas import tpu as pltpu
from jax.sharding import PartitionSpec as P

MESH = pl.DeviceIdType.MESH
HB = 3
SWEEPS = 3
DEGREE = 4
KB = 5
NV = 16
LANES = 128
FOLDS = 8
CHIPS = 4
DEPTH = 2

upper_bound = 4.5
lower_bound = 1.35


def step_factors():
    theta = (upper_bound + lower_bound) / 2.0
    delta = (upper_bound - lower_bound) / 2.0
    keep, gain = [0.0], [1.0 / theta]
    ratio = delta / theta
    for step in range(DEGREE - 1):
        ratio_next = 1.0 / (2.0 * theta / delta - ratio)
        keep.append(ratio_next * ratio)
        gain.append(2.0 * ratio_next / delta)
        ratio = ratio_next
    return keep, gain


def split(value):
    high = value.astype(jnp.bfloat16)
    low = (value - high.astype(jnp.float32)).astype(jnp.bfloat16)
    return high, low


def position_of(fold):
    chip, core = fold // 2, fold % 2
    return chip + core * (7 - 2 * chip)


def fold_of(position):
    core = position // 4
    chip = position + core * (7 - 2 * position)
    return 2 * chip + core


def kernel(
    rows, groups, depth,
    counts_in, columns, right_side, initial, blocks, out,
    counts, mine, raw, aligned, sent, parts, raw_own, raw_left, raw_right, weights, order, all_columns, edge_columns,
    vector_even, vector_odd, update, resid, mid_update, mid_resid, iterate, partial, halo_update, halo_resid, gathered,
    block_sem, column_sem, edge_send, edge_recv, a_send, a_recv, b_send, b_recv, h_send, h_recv, c_send, c_recv,
):
    group, fold = lax.axis_index("group"), lax.axis_index("fold")
    chip, core = fold // 2, fold % 2
    place = position_of(fold)
    partner = chip * 2 + (1 - core)
    slots = right_side.shape[1] // LANES
    owned = rows * FOLDS
    reach = HB * depth
    outer = HB * (depth - 1)
    wide = rows + 2 * outer
    zero = jnp.zeros((NV, LANES), jnp.float32)

    rank = group * FOLDS + place
    last = groups * FOLDS - 1
    has_left, has_right = rank > 0, rank < last
    left_edge, right_edge = jnp.logical_and(place == 0, has_left), jnp.logical_and(place == FOLDS - 1, has_right)
    left = {"group": group - (7 - place) // 7, "fold": fold_of((place + 7) % 8)}
    right = {"group": group + place // 7, "fold": fold_of((place + 1) % 8)}

    own_blocks = pltpu.make_async_copy(
        blocks.at[pl.ds(place * rows, rows)], raw_own, block_sem.at[0]
    )
    left_blocks = pltpu.make_async_copy(
        blocks.at[pl.ds(jnp.maximum(place * rows - outer, 0), outer)], raw_left, block_sem.at[1]
    )
    right_blocks = pltpu.make_async_copy(
        blocks.at[pl.ds(jnp.minimum(place * rows + rows, owned - outer), outer)],
        raw_right, block_sem.at[2]
    )
    own_columns = pltpu.make_async_copy(columns, all_columns.at[1], column_sem.at[0])
    barrier = pltpu.get_barrier_semaphore()
    @pl.when(left_edge)
    def _():
        pl.semaphore_signal(barrier, inc=1, device_id=left, device_id_type=MESH)

    @pl.when(right_edge)
    def _():
        pl.semaphore_signal(barrier, inc=1, device_id=right, device_id_type=MESH)

    for other in (4, 3, 5, 2, 6, 1, 7):
        pl.semaphore_signal(barrier, inc=1, device_id={"group": group, "fold": (fold + other) % FOLDS}, device_id_type=MESH)

    own_counts = pltpu.make_async_copy(counts_in, counts, column_sem.at[3])
    own_counts.start()

    def own_slots_copy(source):
        return pltpu.make_async_copy(source, mine, block_sem.at[3])

    @pl.when(core == 0)
    def _():
        own_slots_copy(right_side).start()

    @pl.when(core == 1)
    def _():
        own_slots_copy(initial).start()

    own_columns.start()
    own_blocks.start()

    @pl.when(place > 0)
    def _():
        left_blocks.start()

    @pl.when(place < FOLDS - 1)
    def _():
        right_blocks.start()

    outside = (7 - place) // 7 * ((rank + last) // (last + 1)) + place // 7 * (1 - (rank + 1) // (last + 1))
    pl.semaphore_wait(barrier, FOLDS - 1 + outside)

    def swap(source):
        return pltpu.make_async_remote_copy(
            src_ref=source, dst_ref=raw, send_sem=a_send, recv_sem=a_recv,
            device_id={"group": group, "fold": partner}, device_id_type=MESH,
        )

    @pl.when(core == 0)
    def _():
        swap(initial).start()

    @pl.when(core == 1)
    def _():
        swap(right_side).start()

    def edge_left():
        return [
            pltpu.make_async_remote_copy(
                src_ref=columns, dst_ref=edge_columns.at[1],
                send_sem=edge_send.at[0, 0], recv_sem=edge_recv.at[0, 1], device_id=left, device_id_type=MESH,
            ),
            pltpu.make_async_remote_copy(
                src_ref=blocks.at[pl.ds(0, outer)], dst_ref=raw_right,
                send_sem=edge_send.at[1, 0], recv_sem=edge_recv.at[1, 1], device_id=left, device_id_type=MESH,
            ),
        ]

    def edge_right():
        return [
            pltpu.make_async_remote_copy(
                src_ref=columns, dst_ref=edge_columns.at[0],
                send_sem=edge_send.at[0, 1], recv_sem=edge_recv.at[0, 0], device_id=right, device_id_type=MESH,
            ),
            pltpu.make_async_remote_copy(
                src_ref=blocks.at[pl.ds(owned - outer, outer)], dst_ref=raw_left,
                send_sem=edge_send.at[1, 1], recv_sem=edge_recv.at[1, 0], device_id=right, device_id_type=MESH,
            ),
        ]

    @pl.when(left_edge)
    def _():
        for copy in edge_left():
            copy.start()

    @pl.when(right_edge)
    def _():
        for copy in edge_right():
            copy.start()

    lane = lax.broadcasted_iota(jnp.int32, (NV, LANES), 1)

    def start_of(which):
        total = jnp.int32(0)
        for i in range(FOLDS):
            total = total + jnp.where(i < which, counts[0, i], 0)
        return total

    def count_of(which):
        total = jnp.int32(0)
        for i in range(FOLDS):
            total = total + jnp.where(i == which, counts[0, i], 0)
        return total

    def align(source, which):
        start, count = start_of(chip * 2 + which), count_of(chip * 2 + which)
        shift = start & (LANES - 1)
        aligned[which, 0] = zero
        aligned[which, slots + 2] = zero
        before = zero
        for m in range(slots + 1):
            if m < slots:
                now = pltpu.roll(source[:, m * LANES:(m + 1) * LANES], shift, 1)
            else:
                now = zero
            slot = lane + (m * LANES - shift)
            value = jnp.where(lane < shift, before, now)
            live = jnp.logical_and(slot >= 0, slot < count)
            aligned[which, m + 1] = jnp.where(live, value, 0.0)
            before = now

    own_counts.wait()
    own_slots_copy(initial).wait()

    @pl.when(core == 0)
    def _():
        align(mine, 0)

    @pl.when(core == 1)
    def _():
        align(mine, 1)

    swap(initial).wait()

    @pl.when(core == 0)
    def _():
        align(raw, 1)

    @pl.when(core == 1)
    def _():
        align(raw, 0)

    first = [start_of(chip * 2) // LANES, start_of(chip * 2 + 1) // LANES]

    def row_block(index):
        at = [jnp.clip(index - first[i], -1, slots + 1) + 1 for i in range(2)]
        return aligned[0, at[0]] + aligned[1, at[1]]

    def message(other):
        dest = (fold + other) % FOLDS
        where = position_of(dest) * rows
        return where, pltpu.make_async_remote_copy(
            src_ref=sent.at[pl.ds(where, rows)], dst_ref=parts.at[fold],
            send_sem=b_send.at[other], recv_sem=b_recv.at[fold],
            device_id={"group": group, "fold": dest}, device_id_type=MESH,
        )

    def reachable(source, dest):
        low = jnp.logical_and(source == CHIPS - 1, dest < FOLDS // 2)
        return jnp.logical_not(jnp.logical_or(low, jnp.logical_and(source == 0, dest >= FOLDS // 2)))

    def arrival(source):
        return pltpu.make_async_remote_copy(
            src_ref=sent.at[pl.ds(0, rows)], dst_ref=parts.at[source],
            send_sem=b_send.at[0], recv_sem=b_recv.at[source],
            device_id={"group": group, "fold": fold}, device_id_type=MESH,
        )

    for other in (4, 3, 5, 2, 6, 1, 7):
        where, copy = message(other)
        for b in range(rows):
            sent[where + b] = row_block(where + b)

        @pl.when(reachable(chip, position_of((fold + other) % FOLDS)))
        def _():
            copy.start()

    for b in range(rows):
        parts[fold, b] = row_block(place * rows + b)
    for other in range(1, FOLDS):
        source = (fold + other) % FOLDS

        @pl.when(jnp.logical_not(reachable(source // 2, place)))
        def _():
            for b in range(rows):
                parts[source, b] = zero


    def prepare(source, low, high):
        @pl.loop(low, high)
        def _(e):
            at_row = place * rows + e - outer + owned
            owner, within = at_row // owned, at_row % owned
            move = (owner - 1) * owned - place * rows + outer
            column = [all_columns[owner, k, within] for k in range(KB)]
            ranks = []
            for k in range(KB):
                r = jnp.int32(0)
                for other in range(KB):
                    if other != k:
                        ahead = column[other] <= column[k] if other < k else column[other] < column[k]
                        r = r + ahead.astype(jnp.int32)
                ranks.append(r)
            for s in range(KB):
                from_slot, at = jnp.int32(0), jnp.int32(0)
                for k in range(KB):
                    from_slot = from_slot + jnp.where(ranks[k] == s, k, 0)
                    at = at + jnp.where(ranks[k] == s, column[k], 0)
                order[e, s] = jnp.clip(at + move, 0, rows + 2 * reach - 1)
                high_part, low_part = split(source[e - low, from_slot].T)
                weights[e, s * LANES:(s + 1) * LANES, 0:LANES] = high_part
                weights[e, s * LANES:(s + 1) * LANES, LANES:2 * LANES] = low_part

    def absent(low, side):
        for e in range(low, low + outer):
            for s in range(KB):
                order[e, s] = 0
            weights[e] = jnp.zeros((KB * LANES, 2 * LANES), jnp.bfloat16)
        for parity in range(2):
            for b in range(reach):
                halo_update[parity, side, b] = zero
            for b in range(outer):
                halo_resid[parity, side, b] = zero

    own_columns.wait()
    own_blocks.wait()
    prepare(raw_own, outer, outer + rows)

    @pl.when(place > 0)
    def _():
        left_blocks.wait()
        prepare(raw_left, 0, outer)

    @pl.when(place < FOLDS - 1)
    def _():
        right_blocks.wait()
        prepare(raw_right, outer + rows, wide)

    @pl.when(jnp.logical_not(has_left))
    def _():
        absent(0, 0)

    @pl.when(jnp.logical_not(has_right))
    def _():
        absent(outer + rows, 1)

    vectors = [vector_even, vector_odd]

    def store_vector(which, index, value):
        high, low = split(value)
        vectors[which][index, 0:NV] = high
        vectors[which][index, NV:2 * NV] = low

    for other in range(1, FOLDS):
        source = (fold + other) % FOLDS

        @pl.when(reachable(source // 2, place))
        def _():
            arrival(source).wait_recv()

    for b in range(rows):
        resid[0, b] = (parts[0, b] + parts[2, b]) + (parts[4, b] + parts[6, b])
        begun = (parts[1, b] + parts[3, b]) + (parts[5, b] + parts[7, b])
        update[0, b] = begun
        iterate[b] = zero
        store_vector(0, reach + b, begun)

    def exchange(parity):
        def copy(source, target, side, which):
            return pltpu.make_async_remote_copy(
                src_ref=source, dst_ref=target,
                send_sem=h_send.at[parity, side, which], recv_sem=h_recv.at[parity, 1 - side, which],
                device_id=right if side else left, device_id_type=MESH,
            )

        return [
            [
                copy(update.at[parity, pl.ds(0, reach)], halo_update.at[parity, 1], 0, 0),
                copy(resid.at[parity, pl.ds(0, outer)], halo_resid.at[parity, 1], 0, 1),
            ],
            [
                copy(update.at[parity, pl.ds(rows - reach, reach)], halo_update.at[parity, 0], 1, 0),
                copy(resid.at[parity, pl.ds(rows - outer, outer)], halo_resid.at[parity, 0], 1, 1),
            ],
        ]

    def send(parity):
        copies = exchange(parity)
        for which in range(2):
            @pl.when(has_left)
            def _():
                copies[0][which].start()

            @pl.when(has_right)
            def _():
                copies[1][which].start()

    def receive(parity, which):
        copies = exchange(parity)

        @pl.when(has_left)
        def _():
            copies[1][which].wait_recv()

        @pl.when(has_right)
        def _():
            copies[0][which].wait_recv()

    send(0)

    for other in range(1, FOLDS):
        @pl.when(reachable(chip, position_of((fold + other) % FOLDS)))
        def _():
            message(other)[1].wait_send()


    def edge_done(side):
        arrived = (edge_left if side else edge_right)()
        arrived[0].wait_recv()
        into = pltpu.make_async_copy(
            edge_columns.at[side], all_columns.at[2 * side], column_sem.at[1 + side]
        )
        into.start()
        into.wait()
        arrived[1].wait_recv()
        prepare(raw_right if side else raw_left, side * (outer + rows), side * (outer + rows) + outer)
        for copy in (edge_right if side else edge_left)():
            copy.wait_send()

    def product(which, e, low, high):
        lhs = jnp.concatenate([vectors[which][order[e, s]] for s in range(low, high)], axis=1)
        full = jnp.dot(lhs, weights[e, low * LANES:high * LANES, :], preferred_element_type=jnp.float32)
        return (full[:NV, :LANES] + full[:NV, LANES:]) + (full[NV:, :LANES] + full[NV:, LANES:])

    def own_slots(j):
        return max(0, HB - j), KB - max(0, HB - (rows - 1 - j))

    keeps, gains = step_factors()
    rounds = SWEEPS * DEGREE // depth

    @pl.loop(0, rounds)
    def _(turn):
        parity = turn % 2

        for level in range(depth):
            now, later = level % 2, (level + 1) % 2
            keep, gain = jnp.float32(keeps[level]), jnp.float32(gains[level])
            for phase in range(1, DEGREE // depth):
                chosen = turn % (DEGREE // depth) == phase
                keep = jnp.where(chosen, jnp.float32(keeps[phase * depth + level]), keep)
                gain = jnp.where(chosen, jnp.float32(gains[phase * depth + level]), gain)

            def finish(e, applied):
                own = e - outer
                inside = 0 <= own < rows
                if level > 0:
                    old, left_over = mid_update[e], mid_resid[e]
                elif inside:
                    old, left_over = update[parity, own], resid[parity, own]
                elif own < 0:
                    old, left_over = halo_update[parity, 0, e + HB], halo_resid[parity, 0, e]
                else:
                    old, left_over = halo_update[parity, 1, own - rows], halo_resid[parity, 1, own - rows]
                left_over = left_over - applied
                fresh = keep * old + gain * left_over
                if inside:
                    iterate[own] = iterate[own] + old
                if level == depth - 1:
                    update[1 - parity, own] = fresh
                    resid[1 - parity, own] = left_over
                else:
                    mid_update[e] = fresh
                    mid_resid[e] = left_over
                store_vector(later, e + HB, fresh)

            margin = HB * (depth - 1 - level)
            if level > 0:
                for e in range(outer - margin, outer + rows + margin):
                    finish(e, product(now, e, 0, KB))
                continue

            for j in range(rows):
                low, high = own_slots(j)
                applied = product(now, j + outer, low, high)
                if high - low == KB:
                    finish(j + outer, applied)
                else:
                    partial[j] = applied
            receive(parity, 0)
            for b in range(reach):
                store_vector(now, b, halo_update[parity, 0, b])
                store_vector(now, reach + rows + b, halo_update[parity, 1, b])
            for j in range(rows):
                low, high = own_slots(j)
                if low > 0:
                    finish(j + outer, partial[j] + product(now, j + outer, 0, low))
                elif high < KB:
                    finish(j + outer, partial[j] + product(now, j + outer, high, KB))
            receive(parity, 1)

            @pl.when(jnp.logical_and(turn == 0, left_edge))
            def _():
                edge_done(0)

            @pl.when(jnp.logical_and(turn == 0, right_edge))
            def _():
                edge_done(1)

            for e in list(range(outer)) + list(range(outer + rows, wide)):
                finish(e, product(now, e, 0, KB))

        copies = exchange(parity)
        for which in range(2):
            @pl.when(has_left)
            def _():
                copies[0][which].wait_send()

            @pl.when(has_right)
            def _():
                copies[1][which].wait_send()

        @pl.when(turn + 1 < rounds)
        def _():
            send(1 - parity)

    for b in range(rows):
        gathered[place * rows + b] = iterate[b] + update[rounds % 2, b]

    def piece(where, dest, which):
        return pltpu.make_async_remote_copy(
            src_ref=gathered.at[pl.ds(where * rows, rows)], dst_ref=gathered.at[pl.ds(where * rows, rows)],
            send_sem=c_send.at[which], recv_sem=c_recv.at[where],
            device_id={"group": group, "fold": dest}, device_id_type=MESH,
        )

    for other in (2, 1, 3):
        piece(place, (fold + 2 * other) % FOLDS, other).start()
    piece(place, partner, 0).start()
    for other in (1, 3, 2):
        where = position_of((fold + 2 * other) % FOLDS)
        piece(where, partner, 0).wait_recv()
        piece(where, partner, 3 + other).start()
    for other in range(CHIPS):
        where = position_of((partner + 2 * other) % FOLDS)
        piece(where, partner, 0).wait_recv()

    begin, live = start_of(fold), count_of(fold)
    shift = begin & (LANES - 1)
    base = begin // LANES
    back = (LANES - shift) & (LANES - 1)

    def shifted(m):
        return pltpu.roll(gathered[jnp.minimum(base + m, owned - 1)], back, 1)

    here = shifted(0)
    for m in range(slots):
        after = shifted(m + 1)
        value = jnp.where(lane < LANES - shift, here, after)
        out[:, m * LANES:(m + 1) * LANES] = jnp.where(lane + m * LANES < live, value, 0.0)
        here = after

    for which in range(7):
        piece(place, partner, which).wait_send()


def on_device(right_side, initial, counts, columns, blocks):
    folds, groups = lax.axis_size("fold"), lax.axis_size("group")
    slots = right_side.shape[1] // LANES
    owned = blocks.shape[0]
    rows = owned // folds
    depth = DEPTH
    reach, outer = HB * depth, HB * (depth - 1)
    vmem = pl.BlockSpec(memory_space=pltpu.VMEM)
    anywhere = pl.BlockSpec(memory_space=pl.ANY)
    f32, i32 = jnp.float32, jnp.int32
    dma = pltpu.SemaphoreType.DMA

    def vectors(*shape):
        return pltpu.VMEM(shape + (NV, LANES), f32)

    return pl.pallas_call(
        functools.partial(kernel, rows, groups, depth),
        out_shape=jax.ShapeDtypeStruct(right_side.shape, f32),
        in_specs=[anywhere] * 5,
        out_specs=vmem,
        scratch_shapes=[
            pltpu.SMEM(counts.shape, i32),
            pltpu.VMEM(right_side.shape, f32),
            pltpu.VMEM(right_side.shape, f32),
            vectors(2, slots + 3),
            vectors(owned),
            vectors(folds, rows),
            pltpu.VMEM((rows, KB, LANES, LANES), f32),
            pltpu.VMEM((outer, KB, LANES, LANES), f32),
            pltpu.VMEM((outer, KB, LANES, LANES), f32),
            pltpu.VMEM((rows + 2 * outer, KB * LANES, 2 * LANES), jnp.bfloat16),
            pltpu.SMEM((rows + 2 * outer, KB), i32),
            pltpu.SMEM((3, KB, owned), i32),
            pltpu.VMEM((2, KB, owned), i32),
            pltpu.VMEM((rows + 2 * reach, 2 * NV, LANES), jnp.bfloat16),
            pltpu.VMEM((rows + 2 * reach, 2 * NV, LANES), jnp.bfloat16),
            vectors(2, rows),
            vectors(2, rows),
            vectors(rows + 2 * outer),
            vectors(rows + 2 * outer),
            vectors(rows),
            vectors(rows),
            vectors(2, 2, reach),
            vectors(2, 2, outer),
            vectors(owned),
            dma((4,)), dma((4,)), dma((2, 2)), dma((2, 2)), dma, dma, dma((8,)), dma((8,)),
            dma((2, 2, 2)), dma((2, 2, 2)), dma((7,)), dma((8,)),
        ],
        compiler_params=pltpu.CompilerParams(collective_id=0, has_side_effects=True),
    )(counts, columns.T, right_side, initial, blocks)


def solution(mesh):
    placed = (
        P(None, ("group", "fold")),
        P(None, ("group", "fold")),
        P("group", None),
        P("group", None),
        P("group", None, None, None),
    )
    return jax.shard_map(
        on_device, mesh=mesh, in_specs=placed, out_specs=P(None, ("group", "fold")), check_vma=False
    )
```

```python
import functools

import jax
import jax.numpy as jnp
from jax import lax
from jax.experimental import pallas as pl
from jax.experimental.pallas import tpu as pltpu
from jax.sharding import PartitionSpec as P

MESH = pl.DeviceIdType.MESH
HB = 3
SWEEPS = 3
DEGREE = 4
KB = 5
NV = 16
LANES = 128
FOLDS = 8
CHIPS = 4
DEPTH = 2
EARLY = 2

upper_bound = 4.5
lower_bound = 1.35


def step_factors():
    theta = (upper_bound + lower_bound) / 2.0
    delta = (upper_bound - lower_bound) / 2.0
    keep, gain = [0.0], [1.0 / theta]
    ratio = delta / theta
    for step in range(DEGREE - 1):
        ratio_next = 1.0 / (2.0 * theta / delta - ratio)
        keep.append(ratio_next * ratio)
        gain.append(2.0 * ratio_next / delta)
        ratio = ratio_next
    return keep, gain


def split(value):
    high = value.astype(jnp.bfloat16)
    low = (value - high.astype(jnp.float32)).astype(jnp.bfloat16)
    return high, low


def position_of(fold):
    chip, core = fold // 2, fold % 2
    return chip + core * (7 - 2 * chip)


def fold_of(position):
    core = position // 4
    chip = position + core * (7 - 2 * position)
    return 2 * chip + core


def kernel(
    rows, groups, depth,
    counts_in, columns, right_side, initial, blocks, out,
    counts, mine, raw, aligned, sent, parts, raw_own, raw_left, raw_right, left_last, right_last, weights, order, all_columns, edge_columns,
    vector_even, vector_odd, update, resid, mid_update, mid_resid, iterate, partial, halo_update, halo_resid, gathered,
    block_sem, column_sem, edge_send, edge_recv, a_send, a_recv, b_send, b_recv, h_send, h_recv, c_send, c_recv,
):
    group, fold = lax.axis_index("group"), lax.axis_index("fold")
    chip, core = fold // 2, fold % 2
    place = position_of(fold)
    partner = chip * 2 + (1 - core)
    slots = right_side.shape[1] // LANES
    owned = rows * FOLDS
    reach = HB * depth
    outer = HB * (depth - 1)
    wide = rows + 2 * outer
    zero = jnp.zeros((NV, LANES), jnp.float32)

    rank = group * FOLDS + place
    last = groups * FOLDS - 1
    has_left, has_right = rank > 0, rank < last
    left_edge, right_edge = jnp.logical_and(place == 0, has_left), jnp.logical_and(place == FOLDS - 1, has_right)
    left = {"group": group - (7 - place) // 7, "fold": fold_of((place + 7) % 8)}
    right = {"group": group + place // 7, "fold": fold_of((place + 1) % 8)}

    own_blocks = pltpu.make_async_copy(
        blocks.at[pl.ds(place * rows, rows)], raw_own, block_sem.at[0]
    )
    most = outer - 1
    raw_last = [left_last, right_last]

    def beside(side):
        begin = jnp.minimum(place * rows + rows, owned - outer) if side else jnp.maximum(place * rows - outer, 0)
        return [
            pltpu.make_async_copy(
                blocks.at[pl.ds(begin, most)], (raw_right if side else raw_left), block_sem.at[1 + 2 * side]
            ),
            pltpu.make_async_copy(blocks.at[begin + most], raw_last[side], block_sem.at[2 + 2 * side]),
        ]

    own_columns = pltpu.make_async_copy(columns, all_columns.at[1], column_sem.at[0])
    barrier = pltpu.get_barrier_semaphore()
    @pl.when(left_edge)
    def _():
        pl.semaphore_signal(barrier, inc=1, device_id=left, device_id_type=MESH)

    @pl.when(right_edge)
    def _():
        pl.semaphore_signal(barrier, inc=1, device_id=right, device_id_type=MESH)

    for other in (4, 3, 5, 2, 6, 1, 7):
        pl.semaphore_signal(barrier, inc=1, device_id={"group": group, "fold": (fold + other) % FOLDS}, device_id_type=MESH)

    own_counts = pltpu.make_async_copy(counts_in, counts, column_sem.at[3])
    own_counts.start()

    def own_slots_copy(source):
        return pltpu.make_async_copy(source, mine, block_sem.at[5])

    @pl.when(core == 0)
    def _():
        own_slots_copy(right_side).start()

    @pl.when(core == 1)
    def _():
        own_slots_copy(initial).start()

    own_columns.start()
    own_blocks.start()

    @pl.when(place > 0)
    def _():
        for copy in beside(0):
            copy.start()

    @pl.when(place < FOLDS - 1)
    def _():
        for copy in beside(1):
            copy.start()

    outside = (7 - place) // 7 * ((rank + last) // (last + 1)) + place // 7 * (1 - (rank + 1) // (last + 1))
    pl.semaphore_wait(barrier, FOLDS - 1 + outside)

    def swap(source):
        return pltpu.make_async_remote_copy(
            src_ref=source, dst_ref=raw, send_sem=a_send, recv_sem=a_recv,
            device_id={"group": group, "fold": partner}, device_id_type=MESH,
        )

    @pl.when(core == 0)
    def _():
        swap(initial).start()

    @pl.when(core == 1)
    def _():
        swap(right_side).start()

    def edge(side):
        begin = owned - outer if side else 0
        target = 1 - side
        refs = [
            (columns, edge_columns.at[target]),
            (blocks.at[pl.ds(begin, most)], (raw_right if target else raw_left)),
            (blocks.at[begin + most, pl.ds(0, EARLY)], raw_last[target].at[pl.ds(0, EARLY)]),
            (blocks.at[begin + most, pl.ds(EARLY, KB - EARLY)], raw_last[target].at[pl.ds(EARLY, KB - EARLY)]),
        ]
        return [
            pltpu.make_async_remote_copy(
                src_ref=source, dst_ref=dest, send_sem=edge_send.at[i, side], recv_sem=edge_recv.at[i, target],
                device_id=right if side else left, device_id_type=MESH,
            )
            for i, (source, dest) in enumerate(refs)
        ]

    def edge_start(low, high):
        @pl.when(left_edge)
        def _():
            for copy in edge(0)[low:high]:
                copy.start()

        @pl.when(right_edge)
        def _():
            for copy in edge(1)[low:high]:
                copy.start()

    edge_start(0, 3)

    lane = lax.broadcasted_iota(jnp.int32, (NV, LANES), 1)

    def start_of(which):
        total = jnp.int32(0)
        for i in range(FOLDS):
            total = total + jnp.where(i < which, counts[0, i], 0)
        return total

    def count_of(which):
        total = jnp.int32(0)
        for i in range(FOLDS):
            total = total + jnp.where(i == which, counts[0, i], 0)
        return total

    def align(source, which):
        start, count = start_of(chip * 2 + which), count_of(chip * 2 + which)
        shift = start & (LANES - 1)
        aligned[which, 0] = zero
        aligned[which, slots + 2] = zero
        before = zero
        for m in range(slots + 1):
            if m < slots:
                now = pltpu.roll(source[:, m * LANES:(m + 1) * LANES], shift, 1)
            else:
                now = zero
            slot = lane + (m * LANES - shift)
            value = jnp.where(lane < shift, before, now)
            live = jnp.logical_and(slot >= 0, slot < count)
            aligned[which, m + 1] = jnp.where(live, value, 0.0)
            before = now

    own_counts.wait()
    own_slots_copy(initial).wait()

    @pl.when(core == 0)
    def _():
        align(mine, 0)

    @pl.when(core == 1)
    def _():
        align(mine, 1)

    swap(initial).wait()

    @pl.when(core == 0)
    def _():
        align(raw, 1)

    @pl.when(core == 1)
    def _():
        align(raw, 0)

    first = [start_of(chip * 2) // LANES, start_of(chip * 2 + 1) // LANES]

    def row_block(index):
        at = [jnp.clip(index - first[i], -1, slots + 1) + 1 for i in range(2)]
        return aligned[0, at[0]] + aligned[1, at[1]]

    def message(other):
        dest = (fold + other) % FOLDS
        where = position_of(dest) * rows
        return where, pltpu.make_async_remote_copy(
            src_ref=sent.at[pl.ds(where, rows)], dst_ref=parts.at[fold],
            send_sem=b_send.at[other], recv_sem=b_recv.at[fold],
            device_id={"group": group, "fold": dest}, device_id_type=MESH,
        )

    def reachable(source, dest):
        low = jnp.logical_and(source == CHIPS - 1, dest < FOLDS // 2)
        return jnp.logical_not(jnp.logical_or(low, jnp.logical_and(source == 0, dest >= FOLDS // 2)))

    def arrival(source):
        return pltpu.make_async_remote_copy(
            src_ref=sent.at[pl.ds(0, rows)], dst_ref=parts.at[source],
            send_sem=b_send.at[0], recv_sem=b_recv.at[source],
            device_id={"group": group, "fold": fold}, device_id_type=MESH,
        )

    for other in (4, 3, 5, 2, 6, 1, 7):
        where, copy = message(other)
        for b in range(rows):
            sent[where + b] = row_block(where + b)

        @pl.when(reachable(chip, position_of((fold + other) % FOLDS)))
        def _():
            copy.start()

    for b in range(rows):
        parts[fold, b] = row_block(place * rows + b)
    for other in range(1, FOLDS):
        source = (fold + other) % FOLDS

        @pl.when(jnp.logical_not(reachable(source // 2, place)))
        def _():
            for b in range(rows):
                parts[source, b] = zero


    def prepare(source, low, high, single=False):
        @pl.loop(low, high)
        def _(e):
            at_row = place * rows + e - outer + owned
            owner, within = at_row // owned, at_row % owned
            move = (owner - 1) * owned - place * rows + outer
            column = [all_columns[owner, k, within] for k in range(KB)]
            ranks = []
            for k in range(KB):
                r = jnp.int32(0)
                for other in range(KB):
                    if other != k:
                        ahead = column[other] <= column[k] if other < k else column[other] < column[k]
                        r = r + ahead.astype(jnp.int32)
                ranks.append(r)
            for s in range(KB):
                from_slot, at = jnp.int32(0), jnp.int32(0)
                for k in range(KB):
                    from_slot = from_slot + jnp.where(ranks[k] == s, k, 0)
                    at = at + jnp.where(ranks[k] == s, column[k], 0)
                order[e, s] = jnp.clip(at + move, 0, rows + 2 * reach - 1)
                high_part, low_part = split((source[from_slot] if single else source[e - low, from_slot]).T)
                weights[e, s * LANES:(s + 1) * LANES, 0:LANES] = high_part
                weights[e, s * LANES:(s + 1) * LANES, LANES:2 * LANES] = low_part

    def absent(low, side):
        for e in range(low, low + outer):
            for s in range(KB):
                order[e, s] = 0
            weights[e] = jnp.zeros((KB * LANES, 2 * LANES), jnp.bfloat16)
        for parity in range(2):
            for b in range(reach):
                halo_update[parity, side, b] = zero
            for b in range(outer):
                halo_resid[parity, side, b] = zero

    own_columns.wait()
    own_blocks.wait()
    prepare(raw_own, outer, outer + rows)

    def prepare_most(side):
        at = side * (outer + rows)
        prepare(raw_right if side else raw_left, at, at + most)

    def prepare_last(side):
        at = side * (outer + rows) + most
        prepare(raw_last[side], at, at + 1, single=True)

    def prepare_beside(side):
        for copy in beside(side):
            copy.wait()
        prepare_most(side)
        prepare_last(side)

    @pl.when(place > 0)
    def _():
        prepare_beside(0)

    @pl.when(place < FOLDS - 1)
    def _():
        prepare_beside(1)

    @pl.when(jnp.logical_not(has_left))
    def _():
        absent(0, 0)

    @pl.when(jnp.logical_not(has_right))
    def _():
        absent(outer + rows, 1)

    vectors = [vector_even, vector_odd]

    def store_vector(which, index, value):
        high, low = split(value)
        vectors[which][index, 0:NV] = high
        vectors[which][index, NV:2 * NV] = low

    for other in range(1, FOLDS):
        source = (fold + other) % FOLDS

        @pl.when(reachable(source // 2, place))
        def _():
            arrival(source).wait_recv()

    for b in range(rows):
        resid[0, b] = (parts[0, b] + parts[2, b]) + (parts[4, b] + parts[6, b])
        begun = (parts[1, b] + parts[3, b]) + (parts[5, b] + parts[7, b])
        update[0, b] = begun
        iterate[b] = zero
        store_vector(0, reach + b, begun)

    NEAR, REST = [0], [1, 2]

    def exchange(parity, side, which):
        source, target, length, near, into = [
            (update, halo_update, HB, 0, reach - HB), (resid, halo_resid, outer, 0, 0), (update, halo_update, reach - HB, HB, 0),
        ][which]
        if side:
            source_at, target_at = rows - near - length, into
        else:
            source_at, target_at = near, near
        return pltpu.make_async_remote_copy(
            src_ref=source.at[parity, pl.ds(source_at, length)],
            dst_ref=target.at[parity, 1 - side, pl.ds(target_at, length)],
            send_sem=h_send.at[parity, side, which], recv_sem=h_recv.at[parity, 1 - side, which],
            device_id=right if side else left, device_id_type=MESH,
        )

    inner_right = jnp.logical_and(has_right, place < FOLDS - 1)

    def send(parity, chosen):
        @pl.when(right_edge)
        def _():
            for which in chosen:
                exchange(parity, 1, which).start()

        @pl.when(has_left)
        def _():
            for which in chosen:
                exchange(parity, 0, which).start()

        @pl.when(inner_right)
        def _():
            for which in chosen:
                exchange(parity, 1, which).start()

    def sent_all(parity):
        for side, there in enumerate((has_left, has_right)):
            @pl.when(there)
            def _():
                for which in NEAR + REST:
                    exchange(parity, side, which).wait_send()

    def receive(parity, chosen):
        for side, there in enumerate((has_left, has_right)):
            @pl.when(there)
            def _():
                for which in chosen:
                    exchange(parity, 1 - side, which).wait_recv()

    send(0, NEAR)
    send(0, REST)
    edge_start(3, 4)

    for other in range(1, FOLDS):
        @pl.when(reachable(chip, position_of((fold + other) % FOLDS)))
        def _():
            message(other)[1].wait_send()


    def edge_most(side):
        arrived = edge(1 - side)
        arrived[0].wait_recv()
        into = pltpu.make_async_copy(edge_columns.at[side], all_columns.at[2 * side], column_sem.at[1 + side])
        into.start()
        into.wait()
        arrived[1].wait_recv()
        prepare_most(side)

    def edge_last(side):
        for copy in edge(1 - side)[2:]:
            copy.wait_recv()
        prepare_last(side)
        for copy in edge(side):
            copy.wait_send()

    def product(which, e, low, high):
        lhs = jnp.concatenate([vectors[which][order[e, s]] for s in range(low, high)], axis=1)
        full = jnp.dot(lhs, weights[e, low * LANES:high * LANES, :], preferred_element_type=jnp.float32)
        return (full[:NV, :LANES] + full[:NV, LANES:]) + (full[NV:, :LANES] + full[NV:, LANES:])

    def own_slots(j):
        return max(0, HB - j), KB - max(0, HB - (rows - 1 - j))

    keeps, gains = step_factors()
    rounds = SWEEPS * DEGREE // depth

    @pl.loop(0, rounds)
    def _(turn):
        parity = turn % 2

        for level in range(depth):
            now, later = level % 2, (level + 1) % 2
            keep, gain = jnp.float32(keeps[level]), jnp.float32(gains[level])
            for phase in range(1, DEGREE // depth):
                chosen = turn % (DEGREE // depth) == phase
                keep = jnp.where(chosen, jnp.float32(keeps[phase * depth + level]), keep)
                gain = jnp.where(chosen, jnp.float32(gains[phase * depth + level]), gain)

            def finish(e, applied):
                own = e - outer
                inside = 0 <= own < rows
                if level > 0:
                    old, left_over = mid_update[e], mid_resid[e]
                elif inside:
                    old, left_over = update[parity, own], resid[parity, own]
                elif own < 0:
                    old, left_over = halo_update[parity, 0, e + HB], halo_resid[parity, 0, e]
                else:
                    old, left_over = halo_update[parity, 1, own - rows], halo_resid[parity, 1, own - rows]
                left_over = left_over - applied
                fresh = keep * old + gain * left_over
                if inside:
                    iterate[own] = iterate[own] + old
                if level == depth - 1:
                    update[1 - parity, own] = fresh
                    resid[1 - parity, own] = left_over
                else:
                    mid_update[e] = fresh
                    mid_resid[e] = left_over
                store_vector(later, e + HB, fresh)

            margin = HB * (depth - 1 - level)
            if level > 0:
                ends = list(range(HB)) + list(range(rows - HB, rows))
                for j in ends:
                    finish(j + outer, product(now, j + outer, 0, KB))

                @pl.when(turn + 1 < rounds)
                def _():
                    send(1 - parity, NEAR)

                for j in range(HB, rows - HB):
                    finish(j + outer, product(now, j + outer, 0, KB))
                continue

            for j in range(rows):
                low, high = own_slots(j)
                applied = product(now, j + outer, low, high)
                if high - low == KB:
                    finish(j + outer, applied)
                else:
                    partial[j] = applied

            def first_turn(there, act, side):
                @pl.when(jnp.logical_and(turn == 0, there))
                def _():
                    act(side)

            first_turn(left_edge, edge_most, 0)
            first_turn(right_edge, edge_most, 1)
            receive(parity, NEAR)
            for b in range(HB):
                store_vector(now, reach - HB + b, halo_update[parity, 0, reach - HB + b])
                store_vector(now, reach + rows + b, halo_update[parity, 1, b])
            for j in range(rows):
                low, high = own_slots(j)
                if low > 0:
                    finish(j + outer, partial[j] + product(now, j + outer, 0, low))
                elif high < KB:
                    finish(j + outer, partial[j] + product(now, j + outer, high, KB))
            receive(parity, REST)
            for b in range(reach - HB):
                store_vector(now, b, halo_update[parity, 0, b])
                store_vector(now, reach + rows + HB + b, halo_update[parity, 1, HB + b])
            first_turn(left_edge, edge_last, 0)
            first_turn(right_edge, edge_last, 1)
            for e in list(range(outer)) + list(range(outer + rows, wide)):
                finish(e, product(now, e, 0, KB))
            sent_all(parity)

        @pl.when(turn + 1 < rounds)
        def _():
            send(1 - parity, REST)

    for b in range(rows):
        gathered[place * rows + b] = iterate[b] + update[rounds % 2, b]

    def piece(where, dest, which):
        return pltpu.make_async_remote_copy(
            src_ref=gathered.at[pl.ds(where * rows, rows)], dst_ref=gathered.at[pl.ds(where * rows, rows)],
            send_sem=c_send.at[which], recv_sem=c_recv.at[where],
            device_id={"group": group, "fold": dest}, device_id_type=MESH,
        )

    for other in (2, 1, 3):
        piece(place, (fold + 2 * other) % FOLDS, other).start()
    piece(place, partner, 0).start()
    for other in (1, 3, 2):
        where = position_of((fold + 2 * other) % FOLDS)
        piece(where, partner, 0).wait_recv()
        piece(where, partner, 3 + other).start()
    for other in range(CHIPS):
        where = position_of((partner + 2 * other) % FOLDS)
        piece(where, partner, 0).wait_recv()

    begin, live = start_of(fold), count_of(fold)
    shift = begin & (LANES - 1)
    base = begin // LANES
    back = (LANES - shift) & (LANES - 1)

    def shifted(m):
        return pltpu.roll(gathered[jnp.minimum(base + m, owned - 1)], back, 1)

    here = shifted(0)
    for m in range(slots):
        after = shifted(m + 1)
        value = jnp.where(lane < LANES - shift, here, after)
        out[:, m * LANES:(m + 1) * LANES] = jnp.where(lane + m * LANES < live, value, 0.0)
        here = after

    for which in range(7):
        piece(place, partner, which).wait_send()


def on_device(right_side, initial, counts, columns, blocks):
    folds, groups = lax.axis_size("fold"), lax.axis_size("group")
    slots = right_side.shape[1] // LANES
    owned = blocks.shape[0]
    rows = owned // folds
    depth = DEPTH
    reach, outer = HB * depth, HB * (depth - 1)
    vmem = pl.BlockSpec(memory_space=pltpu.VMEM)
    anywhere = pl.BlockSpec(memory_space=pl.ANY)
    f32, i32 = jnp.float32, jnp.int32
    dma = pltpu.SemaphoreType.DMA

    def vectors(*shape):
        return pltpu.VMEM(shape + (NV, LANES), f32)

    return pl.pallas_call(
        functools.partial(kernel, rows, groups, depth),
        out_shape=jax.ShapeDtypeStruct(right_side.shape, f32),
        in_specs=[anywhere] * 5,
        out_specs=vmem,
        scratch_shapes=[
            pltpu.SMEM(counts.shape, i32),
            pltpu.VMEM(right_side.shape, f32),
            pltpu.VMEM(right_side.shape, f32),
            vectors(2, slots + 3),
            vectors(owned),
            vectors(folds, rows),
            pltpu.VMEM((rows, KB, LANES, LANES), f32),
            pltpu.VMEM((outer - 1, KB, LANES, LANES), f32),
            pltpu.VMEM((outer - 1, KB, LANES, LANES), f32),
            pltpu.VMEM((KB, LANES, LANES), f32),
            pltpu.VMEM((KB, LANES, LANES), f32),
            pltpu.VMEM((rows + 2 * outer, KB * LANES, 2 * LANES), jnp.bfloat16),
            pltpu.SMEM((rows + 2 * outer, KB), i32),
            pltpu.SMEM((3, KB, owned), i32),
            pltpu.VMEM((2, KB, owned), i32),
            pltpu.VMEM((rows + 2 * reach, 2 * NV, LANES), jnp.bfloat16),
            pltpu.VMEM((rows + 2 * reach, 2 * NV, LANES), jnp.bfloat16),
            vectors(2, rows),
            vectors(2, rows),
            vectors(rows + 2 * outer),
            vectors(rows + 2 * outer),
            vectors(rows),
            vectors(rows),
            vectors(2, 2, reach),
            vectors(2, 2, outer),
            vectors(owned),
            dma((6,)), dma((4,)), dma((4, 2)), dma((4, 2)), dma, dma, dma((8,)), dma((8,)),
            dma((2, 2, 3)), dma((2, 2, 3)), dma((7,)), dma((8,)),
        ],
        compiler_params=pltpu.CompilerParams(collective_id=0, has_side_effects=True),
    )(counts, columns.T, right_side, initial, blocks)


def solution(mesh):
    placed = (
        P(None, ("group", "fold")),
        P(None, ("group", "fold")),
        P("group", None),
        P("group", None),
        P("group", None, None, None),
    )
    return jax.shard_map(
        on_device, mesh=mesh, in_specs=placed, out_specs=P(None, ("group", "fold")), check_vma=False
    )
```

```python
import functools

import jax
import jax.numpy as jnp
from jax import lax
from jax.experimental import pallas as pl
from jax.experimental.pallas import tpu as pltpu
from jax.sharding import PartitionSpec as P

MESH = pl.DeviceIdType.MESH
HB = 3
SWEEPS = 3
DEGREE = 4
KB = 5
NV = 16
LANES = 128
FOLDS = 8
CHIPS = 4
DEPTH = 2
EARLY = 4

upper_bound = 4.5
lower_bound = 1.35


def step_factors():
    theta = (upper_bound + lower_bound) / 2.0
    delta = (upper_bound - lower_bound) / 2.0
    keep, gain = [0.0], [1.0 / theta]
    ratio = delta / theta
    for step in range(DEGREE - 1):
        ratio_next = 1.0 / (2.0 * theta / delta - ratio)
        keep.append(ratio_next * ratio)
        gain.append(2.0 * ratio_next / delta)
        ratio = ratio_next
    return keep, gain


def split(value):
    high = value.astype(jnp.bfloat16)
    low = (value - high.astype(jnp.float32)).astype(jnp.bfloat16)
    return high, low


def position_of(fold):
    chip, core = fold // 2, fold % 2
    return chip + core * (7 - 2 * chip)


def fold_of(position):
    core = position // 4
    chip = position + core * (7 - 2 * position)
    return 2 * chip + core


def kernel(
    rows, groups, depth,
    counts_in, columns, right_side, initial, blocks, out,
    counts, mine, raw, aligned, sent, parts, raw_own, raw_left, raw_right, left_last, right_last, weights, order, all_columns, edge_columns,
    vector_even, vector_odd, update, resid, mid_update, mid_resid, iterate, partial, halo_update, halo_resid, gathered,
    block_sem, column_sem, edge_send, edge_recv, a_send, a_recv, b_send, b_recv, h_send, h_recv, c_send, c_recv,
):
    group, fold = lax.axis_index("group"), lax.axis_index("fold")
    chip, core = fold // 2, fold % 2
    place = position_of(fold)
    partner = chip * 2 + (1 - core)
    slots = right_side.shape[1] // LANES
    owned = rows * FOLDS
    reach = HB * depth
    outer = HB * (depth - 1)
    wide = rows + 2 * outer
    zero = jnp.zeros((NV, LANES), jnp.float32)

    rank = group * FOLDS + place
    last = groups * FOLDS - 1
    has_left, has_right = rank > 0, rank < last
    left_edge, right_edge = jnp.logical_and(place == 0, has_left), jnp.logical_and(place == FOLDS - 1, has_right)
    left = {"group": (group + groups - (7 - place) // 7) % groups, "fold": fold_of((place + 7) % 8)}
    right = {"group": (group + place // 7) % groups, "fold": fold_of((place + 1) % 8)}

    own_blocks = pltpu.make_async_copy(
        blocks.at[pl.ds(place * rows, rows)], raw_own, block_sem.at[0]
    )
    most = outer - 1
    raw_last = [left_last, right_last]

    def beside(side):
        begin = jnp.minimum(place * rows + rows, owned - outer) if side else jnp.maximum(place * rows - outer, 0)
        return [
            pltpu.make_async_copy(
                blocks.at[pl.ds(begin, most)], (raw_right if side else raw_left), block_sem.at[1 + 2 * side]
            ),
            pltpu.make_async_copy(blocks.at[begin + most], raw_last[side], block_sem.at[2 + 2 * side]),
        ]

    own_columns = pltpu.make_async_copy(columns, all_columns.at[1], column_sem.at[0])
    barrier = pltpu.get_barrier_semaphore()
    @pl.when(place == 0)
    def _():
        pl.semaphore_signal(barrier, inc=1, device_id=left, device_id_type=MESH)

    @pl.when(place == FOLDS - 1)
    def _():
        pl.semaphore_signal(barrier, inc=1, device_id=right, device_id_type=MESH)

    for other in (4, 3, 5, 2, 6, 1, 7):
        pl.semaphore_signal(barrier, inc=1, device_id={"group": group, "fold": (fold + other) % FOLDS}, device_id_type=MESH)

    own_counts = pltpu.make_async_copy(counts_in, counts, column_sem.at[3])
    own_counts.start()

    def own_slots_copy(source):
        return pltpu.make_async_copy(source, mine, block_sem.at[5])

    @pl.when(core == 0)
    def _():
        own_slots_copy(right_side).start()

    @pl.when(core == 1)
    def _():
        own_slots_copy(initial).start()

    own_columns.start()
    own_blocks.start()

    @pl.when(place > 0)
    def _():
        for copy in beside(0):
            copy.start()

    @pl.when(place < FOLDS - 1)
    def _():
        for copy in beside(1):
            copy.start()

    pl.semaphore_wait(barrier, FOLDS - 1 + (7 - place) // 7 + place // 7)

    def swap(source):
        return pltpu.make_async_remote_copy(
            src_ref=source, dst_ref=raw, send_sem=a_send, recv_sem=a_recv,
            device_id={"group": group, "fold": partner}, device_id_type=MESH,
        )

    @pl.when(core == 0)
    def _():
        swap(initial).start()

    @pl.when(core == 1)
    def _():
        swap(right_side).start()

    def edge(side):
        begin = owned - outer if side else 0
        target = 1 - side
        refs = [
            (columns, edge_columns.at[target]),
            (blocks.at[pl.ds(begin, most)], (raw_right if target else raw_left)),
            (blocks.at[begin + most, pl.ds(0, EARLY)], raw_last[target].at[pl.ds(0, EARLY)]),
            (blocks.at[begin + most, pl.ds(EARLY, KB - EARLY)], raw_last[target].at[pl.ds(EARLY, KB - EARLY)]),
        ]
        return [
            pltpu.make_async_remote_copy(
                src_ref=source, dst_ref=dest, send_sem=edge_send.at[i, side], recv_sem=edge_recv.at[i, target],
                device_id=right if side else left, device_id_type=MESH,
            )
            for i, (source, dest) in enumerate(refs)
        ]

    def edge_start(low, high):
        @pl.when(left_edge)
        def _():
            for copy in edge(0)[low:high]:
                copy.start()

        @pl.when(right_edge)
        def _():
            for copy in edge(1)[low:high]:
                copy.start()

    edge_start(0, 3)

    lane = lax.broadcasted_iota(jnp.int32, (NV, LANES), 1)

    def start_of(which):
        total = jnp.int32(0)
        for i in range(FOLDS):
            total = total + jnp.where(i < which, counts[0, i], 0)
        return total

    def count_of(which):
        total = jnp.int32(0)
        for i in range(FOLDS):
            total = total + jnp.where(i == which, counts[0, i], 0)
        return total

    def align(source, which):
        start, count = start_of(chip * 2 + which), count_of(chip * 2 + which)
        shift = start & (LANES - 1)
        aligned[which, 0] = zero
        aligned[which, slots + 2] = zero
        before = zero
        for m in range(slots + 1):
            if m < slots:
                now = pltpu.roll(source[:, m * LANES:(m + 1) * LANES], shift, 1)
            else:
                now = zero
            slot = lane + (m * LANES - shift)
            value = jnp.where(lane < shift, before, now)
            live = jnp.logical_and(slot >= 0, slot < count)
            aligned[which, m + 1] = jnp.where(live, value, 0.0)
            before = now

    own_counts.wait()
    own_slots_copy(initial).wait()

    @pl.when(core == 0)
    def _():
        align(mine, 0)

    @pl.when(core == 1)
    def _():
        align(mine, 1)

    swap(initial).wait()

    @pl.when(core == 0)
    def _():
        align(raw, 1)

    @pl.when(core == 1)
    def _():
        align(raw, 0)

    first = [start_of(chip * 2) // LANES, start_of(chip * 2 + 1) // LANES]

    def row_block(index):
        at = [jnp.clip(index - first[i], -1, slots + 1) + 1 for i in range(2)]
        return aligned[0, at[0]] + aligned[1, at[1]]

    def message(other):
        dest = (fold + other) % FOLDS
        where = position_of(dest) * rows
        return where, pltpu.make_async_remote_copy(
            src_ref=sent.at[pl.ds(where, rows)], dst_ref=parts.at[fold],
            send_sem=b_send.at[other], recv_sem=b_recv.at[fold],
            device_id={"group": group, "fold": dest}, device_id_type=MESH,
        )

    def reachable(source, dest):
        low = jnp.logical_and(source == CHIPS - 1, dest < FOLDS // 2)
        return jnp.logical_not(jnp.logical_or(low, jnp.logical_and(source == 0, dest >= FOLDS // 2)))

    def arrival(source):
        return pltpu.make_async_remote_copy(
            src_ref=sent.at[pl.ds(0, rows)], dst_ref=parts.at[source],
            send_sem=b_send.at[0], recv_sem=b_recv.at[source],
            device_id={"group": group, "fold": fold}, device_id_type=MESH,
        )

    for other in (4, 3, 5, 2, 6, 1, 7):
        where, copy = message(other)
        for b in range(rows):
            sent[where + b] = row_block(where + b)

        @pl.when(reachable(chip, position_of((fold + other) % FOLDS)))
        def _():
            copy.start()

    for b in range(rows):
        parts[fold, b] = row_block(place * rows + b)
    for other in range(1, FOLDS):
        source = (fold + other) % FOLDS

        @pl.when(jnp.logical_not(reachable(source // 2, place)))
        def _():
            for b in range(rows):
                parts[source, b] = zero


    def prepare(source, low, high, single=False):
        @pl.loop(low, high)
        def _(e):
            at_row = place * rows + e - outer + owned
            owner, within = at_row // owned, at_row % owned
            move = (owner - 1) * owned - place * rows + outer
            column = [all_columns[owner, k, within] for k in range(KB)]
            ranks = []
            for k in range(KB):
                r = jnp.int32(0)
                for other in range(KB):
                    if other != k:
                        ahead = column[other] <= column[k] if other < k else column[other] < column[k]
                        r = r + ahead.astype(jnp.int32)
                ranks.append(r)
            for s in range(KB):
                from_slot, at = jnp.int32(0), jnp.int32(0)
                for k in range(KB):
                    from_slot = from_slot + jnp.where(ranks[k] == s, k, 0)
                    at = at + jnp.where(ranks[k] == s, column[k], 0)
                order[e, s] = jnp.clip(at + move, 0, rows + 2 * reach - 1)
                high_part, low_part = split((source[from_slot] if single else source[e - low, from_slot]).T)
                weights[e, s * LANES:(s + 1) * LANES, 0:LANES] = high_part
                weights[e, s * LANES:(s + 1) * LANES, LANES:2 * LANES] = low_part

    def absent(low):
        for e in range(low, low + outer):
            for s in range(KB):
                order[e, s] = 0
            weights[e] = jnp.zeros((KB * LANES, 2 * LANES), jnp.bfloat16)

    own_columns.wait()
    own_blocks.wait()
    prepare(raw_own, outer, outer + rows)

    def prepare_most(side):
        at = side * (outer + rows)
        prepare(raw_right if side else raw_left, at, at + most)

    def prepare_last(side):
        at = side * (outer + rows) + most
        prepare(raw_last[side], at, at + 1, single=True)

    def prepare_beside(side):
        for copy in beside(side):
            copy.wait()
        prepare_most(side)
        prepare_last(side)

    @pl.when(place > 0)
    def _():
        prepare_beside(0)

    @pl.when(place < FOLDS - 1)
    def _():
        prepare_beside(1)

    @pl.when(jnp.logical_not(has_left))
    def _():
        absent(0)

    @pl.when(jnp.logical_not(has_right))
    def _():
        absent(outer + rows)

    vectors = [vector_even, vector_odd]

    def store_vector(which, index, value):
        high, low = split(value)
        vectors[which][index, 0:NV] = high
        vectors[which][index, NV:2 * NV] = low

    for other in range(1, FOLDS):
        source = (fold + other) % FOLDS

        @pl.when(reachable(source // 2, place))
        def _():
            arrival(source).wait_recv()

    for b in range(rows):
        resid[0, b] = (parts[0, b] + parts[2, b]) + (parts[4, b] + parts[6, b])
        begun = (parts[1, b] + parts[3, b]) + (parts[5, b] + parts[7, b])
        update[0, b] = begun
        iterate[b] = zero
        store_vector(0, reach + b, begun)

    NEAR, REST = [0], [1, 2]

    def exchange(parity, side, which):
        source, target, length, near = [
            (update, halo_update, HB, 0), (resid, halo_resid, outer, 0), (update, halo_update, reach - HB, HB),
        ][which]
        mirrored = source is update
        return pltpu.make_async_remote_copy(
            src_ref=source.at[parity, pl.ds(near + side * (rows - 2 * near - length), length)],
            dst_ref=target.at[parity, 1 - side, pl.ds(near + side * (reach - 2 * near - length if mirrored else 0), length)],
            send_sem=h_send.at[parity, side, which], recv_sem=h_recv.at[parity, 1 - side, which],
            device_id={name: left[name] + side * (right[name] - left[name]) for name in left}, device_id_type=MESH,
        )

    sides = [place // 7, 1 - place // 7]

    def send(parity, chosen):
        for which in chosen:
            for side in sides:
                exchange(parity, side, which).start()

    def sent_all(parity):
        for which in NEAR + REST:
            for side in range(2):
                exchange(parity, side, which).wait_send()

    def receive(parity, chosen):
        for which in chosen:
            for side in range(2):
                exchange(parity, 1 - side, which).wait_recv()

    def halo_of(ref, parity, side, b):
        return jnp.where(has_right if side else has_left, ref[parity, side, b], 0.0)

    send(0, NEAR)
    send(0, REST)
    edge_start(3, 4)

    for other in range(1, FOLDS):
        @pl.when(reachable(chip, position_of((fold + other) % FOLDS)))
        def _():
            message(other)[1].wait_send()


    def edge_most(side):
        arrived = edge(1 - side)
        arrived[0].wait_recv()
        into = pltpu.make_async_copy(edge_columns.at[side], all_columns.at[2 * side], column_sem.at[1 + side])
        into.start()
        into.wait()
        arrived[1].wait_recv()
        prepare_most(side)

    def edge_last(side):
        for copy in edge(1 - side)[2:]:
            copy.wait_recv()
        prepare_last(side)
        for copy in edge(side):
            copy.wait_send()

    def product(which, e, low, high):
        lhs = jnp.concatenate([vectors[which][order[e, s]] for s in range(low, high)], axis=1)
        full = jnp.dot(lhs, weights[e, low * LANES:high * LANES, :], preferred_element_type=jnp.float32)
        return (full[:NV, :LANES] + full[:NV, LANES:]) + (full[NV:, :LANES] + full[NV:, LANES:])

    def own_slots(j):
        return max(0, HB - j), KB - max(0, HB - (rows - 1 - j))

    keeps, gains = step_factors()
    rounds = SWEEPS * DEGREE // depth

    def one_turn(turn, parity, first_turn, last_turn):
        for level in range(depth):
            now, later = level % 2, (level + 1) % 2
            keep, gain = jnp.float32(keeps[level]), jnp.float32(gains[level])
            for phase in range(1, DEGREE // depth):
                chosen = turn % (DEGREE // depth) == phase
                keep = jnp.where(chosen, jnp.float32(keeps[phase * depth + level]), keep)
                gain = jnp.where(chosen, jnp.float32(gains[phase * depth + level]), gain)

            def finish(e, applied):
                own = e - outer
                inside = 0 <= own < rows
                if level > 0:
                    old, left_over = mid_update[e], mid_resid[e]
                elif inside:
                    old, left_over = update[parity, own], resid[parity, own]
                elif own < 0:
                    old, left_over = halo_of(halo_update, parity, 0, e + HB), halo_of(halo_resid, parity, 0, e)
                else:
                    old, left_over = halo_of(halo_update, parity, 1, own - rows), halo_of(halo_resid, parity, 1, own - rows)
                left_over = left_over - applied
                fresh = keep * old + gain * left_over
                if inside:
                    iterate[own] = iterate[own] + old
                if level == depth - 1:
                    update[1 - parity, own] = fresh
                    resid[1 - parity, own] = left_over
                else:
                    mid_update[e] = fresh
                    mid_resid[e] = left_over
                store_vector(later, e + HB, fresh)

            margin = HB * (depth - 1 - level)
            if level > 0:
                ends = list(range(HB)) + list(range(rows - HB, rows))
                for j in ends:
                    finish(j + outer, product(now, j + outer, 0, KB))

                if not last_turn:
                    send(1 - parity, NEAR)
                for j in range(HB, rows - HB):
                    finish(j + outer, product(now, j + outer, 0, KB))
                continue

            for j in range(rows):
                low, high = own_slots(j)
                applied = product(now, j + outer, low, high)
                if high - low == KB:
                    finish(j + outer, applied)
                else:
                    partial[j] = applied

            if first_turn:
                at_edges(edge_most)
            sent_all(parity)
            receive(parity, NEAR)
            for b in range(HB):
                store_vector(now, reach - HB + b, halo_of(halo_update, parity, 0, reach - HB + b))
                store_vector(now, reach + rows + b, halo_of(halo_update, parity, 1, b))
            for j in range(rows):
                low, high = own_slots(j)
                if low > 0:
                    finish(j + outer, partial[j] + product(now, j + outer, 0, low))
                elif high < KB:
                    finish(j + outer, partial[j] + product(now, j + outer, high, KB))
            receive(parity, REST)
            for b in range(reach - HB):
                store_vector(now, b, halo_of(halo_update, parity, 0, b))
                store_vector(now, reach + rows + HB + b, halo_of(halo_update, parity, 1, HB + b))
            if first_turn:
                at_edges(edge_last)
            for e in list(range(outer)) + list(range(outer + rows, wide)):
                finish(e, product(now, e, 0, KB))

        if not last_turn:
            send(1 - parity, REST)

    def at_edges(act):
        @pl.when(left_edge)
        def _():
            act(0)

        @pl.when(right_edge)
        def _():
            act(1)

    one_turn(0, 0, True, False)

    @pl.loop(1, rounds - 1)
    def _(turn):
        one_turn(turn, turn % 2, False, False)

    one_turn(rounds - 1, (rounds - 1) % 2, False, True)

    for b in range(rows):
        gathered[place * rows + b] = iterate[b] + update[rounds % 2, b]

    def piece(where, dest, which):
        return pltpu.make_async_remote_copy(
            src_ref=gathered.at[pl.ds(where * rows, rows)], dst_ref=gathered.at[pl.ds(where * rows, rows)],
            send_sem=c_send.at[which], recv_sem=c_recv.at[where],
            device_id={"group": group, "fold": dest}, device_id_type=MESH,
        )

    for other in (2, 1, 3):
        piece(place, (fold + 2 * other) % FOLDS, other).start()
    piece(place, partner, 0).start()
    for other in (1, 3, 2):
        where = position_of((fold + 2 * other) % FOLDS)
        piece(where, partner, 0).wait_recv()
        piece(where, partner, 3 + other).start()
    for other in range(CHIPS):
        where = position_of((partner + 2 * other) % FOLDS)
        piece(where, partner, 0).wait_recv()

    begin, live = start_of(fold), count_of(fold)
    shift = begin & (LANES - 1)
    base = begin // LANES
    back = (LANES - shift) & (LANES - 1)

    def shifted(m):
        return pltpu.roll(gathered[jnp.minimum(base + m, owned - 1)], back, 1)

    here = shifted(0)
    for m in range(slots):
        after = shifted(m + 1)
        value = jnp.where(lane < LANES - shift, here, after)
        out[:, m * LANES:(m + 1) * LANES] = jnp.where(lane + m * LANES < live, value, 0.0)
        here = after

    for which in range(7):
        piece(place, partner, which).wait_send()


def on_device(right_side, initial, counts, columns, blocks):
    folds, groups = lax.axis_size("fold"), lax.axis_size("group")
    slots = right_side.shape[1] // LANES
    owned = blocks.shape[0]
    rows = owned // folds
    depth = DEPTH
    reach, outer = HB * depth, HB * (depth - 1)
    vmem = pl.BlockSpec(memory_space=pltpu.VMEM)
    anywhere = pl.BlockSpec(memory_space=pl.ANY)
    f32, i32 = jnp.float32, jnp.int32
    dma = pltpu.SemaphoreType.DMA

    def vectors(*shape):
        return pltpu.VMEM(shape + (NV, LANES), f32)

    return pl.pallas_call(
        functools.partial(kernel, rows, groups, depth),
        out_shape=jax.ShapeDtypeStruct(right_side.shape, f32),
        in_specs=[anywhere] * 5,
        out_specs=vmem,
        scratch_shapes=[
            pltpu.SMEM(counts.shape, i32),
            pltpu.VMEM(right_side.shape, f32),
            pltpu.VMEM(right_side.shape, f32),
            vectors(2, slots + 3),
            vectors(owned),
            vectors(folds, rows),
            pltpu.VMEM((rows, KB, LANES, LANES), f32),
            pltpu.VMEM((outer - 1, KB, LANES, LANES), f32),
            pltpu.VMEM((outer - 1, KB, LANES, LANES), f32),
            pltpu.VMEM((KB, LANES, LANES), f32),
            pltpu.VMEM((KB, LANES, LANES), f32),
            pltpu.VMEM((rows + 2 * outer, KB * LANES, 2 * LANES), jnp.bfloat16),
            pltpu.SMEM((rows + 2 * outer, KB), i32),
            pltpu.SMEM((3, KB, owned), i32),
            pltpu.VMEM((2, KB, owned), i32),
            pltpu.VMEM((rows + 2 * reach, 2 * NV, LANES), jnp.bfloat16),
            pltpu.VMEM((rows + 2 * reach, 2 * NV, LANES), jnp.bfloat16),
            vectors(2, rows),
            vectors(2, rows),
            vectors(rows + 2 * outer),
            vectors(rows + 2 * outer),
            vectors(rows),
            vectors(rows),
            vectors(2, 2, reach),
            vectors(2, 2, outer),
            vectors(owned),
            dma((6,)), dma((4,)), dma((4, 2)), dma((4, 2)), dma, dma, dma((8,)), dma((8,)),
            dma((2, 2, 3)), dma((2, 2, 3)), dma((7,)), dma((8,)),
        ],
        compiler_params=pltpu.CompilerParams(collective_id=0, has_side_effects=True),
    )(counts, columns.T, right_side, initial, blocks)


def solution(mesh):
    placed = (
        P(None, ("group", "fold")),
        P(None, ("group", "fold")),
        P("group", None),
        P("group", None),
        P("group", None, None, None),
    )
    return jax.shard_map(
        on_device, mesh=mesh, in_specs=placed, out_specs=P(None, ("group", "fold")), check_vma=False
    )
```

```python
import functools

import jax
import jax.numpy as jnp
from jax import lax
from jax.experimental import pallas as pl
from jax.experimental.pallas import tpu as pltpu
from jax.sharding import PartitionSpec as P

MESH = pl.DeviceIdType.MESH
HB = 3
SWEEPS = 3
DEGREE = 4
KB = 5
NV = 16
LANES = 128
FOLDS = 8
CHIPS = 4
DEPTH = 2
EARLY = 4

upper_bound = 4.5
lower_bound = 1.35


def step_factors():
    theta = (upper_bound + lower_bound) / 2.0
    delta = (upper_bound - lower_bound) / 2.0
    keep, gain = [0.0], [1.0 / theta]
    ratio = delta / theta
    for step in range(DEGREE - 1):
        ratio_next = 1.0 / (2.0 * theta / delta - ratio)
        keep.append(ratio_next * ratio)
        gain.append(2.0 * ratio_next / delta)
        ratio = ratio_next
    return keep, gain


def split(value):
    high = value.astype(jnp.bfloat16)
    low = (value - high.astype(jnp.float32)).astype(jnp.bfloat16)
    return high, low


def position_of(fold):
    return (fold + 7) % 8


def fold_of(position):
    return (position + 1) % 8


def kernel(
    rows, groups, depth,
    counts_in, columns, right_side, initial, blocks, out,
    counts, mine, raw, aligned, sent, parts, raw_own, raw_left, raw_right, left_last, right_last, weights, order, all_columns, edge_columns,
    vector_even, vector_odd, update, resid, mid_update, mid_resid, iterate, partial, halo_update, halo_resid, gathered,
    block_sem, column_sem, edge_send, edge_recv, a_send, a_recv, b_send, b_recv, h_send, h_recv, c_send, c_recv,
):
    group, fold = lax.axis_index("group"), lax.axis_index("fold")
    chip, core = fold // 2, fold % 2
    place = position_of(fold)
    partner = chip * 2 + (1 - core)
    slots = right_side.shape[1] // LANES
    owned = rows * FOLDS
    reach = HB * depth
    outer = HB * (depth - 1)
    wide = rows + 2 * outer
    zero = jnp.zeros((NV, LANES), jnp.float32)

    rank = group * FOLDS + place
    last = groups * FOLDS - 1
    has_left, has_right = rank > 0, rank < last
    left_edge, right_edge = jnp.logical_and(place == 0, has_left), jnp.logical_and(place == FOLDS - 1, has_right)
    left = {"group": (group + groups - (7 - place) // 7) % groups, "fold": fold_of((place + 7) % 8)}
    right = {"group": (group + place // 7) % groups, "fold": fold_of((place + 1) % 8)}

    own_blocks = pltpu.make_async_copy(
        blocks.at[pl.ds(place * rows, rows)], raw_own, block_sem.at[0]
    )
    most = outer - 1
    raw_last = [left_last, right_last]

    def beside(side):
        begin = jnp.minimum(place * rows + rows, owned - outer) if side else jnp.maximum(place * rows - outer, 0)
        return [
            pltpu.make_async_copy(
                blocks.at[pl.ds(begin, most)], (raw_right if side else raw_left), block_sem.at[1 + 2 * side]
            ),
            pltpu.make_async_copy(blocks.at[begin + most], raw_last[side], block_sem.at[2 + 2 * side]),
        ]

    own_columns = pltpu.make_async_copy(columns, all_columns.at[1], column_sem.at[0])
    barrier = pltpu.get_barrier_semaphore()
    @pl.when(left_edge)
    def _():
        pl.semaphore_signal(barrier, inc=1, device_id=left, device_id_type=MESH)

    @pl.when(right_edge)
    def _():
        pl.semaphore_signal(barrier, inc=1, device_id=right, device_id_type=MESH)

    for other in (4, 3, 5, 2, 6, 1, 7):
        pl.semaphore_signal(barrier, inc=1, device_id={"group": group, "fold": (fold + other) % FOLDS}, device_id_type=MESH)

    own_counts = pltpu.make_async_copy(counts_in, counts, column_sem.at[3])
    own_counts.start()

    def own_slots_copy(source):
        return pltpu.make_async_copy(source, mine, block_sem.at[5])

    @pl.when(core == 0)
    def _():
        own_slots_copy(right_side).start()

    @pl.when(core == 1)
    def _():
        own_slots_copy(initial).start()

    own_columns.start()
    own_blocks.start()

    @pl.when(place > 0)
    def _():
        for copy in beside(0):
            copy.start()

    @pl.when(place < FOLDS - 1)
    def _():
        for copy in beside(1):
            copy.start()

    outside = (7 - place) // 7 * ((rank + last) // (last + 1)) + place // 7 * (1 - (rank + 1) // (last + 1))
    pl.semaphore_wait(barrier, FOLDS - 1 + outside)

    def swap(source):
        return pltpu.make_async_remote_copy(
            src_ref=source, dst_ref=raw, send_sem=a_send, recv_sem=a_recv,
            device_id={"group": group, "fold": partner}, device_id_type=MESH,
        )

    @pl.when(core == 0)
    def _():
        swap(initial).start()

    @pl.when(core == 1)
    def _():
        swap(right_side).start()

    def edge(side):
        begin = owned - outer if side else 0
        target = 1 - side
        refs = [
            (columns, edge_columns.at[target]),
            (blocks.at[pl.ds(begin, most)], (raw_right if target else raw_left)),
            (blocks.at[begin + most, pl.ds(0, EARLY)], raw_last[target].at[pl.ds(0, EARLY)]),
            (blocks.at[begin + most, pl.ds(EARLY, KB - EARLY)], raw_last[target].at[pl.ds(EARLY, KB - EARLY)]),
        ]
        return [
            pltpu.make_async_remote_copy(
                src_ref=source, dst_ref=dest, send_sem=edge_send.at[i, side], recv_sem=edge_recv.at[i, target],
                device_id=right if side else left, device_id_type=MESH,
            )
            for i, (source, dest) in enumerate(refs)
        ]

    def edge_start(low, high):
        @pl.when(left_edge)
        def _():
            for copy in edge(0)[low:high]:
                copy.start()

        @pl.when(right_edge)
        def _():
            for copy in edge(1)[low:high]:
                copy.start()

    edge_start(0, 3)

    lane = lax.broadcasted_iota(jnp.int32, (NV, LANES), 1)

    def start_of(which):
        total = jnp.int32(0)
        for i in range(FOLDS):
            total = total + jnp.where(i < which, counts[0, i], 0)
        return total

    def count_of(which):
        total = jnp.int32(0)
        for i in range(FOLDS):
            total = total + jnp.where(i == which, counts[0, i], 0)
        return total

    def align(source, which):
        start, count = start_of(chip * 2 + which), count_of(chip * 2 + which)
        shift = start & (LANES - 1)
        aligned[which, 0] = zero
        aligned[which, slots + 2] = zero
        before = zero
        for m in range(slots + 1):
            if m < slots:
                now = pltpu.roll(source[:, m * LANES:(m + 1) * LANES], shift, 1)
            else:
                now = zero
            slot = lane + (m * LANES - shift)
            value = jnp.where(lane < shift, before, now)
            live = jnp.logical_and(slot >= 0, slot < count)
            aligned[which, m + 1] = jnp.where(live, value, 0.0)
            before = now

    own_counts.wait()
    own_slots_copy(initial).wait()

    @pl.when(core == 0)
    def _():
        align(mine, 0)

    @pl.when(core == 1)
    def _():
        align(mine, 1)

    swap(initial).wait()

    @pl.when(core == 0)
    def _():
        align(raw, 1)

    @pl.when(core == 1)
    def _():
        align(raw, 0)

    first = [start_of(chip * 2) // LANES, start_of(chip * 2 + 1) // LANES]

    def row_block(index):
        at = [jnp.clip(index - first[i], -1, slots + 1) + 1 for i in range(2)]
        return aligned[0, at[0]] + aligned[1, at[1]]

    def message(other):
        dest = (fold + other) % FOLDS
        where = position_of(dest) * rows
        return where, pltpu.make_async_remote_copy(
            src_ref=sent.at[pl.ds(where, rows)], dst_ref=parts.at[fold],
            send_sem=b_send.at[other], recv_sem=b_recv.at[fold],
            device_id={"group": group, "fold": dest}, device_id_type=MESH,
        )

    def reachable(source, dest):
        low = jnp.logical_and(source == CHIPS - 1, dest < FOLDS // 2)
        return jnp.logical_not(jnp.logical_or(low, jnp.logical_and(source == 0, dest >= FOLDS // 2)))

    def arrival(source):
        return pltpu.make_async_remote_copy(
            src_ref=sent.at[pl.ds(0, rows)], dst_ref=parts.at[source],
            send_sem=b_send.at[0], recv_sem=b_recv.at[source],
            device_id={"group": group, "fold": fold}, device_id_type=MESH,
        )

    for other in (4, 3, 5, 2, 6, 1, 7):
        where, copy = message(other)
        for b in range(rows):
            sent[where + b] = row_block(where + b)

        @pl.when(reachable(chip, position_of((fold + other) % FOLDS)))
        def _():
            copy.start()

    for b in range(rows):
        parts[fold, b] = row_block(place * rows + b)
    for other in range(1, FOLDS):
        source = (fold + other) % FOLDS

        @pl.when(jnp.logical_not(reachable(source // 2, place)))
        def _():
            for b in range(rows):
                parts[source, b] = zero


    def prepare(source, low, high, single=False):
        @pl.loop(low, high)
        def _(e):
            at_row = place * rows + e - outer + owned
            owner, within = at_row // owned, at_row % owned
            move = (owner - 1) * owned - place * rows + outer
            column = [all_columns[owner, k, within] for k in range(KB)]
            ranks = []
            for k in range(KB):
                r = jnp.int32(0)
                for other in range(KB):
                    if other != k:
                        ahead = column[other] <= column[k] if other < k else column[other] < column[k]
                        r = r + ahead.astype(jnp.int32)
                ranks.append(r)
            for s in range(KB):
                from_slot, at = jnp.int32(0), jnp.int32(0)
                for k in range(KB):
                    from_slot = from_slot + jnp.where(ranks[k] == s, k, 0)
                    at = at + jnp.where(ranks[k] == s, column[k], 0)
                order[e, s] = jnp.clip(at + move, 0, rows + 2 * reach - 1)
                high_part, low_part = split((source[from_slot] if single else source[e - low, from_slot]).T)
                weights[e, s * LANES:(s + 1) * LANES, 0:LANES] = high_part
                weights[e, s * LANES:(s + 1) * LANES, LANES:2 * LANES] = low_part

    def absent(low):
        for e in range(low, low + outer):
            for s in range(KB):
                order[e, s] = 0
            weights[e] = jnp.zeros((KB * LANES, 2 * LANES), jnp.bfloat16)

    own_columns.wait()
    own_blocks.wait()
    prepare(raw_own, outer, outer + rows)

    def prepare_most(side):
        at = side * (outer + rows)
        prepare(raw_right if side else raw_left, at, at + most)

    def prepare_last(side):
        at = side * (outer + rows) + most
        prepare(raw_last[side], at, at + 1, single=True)

    def prepare_beside(side):
        for copy in beside(side):
            copy.wait()
        prepare_most(side)
        prepare_last(side)

    @pl.when(place > 0)
    def _():
        prepare_beside(0)

    @pl.when(place < FOLDS - 1)
    def _():
        prepare_beside(1)

    @pl.when(jnp.logical_not(has_left))
    def _():
        absent(0)

    @pl.when(jnp.logical_not(has_right))
    def _():
        absent(outer + rows)

    vectors = [vector_even, vector_odd]

    def store_vector(which, index, value):
        high, low = split(value)
        vectors[which][index, 0:NV] = high
        vectors[which][index, NV:2 * NV] = low

    for other in range(1, FOLDS):
        source = (fold + other) % FOLDS

        @pl.when(reachable(source // 2, place))
        def _():
            arrival(source).wait_recv()

    for b in range(rows):
        resid[0, b] = (parts[0, b] + parts[2, b]) + (parts[4, b] + parts[6, b])
        begun = (parts[1, b] + parts[3, b]) + (parts[5, b] + parts[7, b])
        update[0, b] = begun
        iterate[b] = zero
        store_vector(0, reach + b, begun)

    NEAR, FAR, RESID = [0], [1], [2]

    def exchange(parity, side, which):
        source, target, length, near = [
            (update, halo_update, HB, 0), (update, halo_update, reach - HB, HB), (resid, halo_resid, outer, 0),
        ][which]
        mirrored = source is update
        return pltpu.make_async_remote_copy(
            src_ref=source.at[parity, pl.ds(near + side * (rows - 2 * near - length), length)],
            dst_ref=target.at[parity, 1 - side, pl.ds(near + side * (reach - 2 * near - length if mirrored else 0), length)],
            send_sem=h_send.at[parity, side, which], recv_sem=h_recv.at[parity, 1 - side, which],
            device_id={name: left[name] + side * (right[name] - left[name]) for name in left}, device_id_type=MESH,
        )

    inside = jnp.logical_and(has_left, has_right)

    def neighbours(act):
        @pl.when(inside)
        def _():
            act(range(2))

        @pl.when(jnp.logical_not(has_left))
        def _():
            act([1])

        @pl.when(jnp.logical_not(has_right))
        def _():
            act([0])

    def send(parity, chosen):
        def act(sides):
            for which in chosen:
                for side in sides:
                    exchange(parity, side, which).start()

        neighbours(act)

    def sent_all(parity, chosen):
        def act(sides):
            for which in chosen:
                for side in sides:
                    exchange(parity, side, which).wait_send()

        neighbours(act)

    def receive(parity, chosen):
        def act(sides):
            for which in chosen:
                for side in sides:
                    exchange(parity, 1 - side, which).wait_recv()

        neighbours(act)

    def halo_of(ref, parity, side, b):
        return jnp.where(has_right if side else has_left, ref[parity, side, b], 0.0)

    send(0, NEAR + FAR + RESID)
    edge_start(3, 4)

    for other in range(1, FOLDS):
        @pl.when(reachable(chip, position_of((fold + other) % FOLDS)))
        def _():
            message(other)[1].wait_send()


    def edge_most(side):
        arrived = edge(1 - side)
        arrived[0].wait_recv()
        into = pltpu.make_async_copy(edge_columns.at[side], all_columns.at[2 * side], column_sem.at[1 + side])
        into.start()
        into.wait()
        arrived[1].wait_recv()
        prepare_most(side)

    def edge_last(side):
        for copy in edge(1 - side)[2:]:
            copy.wait_recv()
        prepare_last(side)
        for copy in edge(side):
            copy.wait_send()

    def product(which, e, low, high):
        lhs = jnp.concatenate([vectors[which][order[e, s]] for s in range(low, high)], axis=1)
        full = jnp.dot(lhs, weights[e, low * LANES:high * LANES, :], preferred_element_type=jnp.float32)
        return (full[:NV, :LANES] + full[:NV, LANES:]) + (full[NV:, :LANES] + full[NV:, LANES:])

    def own_slots(j):
        return max(0, HB - j), KB - max(0, HB - (rows - 1 - j))

    keeps, gains = step_factors()
    rounds = SWEEPS * DEGREE // depth

    def one_turn(turn, first_turn=False, last_turn=False):
        parity, phase = turn % 2, turn % (DEGREE // depth)
        given = RESID if first_turn else []
        for level in range(depth):
            now, later = level % 2, (level + 1) % 2
            keep, gain = keeps[phase * depth + level], gains[phase * depth + level]

            def finish(e, applied):
                own = e - outer
                inside = 0 <= own < rows
                if level > 0:
                    old, left_over = mid_update[e], mid_resid[e]
                elif inside:
                    old, left_over = update[parity, own], resid[parity, own]
                else:
                    side, at = (0, e + HB) if own < 0 else (1, own - rows)
                    old = halo_of(halo_update, parity, side, at)
                    if first_turn:
                        left_over = halo_of(halo_resid, parity, side, at - (1 - side) * HB)
                    else:
                        before = (phase * depth + DEGREE - 1) % DEGREE
                        left_over = (old - keeps[before] * mid_update[e]) * (1.0 / gains[before])
                left_over = left_over - applied
                fresh = keep * old + gain * left_over
                if inside:
                    iterate[own] = iterate[own] + old
                if level == depth - 1:
                    update[1 - parity, own] = fresh
                    resid[1 - parity, own] = left_over
                else:
                    mid_update[e] = fresh
                    mid_resid[e] = left_over
                store_vector(later, e + HB, fresh)

            margin = HB * (depth - 1 - level)
            if level > 0:
                ends = list(range(HB)) + list(range(rows - HB, rows))
                for j in ends:
                    finish(j + outer, product(now, j + outer, 0, KB))

                if not last_turn:
                    send(1 - parity, NEAR)
                for j in range(HB, rows - HB):
                    finish(j + outer, product(now, j + outer, 0, KB))
                continue

            for j in range(rows):
                low, high = own_slots(j)
                applied = product(now, j + outer, low, high)
                if high - low == KB:
                    finish(j + outer, applied)
                else:
                    partial[j] = applied

            if first_turn:
                at_edges(edge_most)
            sent_all(parity, NEAR + FAR + given)
            receive(parity, NEAR)
            for b in range(HB):
                store_vector(now, reach - HB + b, halo_of(halo_update, parity, 0, reach - HB + b))
                store_vector(now, reach + rows + b, halo_of(halo_update, parity, 1, b))
            for j in range(rows):
                low, high = own_slots(j)
                if low > 0:
                    finish(j + outer, partial[j] + product(now, j + outer, 0, low))
                elif high < KB:
                    finish(j + outer, partial[j] + product(now, j + outer, high, KB))
            receive(parity, FAR + given)
            for b in range(reach - HB):
                store_vector(now, b, halo_of(halo_update, parity, 0, b))
                store_vector(now, reach + rows + HB + b, halo_of(halo_update, parity, 1, HB + b))
            if first_turn:
                at_edges(edge_last)
            for e in list(range(outer)) + list(range(outer + rows, wide)):
                finish(e, product(now, e, 0, KB))

        if not last_turn:
            send(1 - parity, FAR)

    def at_edges(act):
        @pl.when(left_edge)
        def _():
            act(0)

        @pl.when(right_edge)
        def _():
            act(1)

    one_turn(0, first_turn=True)

    @pl.loop(0, (rounds - 2) // 2)
    def _(_):
        one_turn(1)
        one_turn(2)

    one_turn(rounds - 1, last_turn=True)

    for b in range(rows):
        gathered[place * rows + b] = iterate[b] + update[rounds % 2, b]

    def piece(where, dest, which):
        return pltpu.make_async_remote_copy(
            src_ref=gathered.at[pl.ds(where * rows, rows)], dst_ref=gathered.at[pl.ds(where * rows, rows)],
            send_sem=c_send.at[which], recv_sem=c_recv.at[where],
            device_id={"group": group, "fold": dest}, device_id_type=MESH,
        )

    def wanted(where, dest, act):
        @pl.when(reachable(dest // 2, where))
        def _():
            act()

    def forward(where, which):
        piece(where, partner, 0).wait_recv()
        piece(where, partner, which).start()

    for other in (2, 1, 3):
        dest = (fold + 2 * other) % FOLDS
        wanted(place, dest, piece(place, dest, other).start)
    wanted(place, partner, piece(place, partner, 0).start)
    for other in (1, 3, 2):
        where = position_of((fold + 2 * other) % FOLDS)
        wanted(where, partner, functools.partial(forward, where, 3 + other))
    for other in range(CHIPS):
        where = position_of((partner + 2 * other) % FOLDS)
        wanted(where, fold, piece(where, partner, 0).wait_recv)

    begin, live = start_of(fold), count_of(fold)
    shift = begin & (LANES - 1)
    base = begin // LANES
    back = (LANES - shift) & (LANES - 1)

    def shifted(m):
        return pltpu.roll(gathered[jnp.minimum(base + m, owned - 1)], back, 1)

    here = shifted(0)
    for m in range(slots):
        after = shifted(m + 1)
        value = jnp.where(lane < LANES - shift, here, after)
        out[:, m * LANES:(m + 1) * LANES] = jnp.where(lane + m * LANES < live, value, 0.0)
        here = after

    for other in range(CHIPS):
        wanted(place, (fold + 2 * other) % FOLDS if other else partner, piece(place, partner, other).wait_send)
        if other:
            wanted(position_of((fold + 2 * other) % FOLDS), partner, piece(place, partner, 3 + other).wait_send)


def on_device(right_side, initial, counts, columns, blocks):
    folds, groups = lax.axis_size("fold"), lax.axis_size("group")
    slots = right_side.shape[1] // LANES
    owned = blocks.shape[0]
    rows = owned // folds
    depth = DEPTH
    reach, outer = HB * depth, HB * (depth - 1)
    vmem = pl.BlockSpec(memory_space=pltpu.VMEM)
    anywhere = pl.BlockSpec(memory_space=pl.ANY)
    f32, i32 = jnp.float32, jnp.int32
    dma = pltpu.SemaphoreType.DMA

    def vectors(*shape):
        return pltpu.VMEM(shape + (NV, LANES), f32)

    return pl.pallas_call(
        functools.partial(kernel, rows, groups, depth),
        out_shape=jax.ShapeDtypeStruct(right_side.shape, f32),
        in_specs=[anywhere] * 5,
        out_specs=vmem,
        scratch_shapes=[
            pltpu.SMEM(counts.shape, i32),
            pltpu.VMEM(right_side.shape, f32),
            pltpu.VMEM(right_side.shape, f32),
            vectors(2, slots + 3),
            vectors(owned),
            vectors(folds, rows),
            pltpu.VMEM((rows, KB, LANES, LANES), f32),
            pltpu.VMEM((outer - 1, KB, LANES, LANES), f32),
            pltpu.VMEM((outer - 1, KB, LANES, LANES), f32),
            pltpu.VMEM((KB, LANES, LANES), f32),
            pltpu.VMEM((KB, LANES, LANES), f32),
            pltpu.VMEM((rows + 2 * outer, KB * LANES, 2 * LANES), jnp.bfloat16),
            pltpu.SMEM((rows + 2 * outer, KB), i32),
            pltpu.SMEM((3, KB, owned), i32),
            pltpu.VMEM((2, KB, owned), i32),
            pltpu.VMEM((rows + 2 * reach, 2 * NV, LANES), jnp.bfloat16),
            pltpu.VMEM((rows + 2 * reach, 2 * NV, LANES), jnp.bfloat16),
            vectors(2, rows),
            vectors(2, rows),
            vectors(rows + 2 * outer),
            vectors(rows + 2 * outer),
            vectors(rows),
            vectors(rows),
            vectors(2, 2, reach),
            vectors(2, 2, outer),
            vectors(owned),
            dma((6,)), dma((4,)), dma((4, 2)), dma((4, 2)), dma, dma, dma((8,)), dma((8,)),
            dma((2, 2, 3)), dma((2, 2, 3)), dma((7,)), dma((8,)),
        ],
        compiler_params=pltpu.CompilerParams(collective_id=0, has_side_effects=True),
    )(counts, columns.T, right_side, initial, blocks)


def solution(mesh):
    placed = (
        P(None, ("group", "fold")),
        P(None, ("group", "fold")),
        P("group", None),
        P("group", None),
        P("group", None, None, None),
    )
    return jax.shard_map(
        on_device, mesh=mesh, in_specs=placed, out_specs=P(None, ("group", "fold")), check_vma=False
    )
```

```python
import functools

import jax
import jax.numpy as jnp
from jax import lax
from jax.experimental import pallas as pl
from jax.experimental.pallas import tpu as pltpu
from jax.sharding import PartitionSpec as P

MESH = pl.DeviceIdType.MESH
HB = 3
SWEEPS = 3
DEGREE = 4
KB = 5
NV = 16
LANES = 128
FOLDS = 8
CHIPS = 4
DEPTH = 2
RELAYS = (2, 6)

upper_bound = 4.5
lower_bound = 1.35


def step_factors():
    theta = (upper_bound + lower_bound) / 2.0
    delta = (upper_bound - lower_bound) / 2.0
    keep, gain = [0.0], [1.0 / theta]
    ratio = delta / theta
    for step in range(DEGREE - 1):
        ratio_next = 1.0 / (2.0 * theta / delta - ratio)
        keep.append(ratio_next * ratio)
        gain.append(2.0 * ratio_next / delta)
        ratio = ratio_next
    return keep, gain


def split(value):
    high = value.astype(jnp.bfloat16)
    low = (value - high.astype(jnp.float32)).astype(jnp.bfloat16)
    return high, low


def position_of(fold):
    return (fold + 7) % 8


def fold_of(position):
    return (position + 1) % 8


def kernel(
    rows, groups, depth,
    counts_in, columns, right_side, initial, blocks, out,
    counts, mine, raw, aligned, sent, parts, raw_own, raw_left, raw_right, left_last, right_last, handed, weights, order, all_columns, edge_columns,
    vector_even, vector_odd, update, resid, mid_update, mid_resid, iterate, partial, halo_update, halo_resid, gathered,
    block_sem, column_sem, edge_send, edge_recv, relay_sems, last_sem, a_send, a_recv, b_send, b_recv, h_send, h_recv, c_send, c_recv,
):
    group, fold = lax.axis_index("group"), lax.axis_index("fold")
    chip, core = fold // 2, fold % 2
    place = position_of(fold)
    partner = chip * 2 + (1 - core)
    slots = right_side.shape[1] // LANES
    owned = rows * FOLDS
    reach = HB * depth
    outer = HB * (depth - 1)
    wide = rows + 2 * outer
    zero = jnp.zeros((NV, LANES), jnp.float32)

    rank = group * FOLDS + place
    last = groups * FOLDS - 1
    has_left, has_right = rank > 0, rank < last
    relay_left, relay_right = fold == RELAYS[0], fold == RELAYS[1]
    relay = jnp.logical_or(relay_left, relay_right)
    below, above = {"group": (group + groups - 1) % groups, "fold": fold}, {"group": (group + 1) % groups, "fold": fold}
    left_edge, right_edge = jnp.logical_and(place == 0, has_left), jnp.logical_and(place == FOLDS - 1, has_right)
    left = {"group": (group + groups - (7 - place) // 7) % groups, "fold": fold_of((place + 7) % 8)}
    right = {"group": (group + place // 7) % groups, "fold": fold_of((place + 1) % 8)}

    own_blocks = pltpu.make_async_copy(
        blocks.at[pl.ds(place * rows, rows)], raw_own, block_sem.at[0]
    )
    most = outer - 1
    raw_last = [left_last, right_last]

    def beside(side):
        begin = jnp.minimum(place * rows + rows, owned - outer) if side else jnp.maximum(place * rows - outer, 0)
        return [
            pltpu.make_async_copy(
                blocks.at[pl.ds(begin, most)], (raw_right if side else raw_left), block_sem.at[1 + 2 * side]
            ),
            pltpu.make_async_copy(blocks.at[begin + most], raw_last[side], block_sem.at[2 + 2 * side]),
        ]

    own_columns = pltpu.make_async_copy(columns, all_columns.at[1], column_sem.at[0])
    barrier = pltpu.get_barrier_semaphore()
    @pl.when(left_edge)
    def _():
        pl.semaphore_signal(barrier, inc=1, device_id=left, device_id_type=MESH)

    @pl.when(right_edge)
    def _():
        pl.semaphore_signal(barrier, inc=1, device_id=right, device_id_type=MESH)

    @pl.when(jnp.logical_and(relay, group > 0))
    def _():
        pl.semaphore_signal(barrier, inc=1, device_id=below, device_id_type=MESH)

    @pl.when(jnp.logical_and(relay, group < groups - 1))
    def _():
        pl.semaphore_signal(barrier, inc=1, device_id=above, device_id_type=MESH)

    for other in (4, 3, 5, 2, 6, 1, 7):
        pl.semaphore_signal(barrier, inc=1, device_id={"group": group, "fold": (fold + other) % FOLDS}, device_id_type=MESH)

    own_counts = pltpu.make_async_copy(counts_in, counts, column_sem.at[3])
    own_counts.start()

    def own_slots_copy(source):
        return pltpu.make_async_copy(source, mine, block_sem.at[5])

    @pl.when(core == 0)
    def _():
        own_slots_copy(right_side).start()

    @pl.when(core == 1)
    def _():
        own_slots_copy(initial).start()

    own_columns.start()
    own_blocks.start()

    @pl.when(place > 0)
    def _():
        for copy in beside(0):
            copy.start()

    @pl.when(place < FOLDS - 1)
    def _():
        for copy in beside(1):
            copy.start()

    outside = (7 - place) // 7 * ((rank + last) // (last + 1)) + place // 7 * (1 - (rank + 1) // (last + 1))
    is_relay = jnp.where(relay, 1, 0)
    beyond = is_relay * ((group + groups - 1) // groups + 1 - (group + 1) // groups)
    pl.semaphore_wait(barrier, FOLDS - 1 + outside + beyond)

    def swap(source):
        return pltpu.make_async_remote_copy(
            src_ref=source, dst_ref=raw, send_sem=a_send, recv_sem=a_recv,
            device_id={"group": group, "fold": partner}, device_id_type=MESH,
        )

    @pl.when(core == 0)
    def _():
        swap(initial).start()

    @pl.when(core == 1)
    def _():
        swap(right_side).start()

    def edge(side):
        begin = owned - outer if side else 0
        target = 1 - side
        refs = [
            (columns, edge_columns.at[target]),
            (blocks.at[pl.ds(begin, most)], (raw_right if target else raw_left)),
        ]
        return [
            pltpu.make_async_remote_copy(
                src_ref=source, dst_ref=dest, send_sem=edge_send.at[i, side], recv_sem=edge_recv.at[i, target],
                device_id=right if side else left, device_id_type=MESH,
            )
            for i, (source, dest) in enumerate(refs)
        ]

    def relay_in(side):
        return pltpu.make_async_remote_copy(
            src_ref=blocks.at[(owned - outer if side else 0) + most], dst_ref=handed, send_sem=relay_sems.at[0],
            recv_sem=relay_sems.at[1], device_id=above if side else below, device_id_type=MESH,
        )

    def relay_out(side):
        return pltpu.make_async_remote_copy(
            src_ref=handed, dst_ref=raw_last[side], send_sem=relay_sems.at[2], recv_sem=last_sem.at[side],
            device_id={"group": group, "fold": fold_of(side * (FOLDS - 1))}, device_id_type=MESH,
        )

    @pl.when(left_edge)
    def _():
        for copy in edge(0):
            copy.start()

    @pl.when(right_edge)
    def _():
        for copy in edge(1):
            copy.start()

    @pl.when(jnp.logical_and(relay_left, group < groups - 1))
    def _():
        relay_in(1).start()

    @pl.when(jnp.logical_and(relay_right, group > 0))
    def _():
        relay_in(0).start()

    lane = lax.broadcasted_iota(jnp.int32, (NV, LANES), 1)

    def start_of(which):
        total = jnp.int32(0)
        for i in range(FOLDS):
            total = total + jnp.where(i < which, counts[0, i], 0)
        return total

    def count_of(which):
        total = jnp.int32(0)
        for i in range(FOLDS):
            total = total + jnp.where(i == which, counts[0, i], 0)
        return total

    def align(source, which):
        start, count = start_of(chip * 2 + which), count_of(chip * 2 + which)
        shift = start & (LANES - 1)
        aligned[which, 0] = zero
        aligned[which, slots + 2] = zero
        before = zero
        for m in range(slots + 1):
            if m < slots:
                now = pltpu.roll(source[:, m * LANES:(m + 1) * LANES], shift, 1)
            else:
                now = zero
            slot = lane + (m * LANES - shift)
            value = jnp.where(lane < shift, before, now)
            live = jnp.logical_and(slot >= 0, slot < count)
            aligned[which, m + 1] = jnp.where(live, value, 0.0)
            before = now

    own_counts.wait()
    own_slots_copy(initial).wait()

    @pl.when(core == 0)
    def _():
        align(mine, 0)

    @pl.when(core == 1)
    def _():
        align(mine, 1)

    swap(initial).wait()

    @pl.when(core == 0)
    def _():
        align(raw, 1)

    @pl.when(core == 1)
    def _():
        align(raw, 0)

    first = [start_of(chip * 2) // LANES, start_of(chip * 2 + 1) // LANES]

    def row_block(index):
        at = [jnp.clip(index - first[i], -1, slots + 1) + 1 for i in range(2)]
        return aligned[0, at[0]] + aligned[1, at[1]]

    def message(other):
        dest = (fold + other) % FOLDS
        where = position_of(dest) * rows
        return where, pltpu.make_async_remote_copy(
            src_ref=sent.at[pl.ds(where, rows)], dst_ref=parts.at[fold],
            send_sem=b_send.at[other], recv_sem=b_recv.at[fold],
            device_id={"group": group, "fold": dest}, device_id_type=MESH,
        )

    def reachable(source, dest):
        low = jnp.logical_and(source == CHIPS - 1, dest < FOLDS // 2)
        return jnp.logical_not(jnp.logical_or(low, jnp.logical_and(source == 0, dest >= FOLDS // 2)))

    def arrival(source):
        return pltpu.make_async_remote_copy(
            src_ref=sent.at[pl.ds(0, rows)], dst_ref=parts.at[source],
            send_sem=b_send.at[0], recv_sem=b_recv.at[source],
            device_id={"group": group, "fold": fold}, device_id_type=MESH,
        )

    for other in (4, 3, 5, 2, 6, 1, 7):
        where, copy = message(other)
        for b in range(rows):
            sent[where + b] = row_block(where + b)

        @pl.when(reachable(chip, position_of((fold + other) % FOLDS)))
        def _():
            copy.start()

    for b in range(rows):
        parts[fold, b] = row_block(place * rows + b)
    for other in range(1, FOLDS):
        source = (fold + other) % FOLDS

        @pl.when(jnp.logical_not(reachable(source // 2, place)))
        def _():
            for b in range(rows):
                parts[source, b] = zero


    def prepare(source, low, high, single=False):
        @pl.loop(low, high)
        def _(e):
            at_row = place * rows + e - outer + owned
            owner, within = at_row // owned, at_row % owned
            move = (owner - 1) * owned - place * rows + outer
            column = [all_columns[owner, k, within] for k in range(KB)]
            ranks = []
            for k in range(KB):
                r = jnp.int32(0)
                for other in range(KB):
                    if other != k:
                        ahead = column[other] <= column[k] if other < k else column[other] < column[k]
                        r = r + ahead.astype(jnp.int32)
                ranks.append(r)
            for s in range(KB):
                from_slot, at = jnp.int32(0), jnp.int32(0)
                for k in range(KB):
                    from_slot = from_slot + jnp.where(ranks[k] == s, k, 0)
                    at = at + jnp.where(ranks[k] == s, column[k], 0)
                order[e, s] = jnp.clip(at + move, 0, rows + 2 * reach - 1)
                high_part, low_part = split((source[from_slot] if single else source[e - low, from_slot]).T)
                weights[e, s * LANES:(s + 1) * LANES, 0:LANES] = high_part
                weights[e, s * LANES:(s + 1) * LANES, LANES:2 * LANES] = low_part

    def absent(low):
        for e in range(low, low + outer):
            for s in range(KB):
                order[e, s] = 0
            weights[e] = jnp.zeros((KB * LANES, 2 * LANES), jnp.bfloat16)

    own_columns.wait()
    own_blocks.wait()
    prepare(raw_own, outer, outer + rows)

    def prepare_most(side):
        at = side * (outer + rows)
        prepare(raw_right if side else raw_left, at, at + most)

    def prepare_last(side):
        at = side * (outer + rows) + most
        prepare(raw_last[side], at, at + 1, single=True)

    def prepare_beside(side):
        for copy in beside(side):
            copy.wait()
        prepare_most(side)
        prepare_last(side)

    @pl.when(place > 0)
    def _():
        prepare_beside(0)

    @pl.when(place < FOLDS - 1)
    def _():
        prepare_beside(1)

    @pl.when(jnp.logical_not(has_left))
    def _():
        absent(0)

    @pl.when(jnp.logical_not(has_right))
    def _():
        absent(outer + rows)

    vectors = [vector_even, vector_odd]

    def store_vector(which, index, value):
        high, low = split(value)
        vectors[which][index, 0:NV] = high
        vectors[which][index, NV:2 * NV] = low

    @pl.when(jnp.logical_and(relay_left, group > 0))
    def _():
        relay_in(1).wait_recv()
        relay_out(0).start()

    @pl.when(jnp.logical_and(relay_right, group < groups - 1))
    def _():
        relay_in(0).wait_recv()
        relay_out(1).start()

    for other in range(1, FOLDS):
        source = (fold + other) % FOLDS

        @pl.when(reachable(source // 2, place))
        def _():
            arrival(source).wait_recv()

    for b in range(rows):
        resid[0, b] = (parts[0, b] + parts[2, b]) + (parts[4, b] + parts[6, b])
        begun = (parts[1, b] + parts[3, b]) + (parts[5, b] + parts[7, b])
        update[0, b] = begun
        iterate[b] = zero
        store_vector(0, reach + b, begun)

    NEAR, FAR, RESID = [0], [1], [2]

    def exchange(parity, side, which):
        source, target, length, near = [
            (update, halo_update, HB, 0), (update, halo_update, reach - HB, HB), (resid, halo_resid, outer, 0),
        ][which]
        mirrored = source is update
        return pltpu.make_async_remote_copy(
            src_ref=source.at[parity, pl.ds(near + side * (rows - 2 * near - length), length)],
            dst_ref=target.at[parity, 1 - side, pl.ds(near + side * (reach - 2 * near - length if mirrored else 0), length)],
            send_sem=h_send.at[parity, side, which], recv_sem=h_recv.at[parity, 1 - side, which],
            device_id={name: left[name] + side * (right[name] - left[name]) for name in left}, device_id_type=MESH,
        )

    inside = jnp.logical_and(has_left, has_right)

    def neighbours(act):
        @pl.when(inside)
        def _():
            act(range(2))

        @pl.when(jnp.logical_not(has_left))
        def _():
            act([1])

        @pl.when(jnp.logical_not(has_right))
        def _():
            act([0])

    def send(parity, chosen):
        def act(sides):
            for which in chosen:
                for side in sides:
                    exchange(parity, side, which).start()

        neighbours(act)

    def sent_all(parity, chosen):
        def act(sides):
            for which in chosen:
                for side in sides:
                    exchange(parity, side, which).wait_send()

        neighbours(act)

    def receive(parity, chosen):
        def act(sides):
            for which in chosen:
                for side in sides:
                    exchange(parity, 1 - side, which).wait_recv()

        neighbours(act)

    def halo_of(ref, parity, side, b):
        return jnp.where(has_right if side else has_left, ref[parity, side, b], 0.0)

    send(0, NEAR + FAR + RESID)

    for other in range(1, FOLDS):
        @pl.when(reachable(chip, position_of((fold + other) % FOLDS)))
        def _():
            message(other)[1].wait_send()


    def edge_most(side):
        arrived = edge(1 - side)
        arrived[0].wait_recv()
        into = pltpu.make_async_copy(edge_columns.at[side], all_columns.at[2 * side], column_sem.at[1 + side])
        into.start()
        into.wait()
        arrived[1].wait_recv()
        prepare_most(side)

    def edge_last(side):
        relay_out(side).wait_recv()
        prepare_last(side)
        for copy in edge(side):
            copy.wait_send()

    def product(which, e, low, high):
        lhs = jnp.concatenate([vectors[which][order[e, s]] for s in range(low, high)], axis=1)
        full = jnp.dot(lhs, weights[e, low * LANES:high * LANES, :], preferred_element_type=jnp.float32)
        return (full[:NV, :LANES] + full[:NV, LANES:]) + (full[NV:, :LANES] + full[NV:, LANES:])

    def own_slots(j):
        return max(0, HB - j), KB - max(0, HB - (rows - 1 - j))

    keeps, gains = step_factors()
    rounds = SWEEPS * DEGREE // depth

    def one_turn(turn, first_turn=False, last_turn=False):
        parity, phase = turn % 2, turn % (DEGREE // depth)
        given = RESID if first_turn else []
        for level in range(depth):
            now, later = level % 2, (level + 1) % 2
            keep, gain = keeps[phase * depth + level], gains[phase * depth + level]

            def finish(e, applied):
                own = e - outer
                inside = 0 <= own < rows
                if level > 0:
                    old, left_over = mid_update[e], mid_resid[e]
                elif inside:
                    old, left_over = update[parity, own], resid[parity, own]
                else:
                    side, at = (0, e + HB) if own < 0 else (1, own - rows)
                    old = halo_of(halo_update, parity, side, at)
                    if first_turn:
                        left_over = halo_of(halo_resid, parity, side, at - (1 - side) * HB)
                    else:
                        before = (phase * depth + DEGREE - 1) % DEGREE
                        left_over = (old - keeps[before] * mid_update[e]) * (1.0 / gains[before])
                left_over = left_over - applied
                fresh = keep * old + gain * left_over
                if inside:
                    iterate[own] = iterate[own] + old
                if level == depth - 1:
                    update[1 - parity, own] = fresh
                    resid[1 - parity, own] = left_over
                else:
                    mid_update[e] = fresh
                    mid_resid[e] = left_over
                store_vector(later, e + HB, fresh)

            margin = HB * (depth - 1 - level)
            if level > 0:
                ends = list(range(HB)) + list(range(rows - HB, rows))
                for j in ends:
                    finish(j + outer, product(now, j + outer, 0, KB))

                if not last_turn:
                    send(1 - parity, NEAR)
                for j in range(HB, rows - HB):
                    finish(j + outer, product(now, j + outer, 0, KB))
                continue

            for j in range(rows):
                low, high = own_slots(j)
                applied = product(now, j + outer, low, high)
                if high - low == KB:
                    finish(j + outer, applied)
                else:
                    partial[j] = applied

            if first_turn:
                at_edges(edge_most)
            sent_all(parity, NEAR + FAR + given)
            receive(parity, NEAR)
            for b in range(HB):
                store_vector(now, reach - HB + b, halo_of(halo_update, parity, 0, reach - HB + b))
                store_vector(now, reach + rows + b, halo_of(halo_update, parity, 1, b))
            for j in range(rows):
                low, high = own_slots(j)
                if low > 0:
                    finish(j + outer, partial[j] + product(now, j + outer, 0, low))
                elif high < KB:
                    finish(j + outer, partial[j] + product(now, j + outer, high, KB))
            receive(parity, FAR + given)
            for b in range(reach - HB):
                store_vector(now, b, halo_of(halo_update, parity, 0, b))
                store_vector(now, reach + rows + HB + b, halo_of(halo_update, parity, 1, HB + b))
            if first_turn:
                at_edges(edge_last)
            for e in list(range(outer)) + list(range(outer + rows, wide)):
                finish(e, product(now, e, 0, KB))

        if not last_turn:
            send(1 - parity, FAR)

    def at_edges(act):
        @pl.when(left_edge)
        def _():
            act(0)

        @pl.when(right_edge)
        def _():
            act(1)

    one_turn(0, first_turn=True)

    @pl.loop(0, (rounds - 2) // 2)
    def _(_):
        one_turn(1)
        one_turn(2)

    one_turn(rounds - 1, last_turn=True)

    @pl.when(jnp.logical_and(relay_left, group < groups - 1))
    def _():
        relay_in(1).wait_send()

    @pl.when(jnp.logical_and(relay_right, group > 0))
    def _():
        relay_in(0).wait_send()

    @pl.when(jnp.logical_or(jnp.logical_and(relay_left, group > 0), jnp.logical_and(relay_right, group < groups - 1)))
    def _():
        relay_out(0).wait_send()

    for b in range(rows):
        gathered[place * rows + b] = iterate[b] + update[rounds % 2, b]

    def piece(where, dest, which):
        return pltpu.make_async_remote_copy(
            src_ref=gathered.at[pl.ds(where * rows, rows)], dst_ref=gathered.at[pl.ds(where * rows, rows)],
            send_sem=c_send.at[which], recv_sem=c_recv.at[where],
            device_id={"group": group, "fold": dest}, device_id_type=MESH,
        )

    def wanted(where, dest, act):
        @pl.when(reachable(dest // 2, where))
        def _():
            act()

    def forward(where, which):
        piece(where, partner, 0).wait_recv()
        piece(where, partner, which).start()

    for other in (2, 1, 3):
        dest = (fold + 2 * other) % FOLDS
        wanted(place, dest, piece(place, dest, other).start)
    wanted(place, partner, piece(place, partner, 0).start)
    for other in (1, 3, 2):
        where = position_of((fold + 2 * other) % FOLDS)
        wanted(where, partner, functools.partial(forward, where, 3 + other))
    for other in range(CHIPS):
        where = position_of((partner + 2 * other) % FOLDS)
        wanted(where, fold, piece(where, partner, 0).wait_recv)

    begin, live = start_of(fold), count_of(fold)
    shift = begin & (LANES - 1)
    base = begin // LANES
    back = (LANES - shift) & (LANES - 1)

    def shifted(m):
        return pltpu.roll(gathered[jnp.minimum(base + m, owned - 1)], back, 1)

    here = shifted(0)
    for m in range(slots):
        after = shifted(m + 1)
        value = jnp.where(lane < LANES - shift, here, after)
        out[:, m * LANES:(m + 1) * LANES] = jnp.where(lane + m * LANES < live, value, 0.0)
        here = after

    for other in range(CHIPS):
        wanted(place, (fold + 2 * other) % FOLDS if other else partner, piece(place, partner, other).wait_send)
        if other:
            wanted(position_of((fold + 2 * other) % FOLDS), partner, piece(place, partner, 3 + other).wait_send)


def on_device(right_side, initial, counts, columns, blocks):
    folds, groups = lax.axis_size("fold"), lax.axis_size("group")
    slots = right_side.shape[1] // LANES
    owned = blocks.shape[0]
    rows = owned // folds
    depth = DEPTH
    reach, outer = HB * depth, HB * (depth - 1)
    vmem = pl.BlockSpec(memory_space=pltpu.VMEM)
    anywhere = pl.BlockSpec(memory_space=pl.ANY)
    f32, i32 = jnp.float32, jnp.int32
    dma = pltpu.SemaphoreType.DMA

    def vectors(*shape):
        return pltpu.VMEM(shape + (NV, LANES), f32)

    return pl.pallas_call(
        functools.partial(kernel, rows, groups, depth),
        out_shape=pltpu.VMEM(right_side.shape, f32),
        in_specs=[anywhere] * 5,
        out_specs=vmem,
        scratch_shapes=[
            pltpu.SMEM(counts.shape, i32),
            pltpu.VMEM(right_side.shape, f32),
            pltpu.VMEM(right_side.shape, f32),
            vectors(2, slots + 3),
            vectors(owned),
            vectors(folds, rows),
            pltpu.VMEM((rows, KB, LANES, LANES), f32),
            pltpu.VMEM((outer - 1, KB, LANES, LANES), f32),
            pltpu.VMEM((outer - 1, KB, LANES, LANES), f32),
            pltpu.VMEM((KB, LANES, LANES), f32),
            pltpu.VMEM((KB, LANES, LANES), f32),
            pltpu.VMEM((KB, LANES, LANES), f32),
            pltpu.VMEM((rows + 2 * outer, KB * LANES, 2 * LANES), jnp.bfloat16),
            pltpu.SMEM((rows + 2 * outer, KB), i32),
            pltpu.SMEM((3, KB, owned), i32),
            pltpu.VMEM((2, KB, owned), i32),
            pltpu.VMEM((rows + 2 * reach, 2 * NV, LANES), jnp.bfloat16),
            pltpu.VMEM((rows + 2 * reach, 2 * NV, LANES), jnp.bfloat16),
            vectors(2, rows),
            vectors(2, rows),
            vectors(rows + 2 * outer),
            vectors(rows + 2 * outer),
            vectors(rows),
            vectors(rows),
            vectors(2, 2, reach),
            vectors(2, 2, outer),
            vectors(owned),
            dma((6,)), dma((4,)), dma((2, 2)), dma((2, 2)), dma((3,)), dma((2,)), dma, dma, dma((8,)), dma((8,)),
            dma((2, 2, 3)), dma((2, 2, 3)), dma((7,)), dma((8,)),
        ],
        compiler_params=pltpu.CompilerParams(collective_id=0, has_side_effects=True),
    )(counts, columns.T, right_side, initial, blocks)


def solution(mesh):
    placed = (
        P(None, ("group", "fold")),
        P(None, ("group", "fold")),
        P("group", None),
        P("group", None),
        P("group", None, None, None),
    )
    return jax.shard_map(
        on_device, mesh=mesh, in_specs=placed, out_specs=P(None, ("group", "fold")), check_vma=False
    )
```

```python
import functools

import jax
import jax.numpy as jnp
from jax import lax
from jax.experimental import pallas as pl
from jax.experimental.pallas import tpu as pltpu
from jax.sharding import PartitionSpec as P

MESH = pl.DeviceIdType.MESH
HB = 3
SWEEPS = 3
DEGREE = 4
KB = 5
NV = 16
LANES = 128
FOLDS = 8
CHIPS = 4
DEPTH = 2
RELAYS = (2, 6)
EARLY = 2

upper_bound = 4.5
lower_bound = 1.35


def step_factors():
    theta = (upper_bound + lower_bound) / 2.0
    delta = (upper_bound - lower_bound) / 2.0
    keep, gain = [0.0], [1.0 / theta]
    ratio = delta / theta
    for step in range(DEGREE - 1):
        ratio_next = 1.0 / (2.0 * theta / delta - ratio)
        keep.append(ratio_next * ratio)
        gain.append(2.0 * ratio_next / delta)
        ratio = ratio_next
    return keep, gain


def split(value):
    high = value.astype(jnp.bfloat16)
    low = (value - high.astype(jnp.float32)).astype(jnp.bfloat16)
    return high, low


def position_of(fold):
    return (fold + 7) % 8


def fold_of(position):
    return (position + 1) % 8


def kernel(
    rows, groups, depth,
    counts_in, columns, right_side, initial, blocks, out,
    counts, mine, raw, aligned, sent, parts, raw_own, raw_left, raw_right, left_last, right_last, handed, weights, order, all_columns, edge_columns,
    vector_even, vector_odd, update, resid, mid_update, mid_resid, iterate, partial, halo_update, halo_resid, gathered,
    block_sem, column_sem, edge_send, edge_recv, relay_sems, last_sem, a_send, a_recv, b_send, b_recv, h_send, h_recv, c_send, c_recv,
):
    group, fold = lax.axis_index("group"), lax.axis_index("fold")
    chip, core = fold // 2, fold % 2
    place = position_of(fold)
    partner = chip * 2 + (1 - core)
    slots = right_side.shape[1] // LANES
    owned = rows * FOLDS
    reach = HB * depth
    outer = HB * (depth - 1)
    wide = rows + 2 * outer
    zero = jnp.zeros((NV, LANES), jnp.float32)

    rank = group * FOLDS + place
    last = groups * FOLDS - 1
    has_left, has_right = rank > 0, rank < last
    relay_left, relay_right = fold == RELAYS[0], fold == RELAYS[1]
    relay = jnp.logical_or(relay_left, relay_right)
    below, above = {"group": (group + groups - 1) % groups, "fold": fold}, {"group": (group + 1) % groups, "fold": fold}
    left_edge, right_edge = jnp.logical_and(place == 0, has_left), jnp.logical_and(place == FOLDS - 1, has_right)
    left = {"group": (group + groups - (7 - place) // 7) % groups, "fold": fold_of((place + 7) % 8)}
    right = {"group": (group + place // 7) % groups, "fold": fold_of((place + 1) % 8)}

    own_blocks = pltpu.make_async_copy(
        blocks.at[pl.ds(place * rows, rows)], raw_own, block_sem.at[0]
    )
    most = outer - 1
    raw_last = [left_last, right_last]

    def beside(side):
        begin = jnp.minimum(place * rows + rows, owned - outer) if side else jnp.maximum(place * rows - outer, 0)
        return [
            pltpu.make_async_copy(
                blocks.at[pl.ds(begin, most)], (raw_right if side else raw_left), block_sem.at[1 + 2 * side]
            ),
            pltpu.make_async_copy(blocks.at[begin + most], raw_last[side], block_sem.at[2 + 2 * side]),
        ]

    own_columns = pltpu.make_async_copy(columns, all_columns.at[1], column_sem.at[0])
    barrier = pltpu.get_barrier_semaphore()
    @pl.when(left_edge)
    def _():
        pl.semaphore_signal(barrier, inc=1, device_id=left, device_id_type=MESH)

    @pl.when(right_edge)
    def _():
        pl.semaphore_signal(barrier, inc=1, device_id=right, device_id_type=MESH)

    @pl.when(jnp.logical_and(relay, group > 0))
    def _():
        pl.semaphore_signal(barrier, inc=1, device_id=below, device_id_type=MESH)

    @pl.when(jnp.logical_and(relay, group < groups - 1))
    def _():
        pl.semaphore_signal(barrier, inc=1, device_id=above, device_id_type=MESH)

    for other in (4, 3, 5, 2, 6, 1, 7):
        pl.semaphore_signal(barrier, inc=1, device_id={"group": group, "fold": (fold + other) % FOLDS}, device_id_type=MESH)

    own_counts = pltpu.make_async_copy(counts_in, counts, column_sem.at[3])
    own_counts.start()

    def own_slots_copy(source):
        return pltpu.make_async_copy(source, mine, block_sem.at[5])

    @pl.when(core == 0)
    def _():
        own_slots_copy(right_side).start()

    @pl.when(core == 1)
    def _():
        own_slots_copy(initial).start()

    own_columns.start()
    own_blocks.start()

    @pl.when(place > 0)
    def _():
        for copy in beside(0):
            copy.start()

    @pl.when(place < FOLDS - 1)
    def _():
        for copy in beside(1):
            copy.start()

    outside = (7 - place) // 7 * ((rank + last) // (last + 1)) + place // 7 * (1 - (rank + 1) // (last + 1))
    is_relay = jnp.where(relay, 1, 0)
    beyond = is_relay * ((group + groups - 1) // groups + 1 - (group + 1) // groups)
    pl.semaphore_wait(barrier, FOLDS - 1 + outside + beyond)

    def swap(source):
        return pltpu.make_async_remote_copy(
            src_ref=source, dst_ref=raw, send_sem=a_send, recv_sem=a_recv,
            device_id={"group": group, "fold": partner}, device_id_type=MESH,
        )

    @pl.when(core == 0)
    def _():
        swap(initial).start()

    @pl.when(core == 1)
    def _():
        swap(right_side).start()

    def edge(side):
        begin = owned - outer if side else 0
        target = 1 - side
        refs = [
            (columns, edge_columns.at[target]),
            (blocks.at[pl.ds(begin, most)], (raw_right if target else raw_left)),
            (blocks.at[begin + most, pl.ds(0, EARLY)], raw_last[target].at[pl.ds(0, EARLY)]),
        ]
        return [
            pltpu.make_async_remote_copy(
                src_ref=source, dst_ref=dest, send_sem=edge_send.at[i, side], recv_sem=edge_recv.at[i, target],
                device_id=right if side else left, device_id_type=MESH,
            )
            for i, (source, dest) in enumerate(refs)
        ]

    def relay_in(side):
        return pltpu.make_async_remote_copy(
            src_ref=blocks.at[(owned - outer if side else 0) + most, pl.ds(EARLY, KB - EARLY)], dst_ref=handed, send_sem=relay_sems.at[0],
            recv_sem=relay_sems.at[1], device_id=above if side else below, device_id_type=MESH,
        )

    def relay_out(side):
        return pltpu.make_async_remote_copy(
            src_ref=handed, dst_ref=raw_last[side].at[pl.ds(EARLY, KB - EARLY)], send_sem=relay_sems.at[2], recv_sem=last_sem.at[side],
            device_id={"group": group, "fold": fold_of(side * (FOLDS - 1))}, device_id_type=MESH,
        )

    @pl.when(left_edge)
    def _():
        for copy in edge(0):
            copy.start()

    @pl.when(right_edge)
    def _():
        for copy in edge(1):
            copy.start()

    @pl.when(jnp.logical_and(relay_left, group < groups - 1))
    def _():
        relay_in(1).start()

    @pl.when(jnp.logical_and(relay_right, group > 0))
    def _():
        relay_in(0).start()

    lane = lax.broadcasted_iota(jnp.int32, (NV, LANES), 1)

    def start_of(which):
        total = jnp.int32(0)
        for i in range(FOLDS):
            total = total + jnp.where(i < which, counts[0, i], 0)
        return total

    def count_of(which):
        total = jnp.int32(0)
        for i in range(FOLDS):
            total = total + jnp.where(i == which, counts[0, i], 0)
        return total

    def align(source, which):
        start, count = start_of(chip * 2 + which), count_of(chip * 2 + which)
        shift = start & (LANES - 1)
        aligned[which, 0] = zero
        aligned[which, slots + 2] = zero
        before = zero
        for m in range(slots + 1):
            if m < slots:
                now = pltpu.roll(source[:, m * LANES:(m + 1) * LANES], shift, 1)
            else:
                now = zero
            slot = lane + (m * LANES - shift)
            value = jnp.where(lane < shift, before, now)
            live = jnp.logical_and(slot >= 0, slot < count)
            aligned[which, m + 1] = jnp.where(live, value, 0.0)
            before = now

    own_counts.wait()
    own_slots_copy(initial).wait()

    @pl.when(core == 0)
    def _():
        align(mine, 0)

    @pl.when(core == 1)
    def _():
        align(mine, 1)

    swap(initial).wait()

    @pl.when(core == 0)
    def _():
        align(raw, 1)

    @pl.when(core == 1)
    def _():
        align(raw, 0)

    first = [start_of(chip * 2) // LANES, start_of(chip * 2 + 1) // LANES]

    def row_block(index):
        at = [jnp.clip(index - first[i], -1, slots + 1) + 1 for i in range(2)]
        return aligned[0, at[0]] + aligned[1, at[1]]

    def message(other):
        dest = (fold + other) % FOLDS
        where = position_of(dest) * rows
        return where, pltpu.make_async_remote_copy(
            src_ref=sent.at[pl.ds(where, rows)], dst_ref=parts.at[fold],
            send_sem=b_send.at[other], recv_sem=b_recv.at[fold],
            device_id={"group": group, "fold": dest}, device_id_type=MESH,
        )

    def reachable(source, dest):
        low = jnp.logical_and(source == CHIPS - 1, dest < FOLDS // 2)
        return jnp.logical_not(jnp.logical_or(low, jnp.logical_and(source == 0, dest >= FOLDS // 2)))

    def arrival(source):
        return pltpu.make_async_remote_copy(
            src_ref=sent.at[pl.ds(0, rows)], dst_ref=parts.at[source],
            send_sem=b_send.at[0], recv_sem=b_recv.at[source],
            device_id={"group": group, "fold": fold}, device_id_type=MESH,
        )

    for other in (4, 3, 5, 2, 6, 1, 7):
        where, copy = message(other)
        for b in range(rows):
            sent[where + b] = row_block(where + b)

        @pl.when(reachable(chip, position_of((fold + other) % FOLDS)))
        def _():
            copy.start()

    for b in range(rows):
        parts[fold, b] = row_block(place * rows + b)
    for other in range(1, FOLDS):
        source = (fold + other) % FOLDS

        @pl.when(jnp.logical_not(reachable(source // 2, place)))
        def _():
            for b in range(rows):
                parts[source, b] = zero


    def prepare(source, low, high, single=False):
        @pl.loop(low, high)
        def _(e):
            at_row = place * rows + e - outer + owned
            owner, within = at_row // owned, at_row % owned
            move = (owner - 1) * owned - place * rows + outer
            column = [all_columns[owner, k, within] for k in range(KB)]
            ranks = []
            for k in range(KB):
                r = jnp.int32(0)
                for other in range(KB):
                    if other != k:
                        ahead = column[other] <= column[k] if other < k else column[other] < column[k]
                        r = r + ahead.astype(jnp.int32)
                ranks.append(r)
            for s in range(KB):
                from_slot, at = jnp.int32(0), jnp.int32(0)
                for k in range(KB):
                    from_slot = from_slot + jnp.where(ranks[k] == s, k, 0)
                    at = at + jnp.where(ranks[k] == s, column[k], 0)
                order[e, s] = jnp.clip(at + move, 0, rows + 2 * reach - 1)
                high_part, low_part = split((source[from_slot] if single else source[e - low, from_slot]).T)
                weights[e, s * LANES:(s + 1) * LANES, 0:LANES] = high_part
                weights[e, s * LANES:(s + 1) * LANES, LANES:2 * LANES] = low_part

    def absent(low):
        for e in range(low, low + outer):
            for s in range(KB):
                order[e, s] = 0
            weights[e] = jnp.zeros((KB * LANES, 2 * LANES), jnp.bfloat16)

    own_columns.wait()
    own_blocks.wait()
    prepare(raw_own, outer, outer + rows)

    def prepare_most(side):
        at = side * (outer + rows)
        prepare(raw_right if side else raw_left, at, at + most)

    def prepare_last(side):
        at = side * (outer + rows) + most
        prepare(raw_last[side], at, at + 1, single=True)

    def prepare_beside(side):
        for copy in beside(side):
            copy.wait()
        prepare_most(side)
        prepare_last(side)

    @pl.when(place > 0)
    def _():
        prepare_beside(0)

    @pl.when(place < FOLDS - 1)
    def _():
        prepare_beside(1)

    @pl.when(jnp.logical_not(has_left))
    def _():
        absent(0)

    @pl.when(jnp.logical_not(has_right))
    def _():
        absent(outer + rows)

    vectors = [vector_even, vector_odd]

    def store_vector(which, index, value):
        high, low = split(value)
        vectors[which][index, 0:NV] = high
        vectors[which][index, NV:2 * NV] = low

    @pl.when(jnp.logical_and(relay_left, group > 0))
    def _():
        relay_in(1).wait_recv()
        relay_out(0).start()

    @pl.when(jnp.logical_and(relay_right, group < groups - 1))
    def _():
        relay_in(0).wait_recv()
        relay_out(1).start()

    for other in range(1, FOLDS):
        source = (fold + other) % FOLDS

        @pl.when(reachable(source // 2, place))
        def _():
            arrival(source).wait_recv()

    for b in range(rows):
        resid[0, b] = (parts[0, b] + parts[2, b]) + (parts[4, b] + parts[6, b])
        begun = (parts[1, b] + parts[3, b]) + (parts[5, b] + parts[7, b])
        update[0, b] = begun
        iterate[b] = zero
        store_vector(0, reach + b, begun)

    NEAR, FAR, RESID = [0], [1], [2]

    def exchange(parity, side, which):
        source, target, length, near = [
            (update, halo_update, HB, 0), (update, halo_update, reach - HB, HB), (resid, halo_resid, outer, 0),
        ][which]
        mirrored = source is update
        return pltpu.make_async_remote_copy(
            src_ref=source.at[parity, pl.ds(near + side * (rows - 2 * near - length), length)],
            dst_ref=target.at[parity, 1 - side, pl.ds(near + side * (reach - 2 * near - length if mirrored else 0), length)],
            send_sem=h_send.at[parity, side, which], recv_sem=h_recv.at[parity, 1 - side, which],
            device_id={name: left[name] + side * (right[name] - left[name]) for name in left}, device_id_type=MESH,
        )

    inside = jnp.logical_and(has_left, has_right)

    def neighbours(act):
        @pl.when(inside)
        def _():
            act(range(2))

        @pl.when(jnp.logical_not(has_left))
        def _():
            act([1])

        @pl.when(jnp.logical_not(has_right))
        def _():
            act([0])

    def send(parity, chosen):
        def act(sides):
            for which in chosen:
                for side in sides:
                    exchange(parity, side, which).start()

        neighbours(act)

    def sent_all(parity, chosen):
        def act(sides):
            for which in chosen:
                for side in sides:
                    exchange(parity, side, which).wait_send()

        neighbours(act)

    def receive(parity, chosen):
        def act(sides):
            for which in chosen:
                for side in sides:
                    exchange(parity, 1 - side, which).wait_recv()

        neighbours(act)

    def halo_of(ref, parity, side, b):
        return jnp.where(has_right if side else has_left, ref[parity, side, b], 0.0)

    send(0, NEAR + FAR + RESID)

    for other in range(1, FOLDS):
        @pl.when(reachable(chip, position_of((fold + other) % FOLDS)))
        def _():
            message(other)[1].wait_send()


    def edge_most(side):
        arrived = edge(1 - side)
        arrived[0].wait_recv()
        into = pltpu.make_async_copy(edge_columns.at[side], all_columns.at[2 * side], column_sem.at[1 + side])
        into.start()
        into.wait()
        arrived[1].wait_recv()
        prepare_most(side)

    def edge_last(side):
        edge(1 - side)[2].wait_recv()
        relay_out(side).wait_recv()
        prepare_last(side)
        for copy in edge(side):
            copy.wait_send()

    def product(which, e, low, high):
        lhs = jnp.concatenate([vectors[which][order[e, s]] for s in range(low, high)], axis=1)
        full = jnp.dot(lhs, weights[e, low * LANES:high * LANES, :], preferred_element_type=jnp.float32)
        return (full[:NV, :LANES] + full[:NV, LANES:]) + (full[NV:, :LANES] + full[NV:, LANES:])

    def own_slots(j):
        return max(0, HB - j), KB - max(0, HB - (rows - 1 - j))

    keeps, gains = step_factors()
    rounds = SWEEPS * DEGREE // depth

    def one_turn(turn, first_turn=False, last_turn=False):
        parity, phase = turn % 2, turn % (DEGREE // depth)
        given = RESID if first_turn else []
        for level in range(depth):
            now, later = level % 2, (level + 1) % 2
            keep, gain = keeps[phase * depth + level], gains[phase * depth + level]

            def finish(e, applied):
                own = e - outer
                inside = 0 <= own < rows
                if level > 0:
                    old, left_over = mid_update[e], mid_resid[e]
                elif inside:
                    old, left_over = update[parity, own], resid[parity, own]
                else:
                    side, at = (0, e + HB) if own < 0 else (1, own - rows)
                    old = halo_of(halo_update, parity, side, at)
                    if first_turn:
                        left_over = halo_of(halo_resid, parity, side, at - (1 - side) * HB)
                    else:
                        before = (phase * depth + DEGREE - 1) % DEGREE
                        left_over = (old - keeps[before] * mid_update[e]) * (1.0 / gains[before])
                left_over = left_over - applied
                fresh = keep * old + gain * left_over
                if inside:
                    iterate[own] = iterate[own] + old
                if level == depth - 1:
                    update[1 - parity, own] = fresh
                    resid[1 - parity, own] = left_over
                else:
                    mid_update[e] = fresh
                    mid_resid[e] = left_over
                store_vector(later, e + HB, fresh)

            margin = HB * (depth - 1 - level)
            if level > 0:
                ends = list(range(HB)) + list(range(rows - HB, rows))
                for j in ends:
                    finish(j + outer, product(now, j + outer, 0, KB))

                if not last_turn:
                    send(1 - parity, NEAR)
                for j in range(HB, rows - HB):
                    finish(j + outer, product(now, j + outer, 0, KB))
                continue

            for j in range(rows):
                low, high = own_slots(j)
                applied = product(now, j + outer, low, high)
                if high - low == KB:
                    finish(j + outer, applied)
                else:
                    partial[j] = applied

            if first_turn:
                at_edges(edge_most)
            sent_all(parity, NEAR + FAR + given)
            receive(parity, NEAR)
            for b in range(HB):
                store_vector(now, reach - HB + b, halo_of(halo_update, parity, 0, reach - HB + b))
                store_vector(now, reach + rows + b, halo_of(halo_update, parity, 1, b))
            for j in range(rows):
                low, high = own_slots(j)
                if low > 0:
                    finish(j + outer, partial[j] + product(now, j + outer, 0, low))
                elif high < KB:
                    finish(j + outer, partial[j] + product(now, j + outer, high, KB))
            def settled(e):
                return (HB - e, KB) if e < outer else (0, KB - 1 - (e - outer - rows))

            beyond_rows = list(range(outer)) + list(range(outer + rows, wide))
            if first_turn:
                at_edges(edge_last)
            for i, e in enumerate(beyond_rows):
                partial[i] = product(now, e, *settled(e))
            receive(parity, FAR + given)
            for b in range(reach - HB):
                store_vector(now, b, halo_of(halo_update, parity, 0, b))
                store_vector(now, reach + rows + HB + b, halo_of(halo_update, parity, 1, HB + b))
            for i, e in enumerate(beyond_rows):
                low, high = settled(e)
                finish(e, partial[i] + (product(now, e, 0, low) if low else product(now, e, high, KB)))

        if not last_turn:
            send(1 - parity, FAR)

    def at_edges(act):
        @pl.when(left_edge)
        def _():
            act(0)

        @pl.when(right_edge)
        def _():
            act(1)

    one_turn(0, first_turn=True)

    @pl.loop(0, (rounds - 2) // 2)
    def _(_):
        one_turn(1)
        one_turn(2)

    one_turn(rounds - 1, last_turn=True)

    @pl.when(jnp.logical_and(relay_left, group < groups - 1))
    def _():
        relay_in(1).wait_send()

    @pl.when(jnp.logical_and(relay_right, group > 0))
    def _():
        relay_in(0).wait_send()

    @pl.when(jnp.logical_or(jnp.logical_and(relay_left, group > 0), jnp.logical_and(relay_right, group < groups - 1)))
    def _():
        relay_out(0).wait_send()

    for b in range(rows):
        gathered[place * rows + b] = iterate[b] + update[rounds % 2, b]

    def piece(where, dest, which):
        return pltpu.make_async_remote_copy(
            src_ref=gathered.at[pl.ds(where * rows, rows)], dst_ref=gathered.at[pl.ds(where * rows, rows)],
            send_sem=c_send.at[which], recv_sem=c_recv.at[where],
            device_id={"group": group, "fold": dest}, device_id_type=MESH,
        )

    def needs(dest, where):
        return jnp.logical_and(where >= 2 * dest - FOLDS, where <= 2 * dest + 1)

    def either(chip_of, where):
        return jnp.logical_or(needs(chip_of // 2 * 2, where), needs(chip_of // 2 * 2 + 1, where))

    across = (fold + FOLDS // 2) % FOLDS
    across_partner = (partner + FOLDS // 2) % FOLDS
    beside_me = {other: (fold + 2 * other) % FOLDS for other in (1, 3)}
    outgoing = [(2, place, across, needs(across, place)), (5, place, across_partner, needs(across_partner, place))]
    outgoing += [(other, place, dest, either(dest, place)) for other, dest in beside_me.items()]
    outgoing += [(0, place, partner, needs(partner, place))]
    passed_on = [
        (3 + other, position_of(source), partner, needs(partner, position_of(source))) for other, source in beside_me.items()
    ]

    for which, where, dest, wish in outgoing:
        pl.when(wish)(piece(where, dest, which).start)
    for which, where, dest, wish in passed_on:
        pl.when(either(fold, where))(piece(where, dest, which).wait_recv)
        pl.when(wish)(piece(where, dest, which).start)
    for source in [partner, across, across_partner] + [(partner + 2 * other) % FOLDS for other in (1, 3)]:
        where = position_of(source)
        pl.when(needs(fold, where))(piece(where, partner, 0).wait_recv)

    begin, live = start_of(fold), count_of(fold)
    shift = begin & (LANES - 1)
    base = begin // LANES
    back = (LANES - shift) & (LANES - 1)

    def shifted(m):
        return pltpu.roll(gathered[jnp.minimum(base + m, owned - 1)], back, 1)

    here = shifted(0)
    for m in range(slots):
        after = shifted(m + 1)
        value = jnp.where(lane < LANES - shift, here, after)
        out[:, m * LANES:(m + 1) * LANES] = jnp.where(lane + m * LANES < live, value, 0.0)
        here = after

    for which, where, dest, wish in outgoing + passed_on:
        pl.when(wish)(piece(where, dest, which).wait_send)


def on_device(right_side, initial, counts, columns, blocks):
    folds, groups = lax.axis_size("fold"), lax.axis_size("group")
    slots = right_side.shape[1] // LANES
    owned = blocks.shape[0]
    rows = owned // folds
    depth = DEPTH
    reach, outer = HB * depth, HB * (depth - 1)
    vmem = pl.BlockSpec(memory_space=pltpu.VMEM)
    anywhere = pl.BlockSpec(memory_space=pl.ANY)
    f32, i32 = jnp.float32, jnp.int32
    dma = pltpu.SemaphoreType.DMA

    def vectors(*shape):
        return pltpu.VMEM(shape + (NV, LANES), f32)

    return pl.pallas_call(
        functools.partial(kernel, rows, groups, depth),
        out_shape=pltpu.VMEM(right_side.shape, f32),
        in_specs=[anywhere] * 5,
        out_specs=vmem,
        scratch_shapes=[
            pltpu.SMEM(counts.shape, i32),
            pltpu.VMEM(right_side.shape, f32),
            pltpu.VMEM(right_side.shape, f32),
            vectors(2, slots + 3),
            vectors(owned),
            vectors(folds, rows),
            pltpu.VMEM((rows, KB, LANES, LANES), f32),
            pltpu.VMEM((outer - 1, KB, LANES, LANES), f32),
            pltpu.VMEM((outer - 1, KB, LANES, LANES), f32),
            pltpu.VMEM((KB, LANES, LANES), f32),
            pltpu.VMEM((KB, LANES, LANES), f32),
            pltpu.VMEM((KB - EARLY, LANES, LANES), f32),
            pltpu.VMEM((rows + 2 * outer, KB * LANES, 2 * LANES), jnp.bfloat16),
            pltpu.SMEM((rows + 2 * outer, KB), i32),
            pltpu.SMEM((3, KB, owned), i32),
            pltpu.VMEM((2, KB, owned), i32),
            pltpu.VMEM((rows + 2 * reach, 2 * NV, LANES), jnp.bfloat16),
            pltpu.VMEM((rows + 2 * reach, 2 * NV, LANES), jnp.bfloat16),
            vectors(2, rows),
            vectors(2, rows),
            vectors(rows + 2 * outer),
            vectors(rows + 2 * outer),
            vectors(rows),
            vectors(rows),
            vectors(2, 2, reach),
            vectors(2, 2, outer),
            vectors(owned),
            dma((6,)), dma((4,)), dma((3, 2)), dma((3, 2)), dma((3,)), dma((2,)), dma, dma, dma((8,)), dma((8,)),
            dma((2, 2, 3)), dma((2, 2, 3)), dma((7,)), dma((8,)),
        ],
        compiler_params=pltpu.CompilerParams(collective_id=0, has_side_effects=True),
    )(counts, columns.T, right_side, initial, blocks)


def solution(mesh):
    placed = (
        P(None, ("group", "fold")),
        P(None, ("group", "fold")),
        P("group", None),
        P("group", None),
        P("group", None, None, None),
    )
    return jax.shard_map(
        on_device, mesh=mesh, in_specs=placed, out_specs=P(None, ("group", "fold")), check_vma=False
    )
```

```python
import functools

import jax
import jax.numpy as jnp
from jax import lax
from jax.experimental import pallas as pl
from jax.experimental.pallas import tpu as pltpu
from jax.sharding import PartitionSpec as P

MESH = pl.DeviceIdType.MESH
HB = 3
SWEEPS = 3
DEGREE = 4
KB = 5
NV = 16
LANES = 128
FOLDS = 8
CHIPS = 4
DEPTH = 2
RELAYS = (2, 6)
EARLY = 2

upper_bound = 4.5
lower_bound = 1.35


def step_factors():
    theta = (upper_bound + lower_bound) / 2.0
    delta = (upper_bound - lower_bound) / 2.0
    keep, gain = [0.0], [1.0 / theta]
    ratio = delta / theta
    for step in range(DEGREE - 1):
        ratio_next = 1.0 / (2.0 * theta / delta - ratio)
        keep.append(ratio_next * ratio)
        gain.append(2.0 * ratio_next / delta)
        ratio = ratio_next
    return keep, gain


def split(value):
    high = value.astype(jnp.bfloat16)
    low = (value - high.astype(jnp.float32)).astype(jnp.bfloat16)
    return high, low


def position_of(fold):
    return (fold + 7) % 8


def fold_of(position):
    return (position + 1) % 8


def kernel(
    rows, groups, depth,
    counts_in, columns, right_side, initial, blocks, out,
    counts, mine, raw, aligned, sent, parts, raw_own, raw_left, raw_right, left_last, right_last, handed, weights, order, all_columns, edge_columns,
    vector_even, vector_odd, update, resid, mid_update, mid_resid, iterate, partial, halo_update, halo_resid, gathered,
    block_sem, column_sem, edge_send, edge_recv, relay_sems, last_sem, a_send, a_recv, b_send, b_recv, h_send, h_recv, c_send, c_recv,
):
    group, fold = lax.axis_index("group"), lax.axis_index("fold")
    chip, core = fold // 2, fold % 2
    place = position_of(fold)
    partner = chip * 2 + (1 - core)
    slots = right_side.shape[1] // LANES
    owned = rows * FOLDS
    reach = HB * depth
    outer = HB * (depth - 1)
    wide = rows + 2 * outer
    zero = jnp.zeros((NV, LANES), jnp.float32)

    rank = group * FOLDS + place
    last = groups * FOLDS - 1
    has_left, has_right = rank > 0, rank < last
    relay_left, relay_right = fold == RELAYS[0], fold == RELAYS[1]
    relay = jnp.logical_or(relay_left, relay_right)
    below, above = {"group": (group + groups - 1) % groups, "fold": fold}, {"group": (group + 1) % groups, "fold": fold}
    left_edge, right_edge = jnp.logical_and(place == 0, has_left), jnp.logical_and(place == FOLDS - 1, has_right)
    left = {"group": (group + groups - (7 - place) // 7) % groups, "fold": fold_of((place + 7) % 8)}
    right = {"group": (group + place // 7) % groups, "fold": fold_of((place + 1) % 8)}

    own_blocks = pltpu.make_async_copy(
        blocks.at[pl.ds(place * rows, rows)], raw_own, block_sem.at[0]
    )
    most = outer - 1
    raw_last = [left_last, right_last]

    def beside(side):
        begin = jnp.minimum(place * rows + rows, owned - outer) if side else jnp.maximum(place * rows - outer, 0)
        return [
            pltpu.make_async_copy(
                blocks.at[pl.ds(begin, most)], (raw_right if side else raw_left), block_sem.at[1 + 2 * side]
            ),
            pltpu.make_async_copy(blocks.at[begin + most], raw_last[side], block_sem.at[2 + 2 * side]),
        ]

    own_columns = pltpu.make_async_copy(columns, all_columns.at[1], column_sem.at[0])
    barrier = pltpu.get_barrier_semaphore()
    @pl.when(left_edge)
    def _():
        pl.semaphore_signal(barrier, inc=1, device_id=left, device_id_type=MESH)

    @pl.when(right_edge)
    def _():
        pl.semaphore_signal(barrier, inc=1, device_id=right, device_id_type=MESH)

    @pl.when(jnp.logical_and(relay, group > 0))
    def _():
        pl.semaphore_signal(barrier, inc=1, device_id=below, device_id_type=MESH)

    @pl.when(jnp.logical_and(relay, group < groups - 1))
    def _():
        pl.semaphore_signal(barrier, inc=1, device_id=above, device_id_type=MESH)

    for other in (4, 3, 5, 2, 6, 1, 7):
        pl.semaphore_signal(barrier, inc=1, device_id={"group": group, "fold": (fold + other) % FOLDS}, device_id_type=MESH)

    own_counts = pltpu.make_async_copy(counts_in, counts, column_sem.at[3])
    own_counts.start()

    def own_slots_copy(source):
        return pltpu.make_async_copy(source, mine, block_sem.at[5])

    @pl.when(core == 0)
    def _():
        own_slots_copy(right_side).start()

    @pl.when(core == 1)
    def _():
        own_slots_copy(initial).start()

    own_columns.start()
    own_blocks.start()

    @pl.when(place > 0)
    def _():
        for copy in beside(0):
            copy.start()

    @pl.when(place < FOLDS - 1)
    def _():
        for copy in beside(1):
            copy.start()

    outside = (7 - place) // 7 * ((rank + last) // (last + 1)) + place // 7 * (1 - (rank + 1) // (last + 1))
    is_relay = jnp.where(relay, 1, 0)
    beyond = is_relay * ((group + groups - 1) // groups + 1 - (group + 1) // groups)
    pl.semaphore_wait(barrier, FOLDS - 1 + outside + beyond)

    def swap(source):
        return pltpu.make_async_remote_copy(
            src_ref=source, dst_ref=raw, send_sem=a_send, recv_sem=a_recv,
            device_id={"group": group, "fold": partner}, device_id_type=MESH,
        )

    @pl.when(core == 0)
    def _():
        swap(initial).start()

    @pl.when(core == 1)
    def _():
        swap(right_side).start()

    def edge(side):
        begin = owned - outer if side else 0
        target = 1 - side
        refs = [
            (columns, edge_columns.at[target]),
            (blocks.at[pl.ds(begin, most)], (raw_right if target else raw_left)),
            (blocks.at[begin + most, pl.ds(0, EARLY)], raw_last[target].at[pl.ds(0, EARLY)]),
        ]
        return [
            pltpu.make_async_remote_copy(
                src_ref=source, dst_ref=dest, send_sem=edge_send.at[i, side], recv_sem=edge_recv.at[i, target],
                device_id=right if side else left, device_id_type=MESH,
            )
            for i, (source, dest) in enumerate(refs)
        ]

    def relay_in(side):
        return pltpu.make_async_remote_copy(
            src_ref=blocks.at[(owned - outer if side else 0) + most, pl.ds(EARLY, KB - EARLY)], dst_ref=handed, send_sem=relay_sems.at[0],
            recv_sem=relay_sems.at[1], device_id=above if side else below, device_id_type=MESH,
        )

    def relay_out(side):
        return pltpu.make_async_remote_copy(
            src_ref=handed, dst_ref=raw_last[side].at[pl.ds(EARLY, KB - EARLY)], send_sem=relay_sems.at[2], recv_sem=last_sem.at[side],
            device_id={"group": group, "fold": fold_of(side * (FOLDS - 1))}, device_id_type=MESH,
        )

    @pl.when(left_edge)
    def _():
        for copy in edge(0):
            copy.start()

    @pl.when(right_edge)
    def _():
        for copy in edge(1):
            copy.start()

    @pl.when(jnp.logical_and(relay_left, group < groups - 1))
    def _():
        relay_in(1).start()

    @pl.when(jnp.logical_and(relay_right, group > 0))
    def _():
        relay_in(0).start()

    lane = lax.broadcasted_iota(jnp.int32, (NV, LANES), 1)

    def start_of(which):
        total = jnp.int32(0)
        for i in range(FOLDS):
            total = total + jnp.where(i < which, counts[0, i], 0)
        return total

    def count_of(which):
        total = jnp.int32(0)
        for i in range(FOLDS):
            total = total + jnp.where(i == which, counts[0, i], 0)
        return total

    def align(source, which):
        start, count = start_of(chip * 2 + which), count_of(chip * 2 + which)
        shift = start & (LANES - 1)
        aligned[which, 0] = zero
        aligned[which, slots + 2] = zero
        before = zero
        for m in range(slots + 1):
            if m < slots:
                now = pltpu.roll(source[:, m * LANES:(m + 1) * LANES], shift, 1)
            else:
                now = zero
            slot = lane + (m * LANES - shift)
            value = jnp.where(lane < shift, before, now)
            live = jnp.logical_and(slot >= 0, slot < count)
            aligned[which, m + 1] = jnp.where(live, value, 0.0)
            before = now

    own_counts.wait()
    own_slots_copy(initial).wait()

    @pl.when(core == 0)
    def _():
        align(mine, 0)

    @pl.when(core == 1)
    def _():
        align(mine, 1)

    swap(initial).wait()

    @pl.when(core == 0)
    def _():
        align(raw, 1)

    @pl.when(core == 1)
    def _():
        align(raw, 0)

    first = [start_of(chip * 2) // LANES, start_of(chip * 2 + 1) // LANES]

    def row_block(index):
        at = [jnp.clip(index - first[i], -1, slots + 1) + 1 for i in range(2)]
        return aligned[0, at[0]] + aligned[1, at[1]]

    def message(other):
        dest = (fold + other) % FOLDS
        where = position_of(dest) * rows
        return where, pltpu.make_async_remote_copy(
            src_ref=sent.at[pl.ds(where, rows)], dst_ref=parts.at[fold],
            send_sem=b_send.at[other], recv_sem=b_recv.at[fold],
            device_id={"group": group, "fold": dest}, device_id_type=MESH,
        )

    def reachable(source, dest):
        low = jnp.logical_and(source == CHIPS - 1, dest < FOLDS // 2)
        return jnp.logical_not(jnp.logical_or(low, jnp.logical_and(source == 0, dest >= FOLDS // 2)))

    def arrival(source):
        return pltpu.make_async_remote_copy(
            src_ref=sent.at[pl.ds(0, rows)], dst_ref=parts.at[source],
            send_sem=b_send.at[0], recv_sem=b_recv.at[source],
            device_id={"group": group, "fold": fold}, device_id_type=MESH,
        )

    for other in (4, 3, 5, 2, 6, 1, 7):
        where, copy = message(other)
        for b in range(rows):
            sent[where + b] = row_block(where + b)

        @pl.when(reachable(chip, position_of((fold + other) % FOLDS)))
        def _():
            copy.start()

    for b in range(rows):
        parts[fold, b] = row_block(place * rows + b)
    for other in range(1, FOLDS):
        source = (fold + other) % FOLDS

        @pl.when(jnp.logical_not(reachable(source // 2, place)))
        def _():
            for b in range(rows):
                parts[source, b] = zero


    def prepare(source, low, high, single=False):
        @pl.loop(low, high)
        def _(e):
            at_row = place * rows + e - outer + owned
            owner, within = at_row // owned, at_row % owned
            move = (owner - 1) * owned - place * rows + outer
            column = [all_columns[owner, k, within] for k in range(KB)]
            ranks = []
            for k in range(KB):
                r = jnp.int32(0)
                for other in range(KB):
                    if other != k:
                        ahead = column[other] <= column[k] if other < k else column[other] < column[k]
                        r = r + ahead.astype(jnp.int32)
                ranks.append(r)
            for s in range(KB):
                from_slot, at = jnp.int32(0), jnp.int32(0)
                for k in range(KB):
                    from_slot = from_slot + jnp.where(ranks[k] == s, k, 0)
                    at = at + jnp.where(ranks[k] == s, column[k], 0)
                order[e, s] = jnp.clip(at + move, 0, rows + 2 * reach - 1)
                high_part, low_part = split((source[from_slot] if single else source[e - low, from_slot]).T)
                weights[e, s * LANES:(s + 1) * LANES, 0:LANES] = high_part
                weights[e, s * LANES:(s + 1) * LANES, LANES:2 * LANES] = low_part

    def absent(low):
        for e in range(low, low + outer):
            for s in range(KB):
                order[e, s] = 0
            weights[e] = jnp.zeros((KB * LANES, 2 * LANES), jnp.bfloat16)

    own_columns.wait()
    own_blocks.wait()
    prepare(raw_own, outer, outer + rows)

    def prepare_most(side):
        at = side * (outer + rows)
        prepare(raw_right if side else raw_left, at, at + most)

    def prepare_last(side):
        at = side * (outer + rows) + most
        prepare(raw_last[side], at, at + 1, single=True)

    def prepare_beside(side):
        for copy in beside(side):
            copy.wait()
        prepare_most(side)
        prepare_last(side)

    @pl.when(place > 0)
    def _():
        prepare_beside(0)

    @pl.when(place < FOLDS - 1)
    def _():
        prepare_beside(1)

    @pl.when(jnp.logical_not(has_left))
    def _():
        absent(0)

    @pl.when(jnp.logical_not(has_right))
    def _():
        absent(outer + rows)

    vectors = [vector_even, vector_odd]

    def store_vector(which, index, value):
        high, low = split(value)
        vectors[which][index, 0:NV] = high
        vectors[which][index, NV:2 * NV] = low

    @pl.when(jnp.logical_and(relay_left, group > 0))
    def _():
        relay_in(1).wait_recv()
        relay_out(0).start()

    @pl.when(jnp.logical_and(relay_right, group < groups - 1))
    def _():
        relay_in(0).wait_recv()
        relay_out(1).start()

    for other in range(1, FOLDS):
        source = (fold + other) % FOLDS

        @pl.when(reachable(source // 2, place))
        def _():
            arrival(source).wait_recv()

    for b in range(rows):
        resid[0, b] = (parts[0, b] + parts[2, b]) + (parts[4, b] + parts[6, b])
        begun = (parts[1, b] + parts[3, b]) + (parts[5, b] + parts[7, b])
        update[0, b] = begun
        iterate[b] = zero
        store_vector(0, reach + b, begun)

    NEAR, FAR, RESID = [0], [1], [2]

    def exchange(parity, side, which):
        source, target, length, near = [
            (update, halo_update, HB, 0), (update, halo_update, reach - HB, HB), (resid, halo_resid, outer, 0),
        ][which]
        mirrored = source is update
        return pltpu.make_async_remote_copy(
            src_ref=source.at[parity, pl.ds(near + side * (rows - 2 * near - length), length)],
            dst_ref=target.at[parity, 1 - side, pl.ds(near + side * (reach - 2 * near - length if mirrored else 0), length)],
            send_sem=h_send.at[parity, side, which], recv_sem=h_recv.at[parity, 1 - side, which],
            device_id={name: left[name] + side * (right[name] - left[name]) for name in left}, device_id_type=MESH,
        )

    inside = jnp.logical_and(has_left, has_right)

    def neighbours(act):
        @pl.when(inside)
        def _():
            act(range(2))

        @pl.when(jnp.logical_not(has_left))
        def _():
            act([1])

        @pl.when(jnp.logical_not(has_right))
        def _():
            act([0])

    def send(parity, chosen):
        def act(sides):
            for which in chosen:
                for side in sides:
                    exchange(parity, side, which).start()

        neighbours(act)

    def sent_all(parity, chosen):
        def act(sides):
            for which in chosen:
                for side in sides:
                    exchange(parity, side, which).wait_send()

        neighbours(act)

    primary = place // (FOLDS - 1)
    secondary = 1 - primary

    def present(side):
        return jnp.where(side == 0, has_left, has_right)

    def halo_of(ref, parity, side, b):
        return jnp.where(present(side), ref[parity, side, b], 0.0)

    def send_one(parity, side, chosen):
        @pl.when(present(side))
        def _():
            for which in chosen:
                exchange(parity, side, which).start()

    def receive_one(parity, side, chosen):
        @pl.when(present(side))
        def _():
            for which in chosen:
                exchange(parity, 1 - side, which).wait_recv()

    send(0, NEAR + FAR + RESID)

    for other in range(1, FOLDS):
        @pl.when(reachable(chip, position_of((fold + other) % FOLDS)))
        def _():
            message(other)[1].wait_send()


    def edge_most(side):
        arrived = edge(1 - side)
        arrived[0].wait_recv()
        into = pltpu.make_async_copy(edge_columns.at[side], all_columns.at[2 * side], column_sem.at[1 + side])
        into.start()
        into.wait()
        arrived[1].wait_recv()
        prepare_most(side)

    def edge_last(side):
        edge(1 - side)[2].wait_recv()
        relay_out(side).wait_recv()
        prepare_last(side)
        for copy in edge(side):
            copy.wait_send()

    def product(which, e, low, length):
        lhs = jnp.concatenate([vectors[which][order[e, low + s]] for s in range(length)], axis=1)
        begin = low * LANES if isinstance(low, int) else pl.multiple_of(low * LANES, LANES)
        full = jnp.dot(lhs, weights[e, pl.ds(begin, length * LANES), :], preferred_element_type=jnp.float32)
        return (full[:NV, :LANES] + full[:NV, LANES:]) + (full[NV:, :LANES] + full[NV:, LANES:])

    def own_slots(j):
        return max(0, HB - j), KB - max(0, HB - (rows - 1 - j))

    keeps, gains = step_factors()
    rounds = SWEEPS * DEGREE // depth

    def one_turn(turn, first_turn=False, last_turn=False):
        parity, phase = turn % 2, turn % (DEGREE // depth)
        given = RESID if first_turn else []
        for level in range(depth):
            now, later = level % 2, (level + 1) % 2
            keep, gain = keeps[phase * depth + level], gains[phase * depth + level]

            def finish(e, applied, side=None, distance=0):
                own = e - outer
                if level > 0:
                    old, left_over = mid_update[e], mid_resid[e]
                elif side is None:
                    old, left_over = update[parity, own], resid[parity, own]
                else:
                    at = (1 - side) * (reach - 1 - distance) + side * distance
                    old = halo_of(halo_update, parity, side, at)
                    if first_turn:
                        left_over = halo_of(halo_resid, parity, side, at - (1 - side) * HB)
                    else:
                        before = (phase * depth + DEGREE - 1) % DEGREE
                        left_over = (old - keeps[before] * mid_update[e]) * (1.0 / gains[before])
                left_over = left_over - applied
                fresh = keep * old + gain * left_over
                if side is None:
                    iterate[own] = iterate[own] + old
                if level == depth - 1:
                    update[1 - parity, own] = fresh
                    resid[1 - parity, own] = left_over
                else:
                    mid_update[e] = fresh
                    mid_resid[e] = left_over
                store_vector(later, e + HB, fresh)

            if level > 0:
                for side in (primary, secondary):
                    for i in range(HB):
                        e = outer + i + side * (rows - 1 - 2 * i)
                        finish(e, product(now, e, 0, KB))
                    if not last_turn:
                        send_one(1 - parity, side, NEAR)
                for j in range(HB, rows - HB):
                    finish(j + outer, product(now, j + outer, 0, KB))
                continue

            for j in range(rows):
                low, high = own_slots(j)
                applied = product(now, j + outer, low, high - low)
                if high - low == KB:
                    finish(j + outer, applied)
                else:
                    partial[j] = applied

            if first_turn:
                at_edges(edge_most)
            sent_all(parity, NEAR + FAR + given)
            for side in (secondary, primary):
                receive_one(parity, side, NEAR)
                far_side = reach - HB
                for b in range(HB):
                    store_vector(now, far_side + b + side * (rows + HB), halo_of(halo_update, parity, side, (1 - side) * far_side + b))
                for i in range(HB):
                    j, length = i + side * (rows - 1 - 2 * i), HB - i
                    finish(j + outer, partial[j] + product(now, j + outer, side * (KB - length), length))
                if first_turn and side is primary:
                    at_edges(edge_last)

                def outer_row(i):
                    return outer - 1 - i + side * (rows + 1 + 2 * i)

                for i in range(outer):
                    partial[rows + i] = product(now, outer_row(i), (1 - side) * (1 + i), KB - 1 - i)
                receive_one(parity, side, FAR + given)
                for b in range(far_side):
                    store_vector(now, b + side * (reach + rows + HB), halo_of(halo_update, parity, side, side * HB + b))
                for i in range(outer):
                    e = outer_row(i)
                    finish(e, partial[rows + i] + product(now, e, side * (KB - 1 - i), 1 + i), side, i)

        if not last_turn:
            for side in (primary, secondary):
                send_one(1 - parity, side, FAR)

    def at_edges(act):
        @pl.when(left_edge)
        def _():
            act(0)

        @pl.when(right_edge)
        def _():
            act(1)

    one_turn(0, first_turn=True)

    @pl.loop(0, (rounds - 2) // 2)
    def _(_):
        one_turn(1)
        one_turn(2)

    one_turn(rounds - 1, last_turn=True)

    @pl.when(jnp.logical_and(relay_left, group < groups - 1))
    def _():
        relay_in(1).wait_send()

    @pl.when(jnp.logical_and(relay_right, group > 0))
    def _():
        relay_in(0).wait_send()

    @pl.when(jnp.logical_or(jnp.logical_and(relay_left, group > 0), jnp.logical_and(relay_right, group < groups - 1)))
    def _():
        relay_out(0).wait_send()

    for b in range(rows):
        gathered[place * rows + b] = iterate[b] + update[rounds % 2, b]

    def piece(where, dest, which):
        return pltpu.make_async_remote_copy(
            src_ref=gathered.at[pl.ds(where * rows, rows)], dst_ref=gathered.at[pl.ds(where * rows, rows)],
            send_sem=c_send.at[which], recv_sem=c_recv.at[where],
            device_id={"group": group, "fold": dest}, device_id_type=MESH,
        )

    def needs(dest, where):
        return jnp.logical_and(where >= 2 * dest - FOLDS, where <= 2 * dest + 1)

    def either(chip_of, where):
        return jnp.logical_or(needs(chip_of // 2 * 2, where), needs(chip_of // 2 * 2 + 1, where))

    across = (fold + FOLDS // 2) % FOLDS
    across_partner = (partner + FOLDS // 2) % FOLDS
    beside_me = {other: (fold + 2 * other) % FOLDS for other in (1, 3)}
    outgoing = [(2, place, across, needs(across, place)), (5, place, across_partner, needs(across_partner, place))]
    outgoing += [(other, place, dest, either(dest, place)) for other, dest in beside_me.items()]
    outgoing += [(0, place, partner, needs(partner, place))]
    passed_on = [
        (3 + other, position_of(source), partner, needs(partner, position_of(source))) for other, source in beside_me.items()
    ]

    for which, where, dest, wish in outgoing:
        pl.when(wish)(piece(where, dest, which).start)
    for which, where, dest, wish in passed_on:
        pl.when(either(fold, where))(piece(where, dest, which).wait_recv)
        pl.when(wish)(piece(where, dest, which).start)
    for source in [partner, across, across_partner] + [(partner + 2 * other) % FOLDS for other in (1, 3)]:
        where = position_of(source)
        pl.when(needs(fold, where))(piece(where, partner, 0).wait_recv)

    begin, live = start_of(fold), count_of(fold)
    shift = begin & (LANES - 1)
    base = begin // LANES
    back = (LANES - shift) & (LANES - 1)

    def shifted(m):
        return pltpu.roll(gathered[jnp.minimum(base + m, owned - 1)], back, 1)

    here = shifted(0)
    for m in range(slots):
        after = shifted(m + 1)
        value = jnp.where(lane < LANES - shift, here, after)
        out[:, m * LANES:(m + 1) * LANES] = jnp.where(lane + m * LANES < live, value, 0.0)
        here = after

    for which, where, dest, wish in outgoing + passed_on:
        pl.when(wish)(piece(where, dest, which).wait_send)


def on_device(right_side, initial, counts, columns, blocks):
    folds, groups = lax.axis_size("fold"), lax.axis_size("group")
    slots = right_side.shape[1] // LANES
    owned = blocks.shape[0]
    rows = owned // folds
    depth = DEPTH
    reach, outer = HB * depth, HB * (depth - 1)
    vmem = pl.BlockSpec(memory_space=pltpu.VMEM)
    anywhere = pl.BlockSpec(memory_space=pl.ANY)
    f32, i32 = jnp.float32, jnp.int32
    dma = pltpu.SemaphoreType.DMA

    def vectors(*shape):
        return pltpu.VMEM(shape + (NV, LANES), f32)

    return pl.pallas_call(
        functools.partial(kernel, rows, groups, depth),
        out_shape=pltpu.VMEM(right_side.shape, f32),
        in_specs=[anywhere] * 5,
        out_specs=vmem,
        scratch_shapes=[
            pltpu.SMEM(counts.shape, i32),
            pltpu.VMEM(right_side.shape, f32),
            pltpu.VMEM(right_side.shape, f32),
            vectors(2, slots + 3),
            vectors(owned),
            vectors(folds, rows),
            pltpu.VMEM((rows, KB, LANES, LANES), f32),
            pltpu.VMEM((outer - 1, KB, LANES, LANES), f32),
            pltpu.VMEM((outer - 1, KB, LANES, LANES), f32),
            pltpu.VMEM((KB, LANES, LANES), f32),
            pltpu.VMEM((KB, LANES, LANES), f32),
            pltpu.VMEM((KB - EARLY, LANES, LANES), f32),
            pltpu.VMEM((rows + 2 * outer, KB * LANES, 2 * LANES), jnp.bfloat16),
            pltpu.SMEM((rows + 2 * outer, KB), i32),
            pltpu.SMEM((3, KB, owned), i32),
            pltpu.VMEM((2, KB, owned), i32),
            pltpu.VMEM((rows + 2 * reach, 2 * NV, LANES), jnp.bfloat16),
            pltpu.VMEM((rows + 2 * reach, 2 * NV, LANES), jnp.bfloat16),
            vectors(2, rows),
            vectors(2, rows),
            vectors(rows + 2 * outer),
            vectors(rows + 2 * outer),
            vectors(rows),
            vectors(rows + HB),
            vectors(2, 2, reach),
            vectors(2, 2, outer),
            vectors(owned),
            dma((6,)), dma((4,)), dma((3, 2)), dma((3, 2)), dma((3,)), dma((2,)), dma, dma, dma((8,)), dma((8,)),
            dma((2, 2, 3)), dma((2, 2, 3)), dma((7,)), dma((8,)),
        ],
        compiler_params=pltpu.CompilerParams(collective_id=0, has_side_effects=True),
    )(counts, columns.T, right_side, initial, blocks)


def solution(mesh):
    placed = (
        P(None, ("group", "fold")),
        P(None, ("group", "fold")),
        P("group", None),
        P("group", None),
        P("group", None, None, None),
    )
    return jax.shard_map(
        on_device, mesh=mesh, in_specs=placed, out_specs=P(None, ("group", "fold")), check_vma=False
    )
```

```python
import functools

import jax
import jax.numpy as jnp
from jax import lax
from jax.experimental import pallas as pl
from jax.experimental.pallas import tpu as pltpu
from jax.sharding import PartitionSpec as P

MESH = pl.DeviceIdType.MESH
HB = 3
SWEEPS = 3
DEGREE = 4
KB = 5
NV = 16
LANES = 128
FOLDS = 8
CHIPS = 4
DEPTH = 2
RELAYS = (3, 7)
EARLY = 2

upper_bound = 4.5
lower_bound = 1.35


def step_factors():
    theta = (upper_bound + lower_bound) / 2.0
    delta = (upper_bound - lower_bound) / 2.0
    keep, gain = [0.0], [1.0 / theta]
    ratio = delta / theta
    for step in range(DEGREE - 1):
        ratio_next = 1.0 / (2.0 * theta / delta - ratio)
        keep.append(ratio_next * ratio)
        gain.append(2.0 * ratio_next / delta)
        ratio = ratio_next
    return keep, gain


def split(value):
    high = value.astype(jnp.bfloat16)
    low = (value - high.astype(jnp.float32)).astype(jnp.bfloat16)
    return high, low


def position_of(fold):
    return (fold + 7) % 8


def fold_of(position):
    return (position + 1) % 8


def kernel(
    rows, groups, depth,
    counts_in, columns, right_side, initial, blocks, out,
    counts, mine, raw, aligned, sent, parts, raw_own, raw_left, raw_right, left_last, right_last, handed, weights, order, all_columns, edge_columns,
    vector_even, vector_odd, update, resid, mid_update, mid_resid, iterate, partial, halo_update, halo_resid, gathered,
    block_sem, column_sem, edge_send, edge_recv, relay_sems, last_sem, a_send, a_recv, b_send, b_recv, h_send, h_recv, c_send, c_recv,
):
    group, fold = lax.axis_index("group"), lax.axis_index("fold")
    chip, core = fold // 2, fold % 2
    place = position_of(fold)
    partner = chip * 2 + (1 - core)
    slots = right_side.shape[1] // LANES
    owned = rows * FOLDS
    reach = HB * depth
    outer = HB * (depth - 1)
    wide = rows + 2 * outer
    zero = jnp.zeros((NV, LANES), jnp.float32)

    rank = group * FOLDS + place
    last = groups * FOLDS - 1
    has_left, has_right = rank > 0, rank < last
    relay_left, relay_right = fold == RELAYS[0], fold == RELAYS[1]
    relay = jnp.logical_or(relay_left, relay_right)
    below, above = {"group": (group + groups - 1) % groups, "fold": fold}, {"group": (group + 1) % groups, "fold": fold}
    left_edge, right_edge = jnp.logical_and(place == 0, has_left), jnp.logical_and(place == FOLDS - 1, has_right)
    left = {"group": (group + groups - (7 - place) // 7) % groups, "fold": fold_of((place + 7) % 8)}
    right = {"group": (group + place // 7) % groups, "fold": fold_of((place + 1) % 8)}

    own_blocks = pltpu.make_async_copy(
        blocks.at[pl.ds(place * rows, rows)], raw_own, block_sem.at[0]
    )
    most = outer - 1
    raw_last = [left_last, right_last]

    def beside(side):
        begin = jnp.minimum(place * rows + rows, owned - outer) if side else jnp.maximum(place * rows - outer, 0)
        return [
            pltpu.make_async_copy(
                blocks.at[pl.ds(begin, most)], (raw_right if side else raw_left), block_sem.at[1 + 2 * side]
            ),
            pltpu.make_async_copy(blocks.at[begin + most], raw_last[side], block_sem.at[2 + 2 * side]),
        ]

    own_columns = pltpu.make_async_copy(columns, all_columns.at[1], column_sem.at[0])
    barrier = pltpu.get_barrier_semaphore()
    @pl.when(left_edge)
    def _():
        pl.semaphore_signal(barrier, inc=1, device_id=left, device_id_type=MESH)

    @pl.when(right_edge)
    def _():
        pl.semaphore_signal(barrier, inc=1, device_id=right, device_id_type=MESH)

    @pl.when(jnp.logical_and(relay, group > 0))
    def _():
        pl.semaphore_signal(barrier, inc=1, device_id=below, device_id_type=MESH)

    @pl.when(jnp.logical_and(relay, group < groups - 1))
    def _():
        pl.semaphore_signal(barrier, inc=1, device_id=above, device_id_type=MESH)

    for other in (4, 3, 5, 2, 6, 1, 7):
        pl.semaphore_signal(barrier, inc=1, device_id={"group": group, "fold": (fold + other) % FOLDS}, device_id_type=MESH)

    own_counts = pltpu.make_async_copy(counts_in, counts, column_sem.at[3])
    own_counts.start()

    def own_slots_copy(source):
        return pltpu.make_async_copy(source, mine, block_sem.at[5])

    @pl.when(core == 0)
    def _():
        own_slots_copy(right_side).start()

    @pl.when(core == 1)
    def _():
        own_slots_copy(initial).start()

    own_columns.start()
    own_blocks.start()

    @pl.when(place > 0)
    def _():
        for copy in beside(0):
            copy.start()

    @pl.when(place < FOLDS - 1)
    def _():
        for copy in beside(1):
            copy.start()

    outside = (7 - place) // 7 * ((rank + last) // (last + 1)) + place // 7 * (1 - (rank + 1) // (last + 1))
    is_relay = jnp.where(relay, 1, 0)
    beyond = is_relay * ((group + groups - 1) // groups + 1 - (group + 1) // groups)
    pl.semaphore_wait(barrier, FOLDS - 1 + outside + beyond)

    def swap(source):
        return pltpu.make_async_remote_copy(
            src_ref=source, dst_ref=raw, send_sem=a_send, recv_sem=a_recv,
            device_id={"group": group, "fold": partner}, device_id_type=MESH,
        )

    @pl.when(core == 0)
    def _():
        swap(initial).start()

    @pl.when(core == 1)
    def _():
        swap(right_side).start()

    def edge(side):
        begin = owned - outer if side else 0
        target = 1 - side
        refs = [
            (columns, edge_columns.at[target]),
            (blocks.at[pl.ds(begin, most)], (raw_right if target else raw_left)),
            (blocks.at[begin + most, pl.ds(0, EARLY)], raw_last[target].at[pl.ds(0, EARLY)]),
        ]
        return [
            pltpu.make_async_remote_copy(
                src_ref=source, dst_ref=dest, send_sem=edge_send.at[i, side], recv_sem=edge_recv.at[i, target],
                device_id=right if side else left, device_id_type=MESH,
            )
            for i, (source, dest) in enumerate(refs)
        ]

    def relay_in(side):
        return pltpu.make_async_remote_copy(
            src_ref=blocks.at[(owned - outer if side else 0) + most, pl.ds(EARLY, KB - EARLY)], dst_ref=handed, send_sem=relay_sems.at[0],
            recv_sem=relay_sems.at[1], device_id=above if side else below, device_id_type=MESH,
        )

    def relay_out(side):
        return pltpu.make_async_remote_copy(
            src_ref=handed, dst_ref=raw_last[side].at[pl.ds(EARLY, KB - EARLY)], send_sem=relay_sems.at[2], recv_sem=last_sem.at[side],
            device_id={"group": group, "fold": fold_of(side * (FOLDS - 1))}, device_id_type=MESH,
        )

    @pl.when(left_edge)
    def _():
        for copy in edge(0):
            copy.start()

    @pl.when(right_edge)
    def _():
        for copy in edge(1):
            copy.start()

    @pl.when(jnp.logical_and(relay_left, group < groups - 1))
    def _():
        relay_in(1).start()

    @pl.when(jnp.logical_and(relay_right, group > 0))
    def _():
        relay_in(0).start()

    lane = lax.broadcasted_iota(jnp.int32, (NV, LANES), 1)

    def start_of(which):
        total = jnp.int32(0)
        for i in range(FOLDS):
            total = total + jnp.where(i < which, counts[0, i], 0)
        return total

    def count_of(which):
        total = jnp.int32(0)
        for i in range(FOLDS):
            total = total + jnp.where(i == which, counts[0, i], 0)
        return total

    def align(source, which):
        start, count = start_of(chip * 2 + which), count_of(chip * 2 + which)
        shift = start & (LANES - 1)
        aligned[which, 0] = zero
        aligned[which, slots + 2] = zero
        before = zero
        for m in range(slots + 1):
            if m < slots:
                now = pltpu.roll(source[:, m * LANES:(m + 1) * LANES], shift, 1)
            else:
                now = zero
            slot = lane + (m * LANES - shift)
            value = jnp.where(lane < shift, before, now)
            live = jnp.logical_and(slot >= 0, slot < count)
            aligned[which, m + 1] = jnp.where(live, value, 0.0)
            before = now

    own_counts.wait()
    own_slots_copy(initial).wait()

    @pl.when(core == 0)
    def _():
        align(mine, 0)

    @pl.when(core == 1)
    def _():
        align(mine, 1)

    swap(initial).wait()

    @pl.when(core == 0)
    def _():
        align(raw, 1)

    @pl.when(core == 1)
    def _():
        align(raw, 0)

    first = [start_of(chip * 2) // LANES, start_of(chip * 2 + 1) // LANES]

    def row_block(index):
        at = [jnp.clip(index - first[i], -1, slots + 1) + 1 for i in range(2)]
        return aligned[0, at[0]] + aligned[1, at[1]]

    def message(other):
        dest = (fold + other) % FOLDS
        where = position_of(dest) * rows
        return where, pltpu.make_async_remote_copy(
            src_ref=sent.at[pl.ds(where, rows)], dst_ref=parts.at[fold],
            send_sem=b_send.at[other], recv_sem=b_recv.at[fold],
            device_id={"group": group, "fold": dest}, device_id_type=MESH,
        )

    def reachable(source, dest):
        low = jnp.logical_and(source == CHIPS - 1, dest < FOLDS // 2)
        return jnp.logical_not(jnp.logical_or(low, jnp.logical_and(source == 0, dest >= FOLDS // 2)))

    def arrival(source):
        return pltpu.make_async_remote_copy(
            src_ref=sent.at[pl.ds(0, rows)], dst_ref=parts.at[source],
            send_sem=b_send.at[0], recv_sem=b_recv.at[source],
            device_id={"group": group, "fold": fold}, device_id_type=MESH,
        )

    for other in (4, 3, 5, 2, 6, 1, 7):
        where, copy = message(other)
        for b in range(rows):
            sent[where + b] = row_block(where + b)

        @pl.when(reachable(chip, position_of((fold + other) % FOLDS)))
        def _():
            copy.start()

    for b in range(rows):
        parts[fold, b] = row_block(place * rows + b)
    for other in range(1, FOLDS):
        source = (fold + other) % FOLDS

        @pl.when(jnp.logical_not(reachable(source // 2, place)))
        def _():
            for b in range(rows):
                parts[source, b] = zero


    def prepare(source, low, high, single=False):
        @pl.loop(low, high)
        def _(e):
            at_row = place * rows + e - outer + owned
            owner, within = at_row // owned, at_row % owned
            move = (owner - 1) * owned - place * rows + outer
            column = [all_columns[owner, k, within] for k in range(KB)]
            ranks = []
            for k in range(KB):
                r = jnp.int32(0)
                for other in range(KB):
                    if other != k:
                        ahead = column[other] <= column[k] if other < k else column[other] < column[k]
                        r = r + ahead.astype(jnp.int32)
                ranks.append(r)
            for s in range(KB):
                from_slot, at = jnp.int32(0), jnp.int32(0)
                for k in range(KB):
                    from_slot = from_slot + jnp.where(ranks[k] == s, k, 0)
                    at = at + jnp.where(ranks[k] == s, column[k], 0)
                order[e, s] = jnp.clip(at + move, 0, rows + 2 * reach - 1)
                high_part, low_part = split((source[from_slot] if single else source[e - low, from_slot]).T)
                weights[e, s * LANES:(s + 1) * LANES, 0:LANES] = high_part
                weights[e, s * LANES:(s + 1) * LANES, LANES:2 * LANES] = low_part

    def absent(low):
        for e in range(low, low + outer):
            for s in range(KB):
                order[e, s] = 0
            weights[e] = jnp.zeros((KB * LANES, 2 * LANES), jnp.bfloat16)

    own_columns.wait()
    own_blocks.wait()
    prepare(raw_own, outer, outer + rows)

    def prepare_most(side):
        at = side * (outer + rows)
        prepare(raw_right if side else raw_left, at, at + most)

    def prepare_last(side):
        at = side * (outer + rows) + most
        prepare(raw_last[side], at, at + 1, single=True)

    def prepare_beside(side):
        for copy in beside(side):
            copy.wait()
        prepare_most(side)
        prepare_last(side)

    @pl.when(place > 0)
    def _():
        prepare_beside(0)

    @pl.when(place < FOLDS - 1)
    def _():
        prepare_beside(1)

    @pl.when(jnp.logical_not(has_left))
    def _():
        absent(0)

    @pl.when(jnp.logical_not(has_right))
    def _():
        absent(outer + rows)

    vectors = [vector_even, vector_odd]

    def store_vector(which, index, value):
        high, low = split(value)
        vectors[which][index, 0:NV] = high
        vectors[which][index, NV:2 * NV] = low

    @pl.when(jnp.logical_and(relay_left, group > 0))
    def _():
        relay_in(1).wait_recv()
        relay_out(0).start()

    @pl.when(jnp.logical_and(relay_right, group < groups - 1))
    def _():
        relay_in(0).wait_recv()
        relay_out(1).start()

    for other in range(1, FOLDS):
        source = (fold + other) % FOLDS

        @pl.when(reachable(source // 2, place))
        def _():
            arrival(source).wait_recv()

    for b in range(rows):
        resid[0, b] = (parts[0, b] + parts[2, b]) + (parts[4, b] + parts[6, b])
        begun = (parts[1, b] + parts[3, b]) + (parts[5, b] + parts[7, b])
        update[0, b] = begun
        iterate[b] = zero
        store_vector(0, reach + b, begun)

    NEAR, FAR, RESID = [0], [1], [2]

    def exchange(parity, side, which):
        source, target, length, near = [
            (update, halo_update, HB, 0), (update, halo_update, reach - HB, HB), (resid, halo_resid, outer, 0),
        ][which]
        mirrored = source is update
        return pltpu.make_async_remote_copy(
            src_ref=source.at[parity, pl.ds(near + side * (rows - 2 * near - length), length)],
            dst_ref=target.at[parity, 1 - side, pl.ds(near + side * (reach - 2 * near - length if mirrored else 0), length)],
            send_sem=h_send.at[parity, side, which], recv_sem=h_recv.at[parity, 1 - side, which],
            device_id={name: left[name] + side * (right[name] - left[name]) for name in left}, device_id_type=MESH,
        )

    inside = jnp.logical_and(has_left, has_right)

    def neighbours(act):
        @pl.when(inside)
        def _():
            act([place // (FOLDS - 1), 1 - place // (FOLDS - 1)])

        @pl.when(jnp.logical_not(has_left))
        def _():
            act([1])

        @pl.when(jnp.logical_not(has_right))
        def _():
            act([0])

    def send(parity, chosen):
        def act(sides):
            for which in chosen:
                for side in sides:
                    exchange(parity, side, which).start()

        neighbours(act)

    def sent_all(parity, chosen):
        def act(sides):
            for which in chosen:
                for side in sides:
                    exchange(parity, side, which).wait_send()

        neighbours(act)

    def receive(parity, chosen):
        def act(sides):
            for which in chosen:
                for side in sides:
                    exchange(parity, 1 - side, which).wait_recv()

        neighbours(act)

    def halo_of(ref, parity, side, b):
        return jnp.where(has_right if side else has_left, ref[parity, side, b], 0.0)

    send(0, NEAR + FAR + RESID)

    for other in range(1, FOLDS):
        @pl.when(reachable(chip, position_of((fold + other) % FOLDS)))
        def _():
            message(other)[1].wait_send()


    def edge_most(side):
        arrived = edge(1 - side)
        arrived[0].wait_recv()
        into = pltpu.make_async_copy(edge_columns.at[side], all_columns.at[2 * side], column_sem.at[1 + side])
        into.start()
        into.wait()
        arrived[1].wait_recv()
        prepare_most(side)

    def edge_last(side):
        edge(1 - side)[2].wait_recv()
        relay_out(side).wait_recv()
        prepare_last(side)
        for copy in edge(side):
            copy.wait_send()

    def product(which, e, low, high):
        lhs = jnp.concatenate([vectors[which][order[e, s]] for s in range(low, high)], axis=1)
        full = jnp.dot(lhs, weights[e, low * LANES:high * LANES, :], preferred_element_type=jnp.float32)
        return (full[:NV, :LANES] + full[:NV, LANES:]) + (full[NV:, :LANES] + full[NV:, LANES:])

    def own_slots(j):
        return max(0, HB - j), KB - max(0, HB - (rows - 1 - j))

    keeps, gains = step_factors()
    rounds = SWEEPS * DEGREE // depth

    def one_turn(turn, first_turn=False, last_turn=False):
        parity, phase = turn % 2, turn % (DEGREE // depth)
        given = RESID if first_turn else []
        for level in range(depth):
            now, later = level % 2, (level + 1) % 2
            keep, gain = keeps[phase * depth + level], gains[phase * depth + level]

            def finish(e, applied):
                own = e - outer
                inside = 0 <= own < rows
                if level > 0:
                    old, left_over = mid_update[e], mid_resid[e]
                elif inside:
                    old, left_over = update[parity, own], resid[parity, own]
                else:
                    side, at = (0, e + HB) if own < 0 else (1, own - rows)
                    old = halo_of(halo_update, parity, side, at)
                    if first_turn:
                        left_over = halo_of(halo_resid, parity, side, at - (1 - side) * HB)
                    else:
                        before = (phase * depth + DEGREE - 1) % DEGREE
                        left_over = (old - keeps[before] * mid_update[e]) * (1.0 / gains[before])
                left_over = left_over - applied
                fresh = keep * old + gain * left_over
                if inside:
                    iterate[own] = iterate[own] + old
                if level == depth - 1:
                    update[1 - parity, own] = fresh
                    resid[1 - parity, own] = left_over
                else:
                    mid_update[e] = fresh
                    mid_resid[e] = left_over
                store_vector(later, e + HB, fresh)

            margin = HB * (depth - 1 - level)
            if level > 0:
                ends = list(range(HB)) + list(range(rows - HB, rows))
                for j in ends:
                    finish(j + outer, product(now, j + outer, 0, KB))

                if not last_turn:
                    send(1 - parity, NEAR)
                for j in range(HB, rows - HB):
                    finish(j + outer, product(now, j + outer, 0, KB))
                continue

            for j in range(rows):
                low, high = own_slots(j)
                applied = product(now, j + outer, low, high)
                if high - low == KB:
                    finish(j + outer, applied)
                else:
                    partial[j] = applied

            if first_turn:
                at_edges(edge_most)
            sent_all(parity, NEAR + FAR + given)
            receive(parity, NEAR)
            for b in range(HB):
                store_vector(now, reach - HB + b, halo_of(halo_update, parity, 0, reach - HB + b))
                store_vector(now, reach + rows + b, halo_of(halo_update, parity, 1, b))
            for j in range(rows):
                low, high = own_slots(j)
                if low > 0:
                    finish(j + outer, partial[j] + product(now, j + outer, 0, low))
                elif high < KB:
                    finish(j + outer, partial[j] + product(now, j + outer, high, KB))
            def settled(e):
                return (HB - e, KB) if e < outer else (0, KB - 1 - (e - outer - rows))

            beyond_rows = list(range(outer)) + list(range(outer + rows, wide))
            if first_turn:
                at_edges(edge_last)
            for i, e in enumerate(beyond_rows):
                partial[i] = product(now, e, *settled(e))
            receive(parity, FAR + given)
            for b in range(reach - HB):
                store_vector(now, b, halo_of(halo_update, parity, 0, b))
                store_vector(now, reach + rows + HB + b, halo_of(halo_update, parity, 1, HB + b))
            for i, e in enumerate(beyond_rows):
                low, high = settled(e)
                finish(e, partial[i] + (product(now, e, 0, low) if low else product(now, e, high, KB)))

        if not last_turn:
            send(1 - parity, FAR)

    def at_edges(act):
        @pl.when(left_edge)
        def _():
            act(0)

        @pl.when(right_edge)
        def _():
            act(1)

    one_turn(0, first_turn=True)

    @pl.loop(0, (rounds - 2) // 2)
    def _(_):
        one_turn(1)
        one_turn(2)

    one_turn(rounds - 1, last_turn=True)

    @pl.when(jnp.logical_and(relay_left, group < groups - 1))
    def _():
        relay_in(1).wait_send()

    @pl.when(jnp.logical_and(relay_right, group > 0))
    def _():
        relay_in(0).wait_send()

    @pl.when(jnp.logical_or(jnp.logical_and(relay_left, group > 0), jnp.logical_and(relay_right, group < groups - 1)))
    def _():
        relay_out(0).wait_send()

    for b in range(rows):
        gathered[place * rows + b] = iterate[b] + update[rounds % 2, b]

    def piece(where, dest, which):
        return pltpu.make_async_remote_copy(
            src_ref=gathered.at[pl.ds(where * rows, rows)], dst_ref=gathered.at[pl.ds(where * rows, rows)],
            send_sem=c_send.at[which], recv_sem=c_recv.at[where],
            device_id={"group": group, "fold": dest}, device_id_type=MESH,
        )

    def needs(dest, where):
        return jnp.logical_and(where >= 2 * dest - FOLDS, where <= 2 * dest + 1)

    others = [(fold + other) % FOLDS for other in (4, 3, 5, 2, 6, 1, 7)]
    outgoing = [(i, place, dest, needs(dest, place)) for i, dest in enumerate(others)]

    for which, where, dest, wish in outgoing:
        pl.when(wish)(piece(where, dest, which).start)
    for source in others:
        where = position_of(source)
        pl.when(needs(fold, where))(piece(where, partner, 0).wait_recv)

    begin, live = start_of(fold), count_of(fold)
    shift = begin & (LANES - 1)
    base = begin // LANES
    back = (LANES - shift) & (LANES - 1)

    def shifted(m):
        return pltpu.roll(gathered[jnp.minimum(base + m, owned - 1)], back, 1)

    here = shifted(0)
    for m in range(slots):
        after = shifted(m + 1)
        value = jnp.where(lane < LANES - shift, here, after)
        out[:, m * LANES:(m + 1) * LANES] = jnp.where(lane + m * LANES < live, value, 0.0)
        here = after

    for which, where, dest, wish in outgoing:
        pl.when(wish)(piece(where, dest, which).wait_send)


def on_device(right_side, initial, counts, columns, blocks):
    folds, groups = lax.axis_size("fold"), lax.axis_size("group")
    slots = right_side.shape[1] // LANES
    owned = blocks.shape[0]
    rows = owned // folds
    depth = DEPTH
    reach, outer = HB * depth, HB * (depth - 1)
    vmem = pl.BlockSpec(memory_space=pltpu.VMEM)
    anywhere = pl.BlockSpec(memory_space=pl.ANY)
    f32, i32 = jnp.float32, jnp.int32
    dma = pltpu.SemaphoreType.DMA

    def vectors(*shape):
        return pltpu.VMEM(shape + (NV, LANES), f32)

    return pl.pallas_call(
        functools.partial(kernel, rows, groups, depth),
        out_shape=pltpu.VMEM(right_side.shape, f32),
        in_specs=[anywhere] * 5,
        out_specs=vmem,
        scratch_shapes=[
            pltpu.SMEM(counts.shape, i32),
            pltpu.VMEM(right_side.shape, f32),
            pltpu.VMEM(right_side.shape, f32),
            vectors(2, slots + 3),
            vectors(owned),
            vectors(folds, rows),
            pltpu.VMEM((rows, KB, LANES, LANES), f32),
            pltpu.VMEM((outer - 1, KB, LANES, LANES), f32),
            pltpu.VMEM((outer - 1, KB, LANES, LANES), f32),
            pltpu.VMEM((KB, LANES, LANES), f32),
            pltpu.VMEM((KB, LANES, LANES), f32),
            pltpu.VMEM((KB - EARLY, LANES, LANES), f32),
            pltpu.VMEM((rows + 2 * outer, KB * LANES, 2 * LANES), jnp.bfloat16),
            pltpu.SMEM((rows + 2 * outer, KB), i32),
            pltpu.SMEM((3, KB, owned), i32),
            pltpu.VMEM((2, KB, owned), i32),
            pltpu.VMEM((rows + 2 * reach, 2 * NV, LANES), jnp.bfloat16),
            pltpu.VMEM((rows + 2 * reach, 2 * NV, LANES), jnp.bfloat16),
            vectors(2, rows),
            vectors(2, rows),
            vectors(rows + 2 * outer),
            vectors(rows + 2 * outer),
            vectors(rows),
            vectors(rows),
            vectors(2, 2, reach),
            vectors(2, 2, outer),
            vectors(owned),
            dma((6,)), dma((4,)), dma((3, 2)), dma((3, 2)), dma((3,)), dma((2,)), dma, dma, dma((8,)), dma((8,)),
            dma((2, 2, 3)), dma((2, 2, 3)), dma((7,)), dma((8,)),
        ],
        compiler_params=pltpu.CompilerParams(collective_id=0, has_side_effects=True),
    )(counts, columns.T, right_side, initial, blocks)


def solution(mesh):
    placed = (
        P(None, ("group", "fold")),
        P(None, ("group", "fold")),
        P("group", None),
        P("group", None),
        P("group", None, None, None),
    )
    return jax.shard_map(
        on_device, mesh=mesh, in_specs=placed, out_specs=P(None, ("group", "fold")), check_vma=False
    )
```

```python
import functools

import jax
import jax.numpy as jnp
from jax import lax
from jax.experimental import pallas as pl
from jax.experimental.pallas import tpu as pltpu
from jax.sharding import PartitionSpec as P

MESH = pl.DeviceIdType.MESH
HB = 3
SWEEPS = 3
DEGREE = 4
KB = 5
NV = 16
LANES = 128
FOLDS = 8
CHIPS = 4
DEPTH = 2
RELAYS = (3, 7)
EARLY = 2

upper_bound = 4.5
lower_bound = 1.35


def step_factors():
    theta = (upper_bound + lower_bound) / 2.0
    delta = (upper_bound - lower_bound) / 2.0
    keep, gain = [0.0], [1.0 / theta]
    ratio = delta / theta
    for step in range(DEGREE - 1):
        ratio_next = 1.0 / (2.0 * theta / delta - ratio)
        keep.append(ratio_next * ratio)
        gain.append(2.0 * ratio_next / delta)
        ratio = ratio_next
    return keep, gain


def split(value):
    high = value.astype(jnp.bfloat16)
    low = (value - high.astype(jnp.float32)).astype(jnp.bfloat16)
    return high, low


def position_of(fold):
    return (fold + 7) % 8


def fold_of(position):
    return (position + 1) % 8


def kernel(
    rows, groups, depth,
    counts_in, columns, right_side, initial, blocks, out,
    counts, mine, raw, aligned, sent, parts, raw_own, raw_left, raw_right, left_last, right_last, handed, weights, order, all_columns, edge_columns,
    vector_even, vector_odd, update, resid, mid_update, mid_resid, iterate, partial, halo_update, halo_resid, gathered,
    block_sem, column_sem, edge_send, edge_recv, relay_sems, last_sem, a_send, a_recv, b_send, b_recv, h_send, h_recv, c_send, c_recv,
):
    group, fold = lax.axis_index("group"), lax.axis_index("fold")
    chip, core = fold // 2, fold % 2
    place = position_of(fold)
    partner = chip * 2 + (1 - core)
    slots = right_side.shape[1] // LANES
    owned = rows * FOLDS
    reach = HB * depth
    outer = HB * (depth - 1)
    wide = rows + 2 * outer
    zero = jnp.zeros((NV, LANES), jnp.float32)

    rank = group * FOLDS + place
    last = groups * FOLDS - 1
    has_left, has_right = rank > 0, rank < last
    relay_left, relay_right = fold == RELAYS[0], fold == RELAYS[1]
    relay = jnp.logical_or(relay_left, relay_right)
    below, above = {"group": (group + groups - 1) % groups, "fold": fold}, {"group": (group + 1) % groups, "fold": fold}
    left_edge, right_edge = jnp.logical_and(place == 0, has_left), jnp.logical_and(place == FOLDS - 1, has_right)
    left = {"group": (group + groups - (7 - place) // 7) % groups, "fold": fold_of((place + 7) % 8)}
    right = {"group": (group + place // 7) % groups, "fold": fold_of((place + 1) % 8)}

    own_blocks = pltpu.make_async_copy(
        blocks.at[pl.ds(place * rows, rows)], raw_own, block_sem.at[0]
    )
    most = outer - 1
    raw_last = [left_last, right_last]

    def beside(side):
        begin = jnp.minimum(place * rows + rows, owned - outer) if side else jnp.maximum(place * rows - outer, 0)
        return [
            pltpu.make_async_copy(
                blocks.at[pl.ds(begin, most)], (raw_right if side else raw_left), block_sem.at[1 + 2 * side]
            ),
            pltpu.make_async_copy(blocks.at[begin + most], raw_last[side], block_sem.at[2 + 2 * side]),
        ]

    own_columns = pltpu.make_async_copy(columns, all_columns.at[1], column_sem.at[0])
    barrier = pltpu.get_barrier_semaphore()
    @pl.when(left_edge)
    def _():
        pl.semaphore_signal(barrier, inc=1, device_id=left, device_id_type=MESH)

    @pl.when(right_edge)
    def _():
        pl.semaphore_signal(barrier, inc=1, device_id=right, device_id_type=MESH)

    @pl.when(jnp.logical_and(relay, group > 0))
    def _():
        pl.semaphore_signal(barrier, inc=1, device_id=below, device_id_type=MESH)

    @pl.when(jnp.logical_and(relay, group < groups - 1))
    def _():
        pl.semaphore_signal(barrier, inc=1, device_id=above, device_id_type=MESH)

    for other in (4, 3, 5, 2, 6, 1, 7):
        pl.semaphore_signal(barrier, inc=1, device_id={"group": group, "fold": (fold + other) % FOLDS}, device_id_type=MESH)

    own_counts = pltpu.make_async_copy(counts_in, counts, column_sem.at[3])
    own_counts.start()

    def own_slots_copy(source):
        return pltpu.make_async_copy(source, mine, block_sem.at[5])

    @pl.when(core == 0)
    def _():
        own_slots_copy(right_side).start()

    @pl.when(core == 1)
    def _():
        own_slots_copy(initial).start()

    own_columns.start()
    own_blocks.start()

    @pl.when(place > 0)
    def _():
        for copy in beside(0):
            copy.start()

    @pl.when(place < FOLDS - 1)
    def _():
        for copy in beside(1):
            copy.start()

    outside = (7 - place) // 7 * ((rank + last) // (last + 1)) + place // 7 * (1 - (rank + 1) // (last + 1))
    is_relay = jnp.where(relay, 1, 0)
    beyond = is_relay * ((group + groups - 1) // groups + 1 - (group + 1) // groups)
    pl.semaphore_wait(barrier, FOLDS - 1 + outside + beyond)

    def swap(source):
        return pltpu.make_async_remote_copy(
            src_ref=source, dst_ref=raw, send_sem=a_send, recv_sem=a_recv,
            device_id={"group": group, "fold": partner}, device_id_type=MESH,
        )

    @pl.when(core == 0)
    def _():
        swap(initial).start()

    @pl.when(core == 1)
    def _():
        swap(right_side).start()

    def edge(side):
        begin = owned - outer if side else 0
        target = 1 - side
        refs = [
            (columns, edge_columns.at[target]),
            (blocks.at[pl.ds(begin, most)], (raw_right if target else raw_left)),
            (blocks.at[begin + most, pl.ds(0, EARLY)], raw_last[target].at[pl.ds(0, EARLY)]),
        ]
        return [
            pltpu.make_async_remote_copy(
                src_ref=source, dst_ref=dest, send_sem=edge_send.at[i, side], recv_sem=edge_recv.at[i, target],
                device_id=right if side else left, device_id_type=MESH,
            )
            for i, (source, dest) in enumerate(refs)
        ]

    def relay_in(side):
        return pltpu.make_async_remote_copy(
            src_ref=blocks.at[(owned - outer if side else 0) + most, pl.ds(EARLY, KB - EARLY)], dst_ref=handed, send_sem=relay_sems.at[0],
            recv_sem=relay_sems.at[1], device_id=above if side else below, device_id_type=MESH,
        )

    def relay_out(side):
        return pltpu.make_async_remote_copy(
            src_ref=handed, dst_ref=raw_last[side].at[pl.ds(EARLY, KB - EARLY)], send_sem=relay_sems.at[2], recv_sem=last_sem.at[side],
            device_id={"group": group, "fold": fold_of(side * (FOLDS - 1))}, device_id_type=MESH,
        )

    @pl.when(left_edge)
    def _():
        for copy in edge(0):
            copy.start()

    @pl.when(right_edge)
    def _():
        for copy in edge(1):
            copy.start()

    @pl.when(jnp.logical_and(relay_left, group < groups - 1))
    def _():
        relay_in(1).start()

    @pl.when(jnp.logical_and(relay_right, group > 0))
    def _():
        relay_in(0).start()

    lane = lax.broadcasted_iota(jnp.int32, (NV, LANES), 1)

    def start_of(which):
        total = jnp.int32(0)
        for i in range(FOLDS):
            total = total + jnp.where(i < which, counts[0, i], 0)
        return total

    def count_of(which):
        total = jnp.int32(0)
        for i in range(FOLDS):
            total = total + jnp.where(i == which, counts[0, i], 0)
        return total

    def align(source, which):
        start, count = start_of(chip * 2 + which), count_of(chip * 2 + which)
        shift = start & (LANES - 1)
        aligned[which, 0] = zero
        aligned[which, slots + 2] = zero
        before = zero
        for m in range(slots + 1):
            if m < slots:
                now = pltpu.roll(source[:, m * LANES:(m + 1) * LANES], shift, 1)
            else:
                now = zero
            slot = lane + (m * LANES - shift)
            value = jnp.where(lane < shift, before, now)
            live = jnp.logical_and(slot >= 0, slot < count)
            aligned[which, m + 1] = jnp.where(live, value, 0.0)
            before = now

    own_counts.wait()
    own_slots_copy(initial).wait()

    @pl.when(core == 0)
    def _():
        align(mine, 0)

    @pl.when(core == 1)
    def _():
        align(mine, 1)

    swap(initial).wait()

    @pl.when(core == 0)
    def _():
        align(raw, 1)

    @pl.when(core == 1)
    def _():
        align(raw, 0)

    first = [start_of(chip * 2) // LANES, start_of(chip * 2 + 1) // LANES]

    def row_block(index):
        at = [jnp.clip(index - first[i], -1, slots + 1) + 1 for i in range(2)]
        return aligned[0, at[0]] + aligned[1, at[1]]

    def message(other):
        dest = (fold + other) % FOLDS
        where = position_of(dest) * rows
        return where, pltpu.make_async_remote_copy(
            src_ref=sent.at[pl.ds(where, rows)], dst_ref=parts.at[fold],
            send_sem=b_send.at[other], recv_sem=b_recv.at[fold],
            device_id={"group": group, "fold": dest}, device_id_type=MESH,
        )

    def reachable(source, dest):
        low = jnp.logical_and(source == CHIPS - 1, dest < FOLDS // 2)
        return jnp.logical_not(jnp.logical_or(low, jnp.logical_and(source == 0, dest >= FOLDS // 2)))

    def arrival(source):
        return pltpu.make_async_remote_copy(
            src_ref=sent.at[pl.ds(0, rows)], dst_ref=parts.at[source],
            send_sem=b_send.at[0], recv_sem=b_recv.at[source],
            device_id={"group": group, "fold": fold}, device_id_type=MESH,
        )

    for other in (4, 5, 3, 6, 2, 7, 1):
        where, copy = message(other)
        for b in range(rows):
            sent[where + b] = row_block(where + b)

        @pl.when(reachable(chip, position_of((fold + other) % FOLDS)))
        def _():
            copy.start()

    for b in range(rows):
        parts[fold, b] = row_block(place * rows + b)
    for other in range(1, FOLDS):
        source = (fold + other) % FOLDS

        @pl.when(jnp.logical_not(reachable(source // 2, place)))
        def _():
            for b in range(rows):
                parts[source, b] = zero


    def prepare(source, low, high, single=False):
        @pl.loop(low, high)
        def _(e):
            at_row = place * rows + e - outer + owned
            owner, within = at_row // owned, at_row % owned
            move = (owner - 1) * owned - place * rows + outer
            column = [all_columns[owner, k, within] for k in range(KB)]
            ranks = []
            for k in range(KB):
                r = jnp.int32(0)
                for other in range(KB):
                    if other != k:
                        ahead = column[other] <= column[k] if other < k else column[other] < column[k]
                        r = r + ahead.astype(jnp.int32)
                ranks.append(r)
            for s in range(KB):
                from_slot, at = jnp.int32(0), jnp.int32(0)
                for k in range(KB):
                    from_slot = from_slot + jnp.where(ranks[k] == s, k, 0)
                    at = at + jnp.where(ranks[k] == s, column[k], 0)
                order[e, s] = jnp.clip(at + move, 0, rows + 2 * reach - 1)
                high_part, low_part = split((source[from_slot] if single else source[e - low, from_slot]).T)
                weights[e, s * LANES:(s + 1) * LANES, 0:LANES] = high_part
                weights[e, s * LANES:(s + 1) * LANES, LANES:2 * LANES] = low_part

    def absent(low):
        for e in range(low, low + outer):
            for s in range(KB):
                order[e, s] = 0
            weights[e] = jnp.zeros((KB * LANES, 2 * LANES), jnp.bfloat16)

    own_columns.wait()
    own_blocks.wait()
    prepare(raw_own, outer, outer + rows)

    @pl.when(jnp.logical_and(relay_left, group > 0))
    def _():
        relay_in(1).wait_recv()
        relay_out(0).start()

    @pl.when(jnp.logical_and(relay_right, group < groups - 1))
    def _():
        relay_in(0).wait_recv()
        relay_out(1).start()

    def prepare_most(side):
        at = side * (outer + rows)
        prepare(raw_right if side else raw_left, at, at + most)

    def prepare_last(side):
        at = side * (outer + rows) + most
        prepare(raw_last[side], at, at + 1, single=True)

    def prepare_beside(side):
        for copy in beside(side):
            copy.wait()
        prepare_most(side)
        prepare_last(side)

    @pl.when(place > 0)
    def _():
        prepare_beside(0)

    @pl.when(place < FOLDS - 1)
    def _():
        prepare_beside(1)

    @pl.when(jnp.logical_not(has_left))
    def _():
        absent(0)

    @pl.when(jnp.logical_not(has_right))
    def _():
        absent(outer + rows)

    vectors = [vector_even, vector_odd]

    def store_vector(which, index, value):
        high, low = split(value)
        vectors[which][index, 0:NV] = high
        vectors[which][index, NV:2 * NV] = low

    for other in range(1, FOLDS):
        source = (fold + other) % FOLDS

        @pl.when(reachable(source // 2, place))
        def _():
            arrival(source).wait_recv()

    for b in range(rows):
        resid[0, b] = (parts[0, b] + parts[2, b]) + (parts[4, b] + parts[6, b])
        begun = (parts[1, b] + parts[3, b]) + (parts[5, b] + parts[7, b])
        update[0, b] = begun
        iterate[b] = zero
        store_vector(0, reach + b, begun)

    NEAR, FAR, RESID = [0], [1], [2]

    def exchange(parity, side, which):
        source, target, length, near = [
            (update, halo_update, HB, 0), (update, halo_update, reach - HB, HB), (resid, halo_resid, outer, 0),
        ][which]
        mirrored = source is update
        return pltpu.make_async_remote_copy(
            src_ref=source.at[parity, pl.ds(near + side * (rows - 2 * near - length), length)],
            dst_ref=target.at[parity, 1 - side, pl.ds(near + side * (reach - 2 * near - length if mirrored else 0), length)],
            send_sem=h_send.at[parity, side, which], recv_sem=h_recv.at[parity, 1 - side, which],
            device_id={name: left[name] + side * (right[name] - left[name]) for name in left}, device_id_type=MESH,
        )

    inside = jnp.logical_and(has_left, has_right)

    def neighbours(act):
        @pl.when(inside)
        def _():
            act([place // (FOLDS - 1), 1 - place // (FOLDS - 1)])

        @pl.when(jnp.logical_not(has_left))
        def _():
            act([1])

        @pl.when(jnp.logical_not(has_right))
        def _():
            act([0])

    def send(parity, chosen):
        def act(sides):
            for which in chosen:
                for side in sides:
                    exchange(parity, side, which).start()

        neighbours(act)

    def sent_all(parity, chosen):
        def act(sides):
            for which in chosen:
                for side in sides:
                    exchange(parity, side, which).wait_send()

        neighbours(act)

    def receive(parity, chosen):
        def act(sides):
            for which in chosen:
                for side in sides:
                    exchange(parity, 1 - side, which).wait_recv()

        neighbours(act)

    def halo_of(ref, parity, side, b):
        return jnp.where(has_right if side else has_left, ref[parity, side, b], 0.0)

    send(0, NEAR + FAR + RESID)

    for other in range(1, FOLDS):
        @pl.when(reachable(chip, position_of((fold + other) % FOLDS)))
        def _():
            message(other)[1].wait_send()


    def edge_most(side):
        arrived = edge(1 - side)
        arrived[0].wait_recv()
        into = pltpu.make_async_copy(edge_columns.at[side], all_columns.at[2 * side], column_sem.at[1 + side])
        into.start()
        into.wait()
        arrived[1].wait_recv()
        prepare_most(side)

    def edge_last(side):
        edge(1 - side)[2].wait_recv()
        relay_out(side).wait_recv()
        prepare_last(side)
        for copy in edge(side):
            copy.wait_send()

    def product(which, e, low, high):
        lhs = jnp.concatenate([vectors[which][order[e, s]] for s in range(low, high)], axis=1)
        full = jnp.dot(lhs, weights[e, low * LANES:high * LANES, :], preferred_element_type=jnp.float32)
        return (full[:NV, :LANES] + full[:NV, LANES:]) + (full[NV:, :LANES] + full[NV:, LANES:])

    def own_slots(j):
        return max(0, HB - j), KB - max(0, HB - (rows - 1 - j))

    keeps, gains = step_factors()
    rounds = SWEEPS * DEGREE // depth

    def one_turn(turn, first_turn=False, last_turn=False):
        parity, phase = turn % 2, turn % (DEGREE // depth)
        given = RESID if first_turn else []
        for level in range(depth):
            now, later = level % 2, (level + 1) % 2
            keep, gain = keeps[phase * depth + level], gains[phase * depth + level]

            def finish(e, applied):
                own = e - outer
                inside = 0 <= own < rows
                if level > 0:
                    old, left_over = mid_update[e], mid_resid[e]
                elif inside:
                    old, left_over = update[parity, own], resid[parity, own]
                else:
                    side, at = (0, e + HB) if own < 0 else (1, own - rows)
                    old = halo_of(halo_update, parity, side, at)
                    if first_turn:
                        left_over = halo_of(halo_resid, parity, side, at - (1 - side) * HB)
                    else:
                        before = (phase * depth + DEGREE - 1) % DEGREE
                        left_over = (old - keeps[before] * mid_update[e]) * (1.0 / gains[before])
                left_over = left_over - applied
                fresh = keep * old + gain * left_over
                if inside:
                    iterate[own] = iterate[own] + old
                if level == depth - 1:
                    update[1 - parity, own] = fresh
                    resid[1 - parity, own] = left_over
                else:
                    mid_update[e] = fresh
                    mid_resid[e] = left_over
                store_vector(later, e + HB, fresh)

            margin = HB * (depth - 1 - level)
            if level > 0:
                ends = list(range(HB)) + list(range(rows - HB, rows))
                for j in ends:
                    finish(j + outer, product(now, j + outer, 0, KB))

                if not last_turn:
                    send(1 - parity, NEAR)
                for j in range(HB, rows - HB):
                    finish(j + outer, product(now, j + outer, 0, KB))
                continue

            for j in range(rows):
                low, high = own_slots(j)
                applied = product(now, j + outer, low, high)
                if high - low == KB:
                    finish(j + outer, applied)
                else:
                    partial[j] = applied

            if first_turn:
                at_edges(edge_most)
            sent_all(parity, NEAR + FAR + given)
            receive(parity, NEAR)
            for b in range(HB):
                store_vector(now, reach - HB + b, halo_of(halo_update, parity, 0, reach - HB + b))
                store_vector(now, reach + rows + b, halo_of(halo_update, parity, 1, b))
            for j in range(rows):
                low, high = own_slots(j)
                if low > 0:
                    finish(j + outer, partial[j] + product(now, j + outer, 0, low))
                elif high < KB:
                    finish(j + outer, partial[j] + product(now, j + outer, high, KB))
            def settled(e):
                return (HB - e, KB) if e < outer else (0, KB - 1 - (e - outer - rows))

            beyond_rows = list(range(outer)) + list(range(outer + rows, wide))
            if first_turn:
                at_edges(edge_last)
            for i, e in enumerate(beyond_rows):
                partial[i] = product(now, e, *settled(e))
            receive(parity, FAR + given)
            for b in range(reach - HB):
                store_vector(now, b, halo_of(halo_update, parity, 0, b))
                store_vector(now, reach + rows + HB + b, halo_of(halo_update, parity, 1, HB + b))
            for i, e in enumerate(beyond_rows):
                low, high = settled(e)
                finish(e, partial[i] + (product(now, e, 0, low) if low else product(now, e, high, KB)))

        if not last_turn:
            send(1 - parity, FAR)

    def at_edges(act):
        @pl.when(left_edge)
        def _():
            act(0)

        @pl.when(right_edge)
        def _():
            act(1)

    one_turn(0, first_turn=True)

    @pl.loop(0, (rounds - 2) // 2)
    def _(_):
        one_turn(1)
        one_turn(2)

    one_turn(rounds - 1, last_turn=True)

    @pl.when(jnp.logical_and(relay_left, group < groups - 1))
    def _():
        relay_in(1).wait_send()

    @pl.when(jnp.logical_and(relay_right, group > 0))
    def _():
        relay_in(0).wait_send()

    @pl.when(jnp.logical_or(jnp.logical_and(relay_left, group > 0), jnp.logical_and(relay_right, group < groups - 1)))
    def _():
        relay_out(0).wait_send()

    for b in range(rows):
        gathered[place * rows + b] = iterate[b] + update[rounds % 2, b]

    def piece(where, dest, which):
        return pltpu.make_async_remote_copy(
            src_ref=gathered.at[pl.ds(where * rows, rows)], dst_ref=gathered.at[pl.ds(where * rows, rows)],
            send_sem=c_send.at[which], recv_sem=c_recv.at[where],
            device_id={"group": group, "fold": dest}, device_id_type=MESH,
        )

    def needs(dest, where):
        return jnp.logical_and(where >= 2 * dest - FOLDS, where <= 2 * dest + 1)

    others = [(fold + other) % FOLDS for other in (4, 3, 5, 2, 6, 1, 7)]
    outgoing = [(i, place, dest, needs(dest, place)) for i, dest in enumerate(others)]

    for which, where, dest, wish in outgoing:
        pl.when(wish)(piece(where, dest, which).start)
    for source in others:
        where = position_of(source)
        pl.when(needs(fold, where))(piece(where, partner, 0).wait_recv)

    begin, live = start_of(fold), count_of(fold)
    shift = begin & (LANES - 1)
    base = begin // LANES
    back = (LANES - shift) & (LANES - 1)

    def shifted(m):
        return pltpu.roll(gathered[jnp.minimum(base + m, owned - 1)], back, 1)

    here = shifted(0)
    for m in range(slots):
        after = shifted(m + 1)
        value = jnp.where(lane < LANES - shift, here, after)
        out[:, m * LANES:(m + 1) * LANES] = jnp.where(lane + m * LANES < live, value, 0.0)
        here = after

    for which, where, dest, wish in outgoing:
        pl.when(wish)(piece(where, dest, which).wait_send)


def on_device(right_side, initial, counts, columns, blocks):
    folds, groups = lax.axis_size("fold"), lax.axis_size("group")
    slots = right_side.shape[1] // LANES
    owned = blocks.shape[0]
    rows = owned // folds
    depth = DEPTH
    reach, outer = HB * depth, HB * (depth - 1)
    vmem = pl.BlockSpec(memory_space=pltpu.VMEM)
    anywhere = pl.BlockSpec(memory_space=pl.ANY)
    f32, i32 = jnp.float32, jnp.int32
    dma = pltpu.SemaphoreType.DMA

    def vectors(*shape):
        return pltpu.VMEM(shape + (NV, LANES), f32)

    return pl.pallas_call(
        functools.partial(kernel, rows, groups, depth),
        out_shape=pltpu.VMEM(right_side.shape, f32),
        in_specs=[anywhere] * 5,
        out_specs=vmem,
        scratch_shapes=[
            pltpu.SMEM(counts.shape, i32),
            pltpu.VMEM(right_side.shape, f32),
            pltpu.VMEM(right_side.shape, f32),
            vectors(2, slots + 3),
            vectors(owned),
            vectors(folds, rows),
            pltpu.VMEM((rows, KB, LANES, LANES), f32),
            pltpu.VMEM((outer - 1, KB, LANES, LANES), f32),
            pltpu.VMEM((outer - 1, KB, LANES, LANES), f32),
            pltpu.VMEM((KB, LANES, LANES), f32),
            pltpu.VMEM((KB, LANES, LANES), f32),
            pltpu.VMEM((KB - EARLY, LANES, LANES), f32),
            pltpu.VMEM((rows + 2 * outer, KB * LANES, 2 * LANES), jnp.bfloat16),
            pltpu.SMEM((rows + 2 * outer, KB), i32),
            pltpu.SMEM((3, KB, owned), i32),
            pltpu.VMEM((2, KB, owned), i32),
            pltpu.VMEM((rows + 2 * reach, 2 * NV, LANES), jnp.bfloat16),
            pltpu.VMEM((rows + 2 * reach, 2 * NV, LANES), jnp.bfloat16),
            vectors(2, rows),
            vectors(2, rows),
            vectors(rows + 2 * outer),
            vectors(rows + 2 * outer),
            vectors(rows),
            vectors(rows),
            vectors(2, 2, reach),
            vectors(2, 2, outer),
            vectors(owned),
            dma((6,)), dma((4,)), dma((3, 2)), dma((3, 2)), dma((3,)), dma((2,)), dma, dma, dma((8,)), dma((8,)),
            dma((2, 2, 3)), dma((2, 2, 3)), dma((7,)), dma((8,)),
        ],
        compiler_params=pltpu.CompilerParams(collective_id=0, has_side_effects=True),
    )(counts, columns.T, right_side, initial, blocks)


def solution(mesh):
    placed = (
        P(None, ("group", "fold")),
        P(None, ("group", "fold")),
        P("group", None),
        P("group", None),
        P("group", None, None, None),
    )
    return jax.shard_map(
        on_device, mesh=mesh, in_specs=placed, out_specs=P(None, ("group", "fold")), check_vma=False
    )
```

```python
import functools

import jax
import jax.numpy as jnp
from jax import lax
from jax.experimental import pallas as pl
from jax.experimental.pallas import tpu as pltpu
from jax.sharding import PartitionSpec as P

MESH = pl.DeviceIdType.MESH
HB = 3
SWEEPS = 3
DEGREE = 4
KB = 5
NV = 16
LANES = 128
FOLDS = 8
CHIPS = 4
DEPTH = 2
RELAYS = (3, 7)
EARLY = 3

upper_bound = 4.5
lower_bound = 1.35


def step_factors():
    theta = (upper_bound + lower_bound) / 2.0
    delta = (upper_bound - lower_bound) / 2.0
    keep, gain = [0.0], [1.0 / theta]
    ratio = delta / theta
    for step in range(DEGREE - 1):
        ratio_next = 1.0 / (2.0 * theta / delta - ratio)
        keep.append(ratio_next * ratio)
        gain.append(2.0 * ratio_next / delta)
        ratio = ratio_next
    return keep, gain


def split(value):
    high = value.astype(jnp.bfloat16)
    low = (value - high.astype(jnp.float32)).astype(jnp.bfloat16)
    return high, low


def position_of(fold):
    return (fold + 7) % 8


def fold_of(position):
    return (position + 1) % 8


def kernel(
    rows, groups, depth,
    counts_in, columns, right_side, initial, blocks, out,
    counts, mine, raw, aligned, sent, parts, raw_own, raw_left, raw_right, left_last, right_last, handed, weights, order, all_columns, edge_columns,
    vector_even, vector_odd, update, resid, mid_update, mid_resid, iterate, partial, halo_update, halo_resid, gathered,
    block_sem, column_sem, edge_send, edge_recv, relay_sems, last_sem, a_send, a_recv, b_send, b_recv, h_send, h_recv, c_send, c_recv,
):
    group, fold = lax.axis_index("group"), lax.axis_index("fold")
    chip, core = fold // 2, fold % 2
    place = position_of(fold)
    partner = chip * 2 + (1 - core)
    slots = right_side.shape[1] // LANES
    owned = rows * FOLDS
    reach = HB * depth
    outer = HB * (depth - 1)
    wide = rows + 2 * outer
    zero = jnp.zeros((NV, LANES), jnp.float32)

    rank = group * FOLDS + place
    last = groups * FOLDS - 1
    has_left, has_right = rank > 0, rank < last
    relay_left, relay_right = fold == RELAYS[0], fold == RELAYS[1]
    relay = jnp.logical_or(relay_left, relay_right)
    below, above = {"group": (group + groups - 1) % groups, "fold": fold}, {"group": (group + 1) % groups, "fold": fold}
    left_edge, right_edge = jnp.logical_and(place == 0, has_left), jnp.logical_and(place == FOLDS - 1, has_right)
    left = {"group": (group + groups - (7 - place) // 7) % groups, "fold": fold_of((place + 7) % 8)}
    right = {"group": (group + place // 7) % groups, "fold": fold_of((place + 1) % 8)}

    own_blocks = pltpu.make_async_copy(
        blocks.at[pl.ds(place * rows, rows)], raw_own, block_sem.at[0]
    )
    most = outer - 1
    raw_last = [left_last, right_last]

    def beside(side):
        begin = jnp.minimum(place * rows + rows, owned - outer) if side else jnp.maximum(place * rows - outer, 0)
        return [
            pltpu.make_async_copy(
                blocks.at[pl.ds(begin, most)], (raw_right if side else raw_left), block_sem.at[1 + 2 * side]
            ),
            pltpu.make_async_copy(blocks.at[begin + most], raw_last[side], block_sem.at[2 + 2 * side]),
        ]

    own_columns = pltpu.make_async_copy(columns, all_columns.at[1], column_sem.at[0])
    barrier = pltpu.get_barrier_semaphore()
    @pl.when(left_edge)
    def _():
        pl.semaphore_signal(barrier, inc=1, device_id=left, device_id_type=MESH)

    @pl.when(right_edge)
    def _():
        pl.semaphore_signal(barrier, inc=1, device_id=right, device_id_type=MESH)

    @pl.when(jnp.logical_and(relay, group > 0))
    def _():
        pl.semaphore_signal(barrier, inc=1, device_id=below, device_id_type=MESH)

    @pl.when(jnp.logical_and(relay, group < groups - 1))
    def _():
        pl.semaphore_signal(barrier, inc=1, device_id=above, device_id_type=MESH)

    for other in (4, 3, 5, 2, 6, 1, 7):
        pl.semaphore_signal(barrier, inc=1, device_id={"group": group, "fold": (fold + other) % FOLDS}, device_id_type=MESH)

    own_counts = pltpu.make_async_copy(counts_in, counts, column_sem.at[3])
    own_counts.start()

    def own_slots_copy(source):
        return pltpu.make_async_copy(source, mine, block_sem.at[5])

    @pl.when(core == 0)
    def _():
        own_slots_copy(right_side).start()

    @pl.when(core == 1)
    def _():
        own_slots_copy(initial).start()

    own_columns.start()
    own_blocks.start()

    @pl.when(place > 0)
    def _():
        for copy in beside(0):
            copy.start()

    @pl.when(place < FOLDS - 1)
    def _():
        for copy in beside(1):
            copy.start()

    outside = (7 - place) // 7 * ((rank + last) // (last + 1)) + place // 7 * (1 - (rank + 1) // (last + 1))
    is_relay = jnp.where(relay, 1, 0)
    beyond = is_relay * ((group + groups - 1) // groups + 1 - (group + 1) // groups)
    pl.semaphore_wait(barrier, FOLDS - 1 + outside + beyond)

    def swap(source):
        return pltpu.make_async_remote_copy(
            src_ref=source, dst_ref=raw, send_sem=a_send, recv_sem=a_recv,
            device_id={"group": group, "fold": partner}, device_id_type=MESH,
        )

    @pl.when(core == 0)
    def _():
        swap(initial).start()

    @pl.when(core == 1)
    def _():
        swap(right_side).start()

    def edge(side):
        begin = owned - outer if side else 0
        target = 1 - side
        refs = [
            (columns, edge_columns.at[target]),
            (blocks.at[pl.ds(begin, most)], (raw_right if target else raw_left)),
            (blocks.at[begin + most, pl.ds(0, EARLY)], raw_last[target].at[pl.ds(0, EARLY)]),
        ]
        return [
            pltpu.make_async_remote_copy(
                src_ref=source, dst_ref=dest, send_sem=edge_send.at[i, side], recv_sem=edge_recv.at[i, target],
                device_id=right if side else left, device_id_type=MESH,
            )
            for i, (source, dest) in enumerate(refs)
        ]

    def relay_in(side):
        return pltpu.make_async_remote_copy(
            src_ref=blocks.at[(owned - outer if side else 0) + most, pl.ds(EARLY, KB - EARLY)], dst_ref=handed, send_sem=relay_sems.at[0],
            recv_sem=relay_sems.at[1], device_id=above if side else below, device_id_type=MESH,
        )

    def relay_out(side):
        return pltpu.make_async_remote_copy(
            src_ref=handed, dst_ref=raw_last[side].at[pl.ds(EARLY, KB - EARLY)], send_sem=relay_sems.at[2], recv_sem=last_sem.at[side],
            device_id={"group": group, "fold": fold_of(side * (FOLDS - 1))}, device_id_type=MESH,
        )

    @pl.when(left_edge)
    def _():
        for copy in edge(0):
            copy.start()

    @pl.when(right_edge)
    def _():
        for copy in edge(1):
            copy.start()

    @pl.when(jnp.logical_and(relay_left, group < groups - 1))
    def _():
        relay_in(1).start()

    @pl.when(jnp.logical_and(relay_right, group > 0))
    def _():
        relay_in(0).start()

    lane = lax.broadcasted_iota(jnp.int32, (NV, LANES), 1)

    def start_of(which):
        total = jnp.int32(0)
        for i in range(FOLDS):
            total = total + jnp.where(i < which, counts[0, i], 0)
        return total

    def count_of(which):
        total = jnp.int32(0)
        for i in range(FOLDS):
            total = total + jnp.where(i == which, counts[0, i], 0)
        return total

    def align(source, which):
        start, count = start_of(chip * 2 + which), count_of(chip * 2 + which)
        shift = start & (LANES - 1)
        aligned[which, 0] = zero
        aligned[which, slots + 2] = zero
        before = zero
        for m in range(slots + 1):
            if m < slots:
                now = pltpu.roll(source[:, m * LANES:(m + 1) * LANES], shift, 1)
            else:
                now = zero
            slot = lane + (m * LANES - shift)
            value = jnp.where(lane < shift, before, now)
            live = jnp.logical_and(slot >= 0, slot < count)
            aligned[which, m + 1] = jnp.where(live, value, 0.0)
            before = now

    own_counts.wait()
    own_slots_copy(initial).wait()

    @pl.when(core == 0)
    def _():
        align(mine, 0)

    @pl.when(core == 1)
    def _():
        align(mine, 1)

    swap(initial).wait()

    @pl.when(core == 0)
    def _():
        align(raw, 1)

    @pl.when(core == 1)
    def _():
        align(raw, 0)

    first = [start_of(chip * 2) // LANES, start_of(chip * 2 + 1) // LANES]

    def row_block(index):
        at = [jnp.clip(index - first[i], -1, slots + 1) + 1 for i in range(2)]
        return aligned[0, at[0]] + aligned[1, at[1]]

    def message(other):
        dest = (fold + other) % FOLDS
        where = position_of(dest) * rows
        return where, pltpu.make_async_remote_copy(
            src_ref=sent.at[pl.ds(where, rows)], dst_ref=parts.at[fold],
            send_sem=b_send.at[other], recv_sem=b_recv.at[fold],
            device_id={"group": group, "fold": dest}, device_id_type=MESH,
        )

    def reachable(source, dest):
        low = jnp.logical_and(source == CHIPS - 1, dest < FOLDS // 2)
        return jnp.logical_not(jnp.logical_or(low, jnp.logical_and(source == 0, dest >= FOLDS // 2)))

    def arrival(source):
        return pltpu.make_async_remote_copy(
            src_ref=sent.at[pl.ds(0, rows)], dst_ref=parts.at[source],
            send_sem=b_send.at[0], recv_sem=b_recv.at[source],
            device_id={"group": group, "fold": fold}, device_id_type=MESH,
        )

    for other in (4, 3, 5, 2, 6, 1, 7):
        where, copy = message(other)
        for b in range(rows):
            sent[where + b] = row_block(where + b)

        @pl.when(reachable(chip, position_of((fold + other) % FOLDS)))
        def _():
            copy.start()

    for b in range(rows):
        parts[fold, b] = row_block(place * rows + b)
    for other in range(1, FOLDS):
        source = (fold + other) % FOLDS

        @pl.when(jnp.logical_not(reachable(source // 2, place)))
        def _():
            for b in range(rows):
                parts[source, b] = zero


    def prepare(source, low, high, single=False):
        @pl.loop(low, high)
        def _(e):
            at_row = place * rows + e - outer + owned
            owner, within = at_row // owned, at_row % owned
            move = (owner - 1) * owned - place * rows + outer
            column = [all_columns[owner, k, within] for k in range(KB)]
            ranks = []
            for k in range(KB):
                r = jnp.int32(0)
                for other in range(KB):
                    if other != k:
                        ahead = column[other] <= column[k] if other < k else column[other] < column[k]
                        r = r + ahead.astype(jnp.int32)
                ranks.append(r)
            for s in range(KB):
                from_slot, at = jnp.int32(0), jnp.int32(0)
                for k in range(KB):
                    from_slot = from_slot + jnp.where(ranks[k] == s, k, 0)
                    at = at + jnp.where(ranks[k] == s, column[k], 0)
                order[e, s] = jnp.clip(at + move, 0, rows + 2 * reach - 1)
                high_part, low_part = split((source[from_slot] if single else source[e - low, from_slot]).T)
                weights[e, s * LANES:(s + 1) * LANES, 0:LANES] = high_part
                weights[e, s * LANES:(s + 1) * LANES, LANES:2 * LANES] = low_part

    def absent(low):
        for e in range(low, low + outer):
            for s in range(KB):
                order[e, s] = 0
            weights[e] = jnp.zeros((KB * LANES, 2 * LANES), jnp.bfloat16)

    own_columns.wait()
    own_blocks.wait()
    prepare(raw_own, outer, outer + rows)

    def prepare_most(side):
        at = side * (outer + rows)
        prepare(raw_right if side else raw_left, at, at + most)

    def prepare_last(side):
        at = side * (outer + rows) + most
        prepare(raw_last[side], at, at + 1, single=True)

    def prepare_beside(side):
        for copy in beside(side):
            copy.wait()
        prepare_most(side)
        prepare_last(side)

    @pl.when(place > 0)
    def _():
        prepare_beside(0)

    @pl.when(place < FOLDS - 1)
    def _():
        prepare_beside(1)

    @pl.when(jnp.logical_not(has_left))
    def _():
        absent(0)

    @pl.when(jnp.logical_not(has_right))
    def _():
        absent(outer + rows)

    vectors = [vector_even, vector_odd]

    def store_vector(which, index, value):
        high, low = split(value)
        vectors[which][index, 0:NV] = high
        vectors[which][index, NV:2 * NV] = low

    @pl.when(jnp.logical_and(relay_left, group > 0))
    def _():
        relay_in(1).wait_recv()
        relay_out(0).start()

    @pl.when(jnp.logical_and(relay_right, group < groups - 1))
    def _():
        relay_in(0).wait_recv()
        relay_out(1).start()

    for other in range(1, FOLDS):
        source = (fold + other) % FOLDS

        @pl.when(reachable(source // 2, place))
        def _():
            arrival(source).wait_recv()

    for b in range(rows):
        resid[0, b] = (parts[0, b] + parts[2, b]) + (parts[4, b] + parts[6, b])
        begun = (parts[1, b] + parts[3, b]) + (parts[5, b] + parts[7, b])
        update[0, b] = begun
        iterate[b] = zero
        store_vector(0, reach + b, begun)

    NEAR, FAR, RESID = [0], [1], [2]

    def exchange(parity, side, which):
        source, target, length, near = [
            (update, halo_update, HB, 0), (update, halo_update, reach - HB, HB), (resid, halo_resid, outer, 0),
        ][which]
        mirrored = source is update
        return pltpu.make_async_remote_copy(
            src_ref=source.at[parity, pl.ds(near + side * (rows - 2 * near - length), length)],
            dst_ref=target.at[parity, 1 - side, pl.ds(near + side * (reach - 2 * near - length if mirrored else 0), length)],
            send_sem=h_send.at[parity, side, which], recv_sem=h_recv.at[parity, 1 - side, which],
            device_id={name: left[name] + side * (right[name] - left[name]) for name in left}, device_id_type=MESH,
        )

    inside = jnp.logical_and(has_left, has_right)

    def neighbours(act):
        @pl.when(inside)
        def _():
            act([place // (FOLDS - 1), 1 - place // (FOLDS - 1)])

        @pl.when(jnp.logical_not(has_left))
        def _():
            act([1])

        @pl.when(jnp.logical_not(has_right))
        def _():
            act([0])

    def send(parity, chosen):
        def act(sides):
            for which in chosen:
                for side in sides:
                    exchange(parity, side, which).start()

        neighbours(act)

    def sent_all(parity, chosen):
        def act(sides):
            for which in chosen:
                for side in sides:
                    exchange(parity, side, which).wait_send()

        neighbours(act)

    def receive(parity, chosen):
        def act(sides):
            for which in chosen:
                for side in sides:
                    exchange(parity, 1 - side, which).wait_recv()

        neighbours(act)

    def halo_of(ref, parity, side, b):
        return jnp.where(has_right if side else has_left, ref[parity, side, b], 0.0)

    send(0, NEAR + FAR + RESID)

    for other in range(1, FOLDS):
        @pl.when(reachable(chip, position_of((fold + other) % FOLDS)))
        def _():
            message(other)[1].wait_send()


    def edge_most(side):
        arrived = edge(1 - side)
        arrived[0].wait_recv()
        into = pltpu.make_async_copy(edge_columns.at[side], all_columns.at[2 * side], column_sem.at[1 + side])
        into.start()
        into.wait()
        arrived[1].wait_recv()
        prepare_most(side)

    def edge_last(side):
        edge(1 - side)[2].wait_recv()
        relay_out(side).wait_recv()
        prepare_last(side)
        for copy in edge(side):
            copy.wait_send()

    def product(which, e, low, high):
        lhs = jnp.concatenate([vectors[which][order[e, s]] for s in range(low, high)], axis=1)
        full = jnp.dot(lhs, weights[e, low * LANES:high * LANES, :], preferred_element_type=jnp.float32)
        return (full[:NV, :LANES] + full[:NV, LANES:]) + (full[NV:, :LANES] + full[NV:, LANES:])

    def own_slots(j):
        return max(0, HB - j), KB - max(0, HB - (rows - 1 - j))

    keeps, gains = step_factors()
    rounds = SWEEPS * DEGREE // depth

    def one_turn(turn, first_turn=False, last_turn=False):
        parity, phase = turn % 2, turn % (DEGREE // depth)
        given = RESID if first_turn else []
        for level in range(depth):
            now, later = level % 2, (level + 1) % 2
            keep, gain = keeps[phase * depth + level], gains[phase * depth + level]

            def finish(e, applied):
                own = e - outer
                inside = 0 <= own < rows
                if level > 0:
                    old, left_over = mid_update[e], mid_resid[e]
                elif inside:
                    old, left_over = update[parity, own], resid[parity, own]
                else:
                    side, at = (0, e + HB) if own < 0 else (1, own - rows)
                    old = halo_of(halo_update, parity, side, at)
                    if first_turn:
                        left_over = halo_of(halo_resid, parity, side, at - (1 - side) * HB)
                    else:
                        before = (phase * depth + DEGREE - 1) % DEGREE
                        left_over = (old - keeps[before] * mid_update[e]) * (1.0 / gains[before])
                left_over = left_over - applied
                fresh = keep * old + gain * left_over
                if inside:
                    iterate[own] = iterate[own] + old
                if level == depth - 1:
                    update[1 - parity, own] = fresh
                    resid[1 - parity, own] = left_over
                else:
                    mid_update[e] = fresh
                    mid_resid[e] = left_over
                store_vector(later, e + HB, fresh)

            margin = HB * (depth - 1 - level)
            if level > 0:
                ends = list(range(HB)) + list(range(rows - HB, rows))
                for j in ends:
                    finish(j + outer, product(now, j + outer, 0, KB))

                if not last_turn:
                    send(1 - parity, NEAR)
                for j in range(HB, rows - HB):
                    finish(j + outer, product(now, j + outer, 0, KB))
                continue

            for j in range(rows):
                low, high = own_slots(j)
                applied = product(now, j + outer, low, high)
                if high - low == KB:
                    finish(j + outer, applied)
                else:
                    partial[j] = applied

            if first_turn:
                at_edges(edge_most)
            sent_all(parity, NEAR + FAR + given)
            receive(parity, NEAR)
            for b in range(HB):
                store_vector(now, reach - HB + b, halo_of(halo_update, parity, 0, reach - HB + b))
                store_vector(now, reach + rows + b, halo_of(halo_update, parity, 1, b))
            for j in range(rows):
                low, high = own_slots(j)
                if low > 0:
                    finish(j + outer, partial[j] + product(now, j + outer, 0, low))
                elif high < KB:
                    finish(j + outer, partial[j] + product(now, j + outer, high, KB))
            def settled(e):
                return (HB - e, KB) if e < outer else (0, KB - 1 - (e - outer - rows))

            beyond_rows = list(range(outer)) + list(range(outer + rows, wide))
            if first_turn:
                at_edges(edge_last)
            for i, e in enumerate(beyond_rows):
                partial[i] = product(now, e, *settled(e))
            receive(parity, FAR + given)
            for b in range(reach - HB):
                store_vector(now, b, halo_of(halo_update, parity, 0, b))
                store_vector(now, reach + rows + HB + b, halo_of(halo_update, parity, 1, HB + b))
            for i, e in enumerate(beyond_rows):
                low, high = settled(e)
                finish(e, partial[i] + (product(now, e, 0, low) if low else product(now, e, high, KB)))

        if not last_turn:
            send(1 - parity, FAR)

    def at_edges(act):
        @pl.when(left_edge)
        def _():
            act(0)

        @pl.when(right_edge)
        def _():
            act(1)

    one_turn(0, first_turn=True)

    @pl.loop(0, (rounds - 2) // 2)
    def _(_):
        one_turn(1)
        one_turn(2)

    one_turn(rounds - 1, last_turn=True)

    @pl.when(jnp.logical_and(relay_left, group < groups - 1))
    def _():
        relay_in(1).wait_send()

    @pl.when(jnp.logical_and(relay_right, group > 0))
    def _():
        relay_in(0).wait_send()

    @pl.when(jnp.logical_or(jnp.logical_and(relay_left, group > 0), jnp.logical_and(relay_right, group < groups - 1)))
    def _():
        relay_out(0).wait_send()

    for b in range(rows):
        gathered[place * rows + b] = iterate[b] + update[rounds % 2, b]

    def piece(where, dest, which):
        return pltpu.make_async_remote_copy(
            src_ref=gathered.at[pl.ds(where * rows, rows)], dst_ref=gathered.at[pl.ds(where * rows, rows)],
            send_sem=c_send.at[which], recv_sem=c_recv.at[where],
            device_id={"group": group, "fold": dest}, device_id_type=MESH,
        )

    def needs(dest, where):
        return jnp.logical_and(where >= 2 * dest - FOLDS, where <= 2 * dest + 1)

    others = [(fold + other) % FOLDS for other in (4, 3, 5, 2, 6, 1, 7)]
    outgoing = [(i, place, dest, needs(dest, place)) for i, dest in enumerate(others)]

    for which, where, dest, wish in outgoing:
        pl.when(wish)(piece(where, dest, which).start)
    for source in others:
        where = position_of(source)
        pl.when(needs(fold, where))(piece(where, partner, 0).wait_recv)

    begin, live = start_of(fold), count_of(fold)
    shift = begin & (LANES - 1)
    base = begin // LANES
    back = (LANES - shift) & (LANES - 1)

    def shifted(m):
        return pltpu.roll(gathered[jnp.minimum(base + m, owned - 1)], back, 1)

    here = shifted(0)
    for m in range(slots):
        after = shifted(m + 1)
        value = jnp.where(lane < LANES - shift, here, after)
        out[:, m * LANES:(m + 1) * LANES] = jnp.where(lane + m * LANES < live, value, 0.0)
        here = after

    for which, where, dest, wish in outgoing:
        pl.when(wish)(piece(where, dest, which).wait_send)


def on_device(right_side, initial, counts, columns, blocks):
    folds, groups = lax.axis_size("fold"), lax.axis_size("group")
    slots = right_side.shape[1] // LANES
    owned = blocks.shape[0]
    rows = owned // folds
    depth = DEPTH
    reach, outer = HB * depth, HB * (depth - 1)
    vmem = pl.BlockSpec(memory_space=pltpu.VMEM)
    anywhere = pl.BlockSpec(memory_space=pl.ANY)
    f32, i32 = jnp.float32, jnp.int32
    dma = pltpu.SemaphoreType.DMA

    def vectors(*shape):
        return pltpu.VMEM(shape + (NV, LANES), f32)

    return pl.pallas_call(
        functools.partial(kernel, rows, groups, depth),
        out_shape=pltpu.VMEM(right_side.shape, f32),
        in_specs=[anywhere] * 5,
        out_specs=vmem,
        scratch_shapes=[
            pltpu.SMEM(counts.shape, i32),
            pltpu.VMEM(right_side.shape, f32),
            pltpu.VMEM(right_side.shape, f32),
            vectors(2, slots + 3),
            vectors(owned),
            vectors(folds, rows),
            pltpu.VMEM((rows, KB, LANES, LANES), f32),
            pltpu.VMEM((outer - 1, KB, LANES, LANES), f32),
            pltpu.VMEM((outer - 1, KB, LANES, LANES), f32),
            pltpu.VMEM((KB, LANES, LANES), f32),
            pltpu.VMEM((KB, LANES, LANES), f32),
            pltpu.VMEM((KB - EARLY, LANES, LANES), f32),
            pltpu.VMEM((rows + 2 * outer, KB * LANES, 2 * LANES), jnp.bfloat16),
            pltpu.SMEM((rows + 2 * outer, KB), i32),
            pltpu.SMEM((3, KB, owned), i32),
            pltpu.VMEM((2, KB, owned), i32),
            pltpu.VMEM((rows + 2 * reach, 2 * NV, LANES), jnp.bfloat16),
            pltpu.VMEM((rows + 2 * reach, 2 * NV, LANES), jnp.bfloat16),
            vectors(2, rows),
            vectors(2, rows),
            vectors(rows + 2 * outer),
            vectors(rows + 2 * outer),
            vectors(rows),
            vectors(rows),
            vectors(2, 2, reach),
            vectors(2, 2, outer),
            vectors(owned),
            dma((6,)), dma((4,)), dma((3, 2)), dma((3, 2)), dma((3,)), dma((2,)), dma, dma, dma((8,)), dma((8,)),
            dma((2, 2, 3)), dma((2, 2, 3)), dma((7,)), dma((8,)),
        ],
        compiler_params=pltpu.CompilerParams(collective_id=0, has_side_effects=True),
    )(counts, columns.T, right_side, initial, blocks)


def solution(mesh):
    placed = (
        P(None, ("group", "fold")),
        P(None, ("group", "fold")),
        P("group", None),
        P("group", None),
        P("group", None, None, None),
    )
    return jax.shard_map(
        on_device, mesh=mesh, in_specs=placed, out_specs=P(None, ("group", "fold")), check_vma=False
    )
```
